32 devices in a mesh: die: 4 (over y, x), tile: 8 (over z, core).
Axes of the slice: x: 2, y: 2, z: 4, core: 2. Of those that a mesh axis runs over, the one named last changes fastest.
Arguments:
- source_heating: float32 [16, 128, 2048], P('die', 'tile'), may hold values from -96 to 96, as said below
- material_thermal_values: float32 [6], replicated, may hold values from 0.5 to 8
- layer_material: int32 [16], P('die'), may hold values from 0 to 5
- via_conductance: float32 [4], P('die'), may hold values from 2 to 16
- via_blocks: int32 [4, 24, 4], P('die'), may hold values from 0 to 2048, as said below
Outputs:
- thermal_solution: float32 [16, 128, 2048], P('die', 'tile')
- balance_defect: float32 [16, 128, 2048], P('die', 'tile')
The draws below stay inside these ranges and needn't reach their ends.
Inputs may be any that keep to these rules, and one draw needn't show every extreme that they name: `via_blocks`: entry (d, b) is (first row, first column, height, width) of via block b on top of die d, joining die d's top layer to die d + 1's bottom layer, or to the cooled lid for the top die. Height is 8, 16 or 32 and width 16, 32 or 64, each cut to the plane's 128 x 2048 cells; every block lies inside the plane; blocks may intersect. `source_heating`: heat per cell.
All inputs are finite; a program needn't handle non-finite values.
Results may differ from the reference program's by a relative error of at most 0.0003.
Values sent between devices are 32-bit elements; how exact they have to be, the bound alone decides.
No kernel may reach another device: no remote copies, remote signals or barrier semaphores. Data moves between devices by JAX's collectives and lax.ppermute only.
A program may use at most 128 MiB of HBM per device.

```python
import math
import jax
import jax.numpy as jnp
from jax import lax

LZ = 4
NX = 2048
NVIA = 24
NMAT = 6
NU = 2
NC = 6
NDIE = 4
NZ = 16
NY = 128


def draw_source_heating(key, part):
    key_rough = jax.random.fold_in(key, 0)
    return jnp.clip(16.0 * jax.random.normal(key_rough, (NZ, NY, NX), jnp.float32), -96.0, 96.0)


def draw_via_blocks(key, part):
    keys = jax.random.split(jax.random.fold_in(key, 7), 4)
    tall_pick = jax.random.randint(keys[0], (NDIE, NVIA), 0, 3)
    wide_pick = jax.random.randint(keys[1], (NDIE, NVIA), 0, 3)
    height = jnp.minimum(jnp.array([8, 16, 32], jnp.int32)[tall_pick], NY)
    lateral_extent = jnp.minimum(jnp.array([16, 32, 64], jnp.int32)[wide_pick], NX)
    first_row_index = jax.random.randint(keys[2], (NDIE, NVIA), 0, NY - height + 1)
    col_start = jax.random.randint(keys[3], (NDIE, NVIA), 0, NX - lateral_extent + 1)
    return jnp.stack([first_row_index, col_start, height, lateral_extent], axis=-1).astype(jnp.int32)


def touch_ends(values, key, least, high):
    dims = values.shape
    place = [jax.random.randint(jax.random.fold_in(key, axis), (), 0, dims[axis]) for axis in range(len(dims))]
    values = values.at[tuple(place)].set(least)
    longest = dims.index(max(dims))
    place[longest] = (place[longest] + 1) % dims[longest]
    return values.at[tuple(place)].set(high)


def steps_of(own_key, dims, cuts, smallest, high):
    factor_of = 1.0
    for position, shards_of in cuts:
        draws = jax.random.uniform(jax.random.fold_in(jax.random.fold_in(own_key, 6), position), (shards_of,), jnp.float32, smallest / len(cuts), high / len(cuts))
        factor_of = factor_of * jnp.repeat(jnp.exp(draws), dims[position] // shards_of).reshape((-1,) + (1,) * (len(dims) - 1 - position))
    return factor_of


def setup_inputs(seed: int = 0) -> dict:
    splits = jax.random.split(jax.random.key(seed), 6)
    source_heating = draw_source_heating(jax.random.fold_in(splits[5], 71), 0)
    material_thermal_values = jnp.clip(jnp.exp(jax.random.uniform(splits[1], (NMAT,), jnp.float32, math.log(0.5), math.log(8.0))), 0.5, 8.0)
    layer_material = touch_ends(jax.random.randint(splits[2], (NZ,), 0, NMAT), jax.random.fold_in(splits[2], 1), 0, NMAT - 1).astype(jnp.int32)
    via_conductance = jnp.clip(jnp.exp(math.log(16.0) - 2.0794415 * jax.random.uniform(splits[3], (NDIE,), jnp.float32) ** steps_of(splits[3], (NDIE,), ((0, 4),), -0.2, 0.2)), 2.0, 16.0)
    via_blocks = draw_via_blocks(jax.random.fold_in(splits[5], 71), 0)
    return {"source_heating": source_heating, "material_thermal_values": material_thermal_values, "layer_material": layer_material, "via_conductance": via_conductance, "via_blocks": via_blocks}


OMEGA = 0.8


def block_sums(field):
    depth, height, lateral_extent = field.shape
    return field.reshape(depth, height // 4, 4, lateral_extent // 4, 4).sum(axis=(2, 4))


def spread_out(field):
    return jnp.repeat(jnp.repeat(field, 4, axis=1), 4, axis=2)


def stencil(padded, field, stencil_coefficients, diagonal, upper, lower):
    side = padded[1:-1, 2:, 1:-1] + padded[1:-1, :-2, 1:-1] + padded[1:-1, 1:-1, 2:] + padded[1:-1, 1:-1, :-2]
    return diagonal * field - stencil_coefficients[:, None, None] * side - upper * padded[2:, 1:-1, 1:-1] - lower * padded[:-2, 1:-1, 1:-1]


def reference(source_heating, material_thermal_values, layer_material, via_conductance, via_blocks):
    onehot = (layer_material[:, None] == jnp.arange(NMAT, dtype=jnp.int32)[None, :]).astype(jnp.float32)
    layer_cond = jnp.sum(onehot * material_thermal_values[None, :], axis=1)
    following = jnp.concatenate([layer_cond[1:], layer_cond[-1:]])
    vertical = 2.0 * layer_cond * following / (layer_cond + following)
    row_ids = jnp.arange(NY, dtype=jnp.int32)
    col_ids = jnp.arange(NX, dtype=jnp.int32)

    def die_mask(blocks):
        input_rows = ((row_ids[None, :] >= blocks[:, 0:1]) & (row_ids[None, :] < blocks[:, 0:1] + blocks[:, 2:3])).astype(jnp.float32)
        in_cols = ((col_ids[None, :] >= blocks[:, 1:2]) & (col_ids[None, :] < blocks[:, 1:2] + blocks[:, 3:4])).astype(jnp.float32)
        return jnp.dot(input_rows.T, in_cols, precision=lax.Precision.HIGHEST, preferred_element_type=jnp.float32)

    masks = lax.map(die_mask, via_blocks)
    via_planes = masks * via_conductance[:, None, None]
    via_layers = jnp.repeat(via_planes, LZ, axis=0)
    placed_above = (jnp.arange(NZ, dtype=jnp.int32) % LZ) == LZ - 1
    upper_zero = jnp.where(placed_above[:, None, None], via_layers, vertical[:, None, None])
    lower_zero = jnp.concatenate([jnp.zeros((1, NY, NX), jnp.float32), upper_zero[:-1]], axis=0)
    upper_one = block_sums(upper_zero)
    lower_one = block_sums(lower_zero)
    uppers = [upper_zero, upper_one, block_sums(upper_one)]
    lowers = [lower_zero, lower_one, block_sums(lower_one)]
    stencil_coefficients = [layer_cond, layer_cond * 4.0, layer_cond * 16.0]
    diagonals = [4.0 * stencil_coefficients[lev][:, None, None] + uppers[lev] + lowers[lev] for lev in range(3)]

    def conduction_product(field, level):
        return stencil(jnp.pad(field, 1), field, stencil_coefficients[level], diagonals[level], uppers[level], lowers[level])

    def smooth(field, rhs, level):
        return field + OMEGA * (rhs - conduction_product(field, level)) / diagonals[level]

    def hierarchy_round(level, rhs, field):
        sweeps = NC if level == 2 else NU
        if field is None:
            field = OMEGA * rhs / diagonals[level]
            sweeps = sweeps - 1
        for sweep_index in range(sweeps):
            field = smooth(field, rhs, level)
        if level == 2:
            return field
        remainder = rhs - conduction_product(field, level)
        field = field + spread_out(hierarchy_round(level + 1, block_sums(remainder), None))
        for sweep_index in range(NU):
            field = smooth(field, rhs, level)
        return field

    thermal_solution = hierarchy_round(0, source_heating, None)
    thermal_solution = hierarchy_round(0, source_heating, thermal_solution)
    balance_defect = source_heating - conduction_product(thermal_solution, 0)
    return thermal_solution, balance_defect
```

```python
import functools

import jax
import jax.numpy as jnp
import numpy as np
from jax import lax
from jax.experimental import pallas as pl
from jax.experimental.pallas import tpu as pltpu
from jax.sharding import PartitionSpec as P

OMEGA = 0.8
NC = 6
LN = 128
HX = 64
HY = 8
F32 = jnp.float32
BF16 = jnp.bfloat16


def iota(shape, axis):
    return lax.broadcasted_iota(jnp.int32, shape, axis)


def split_dot(x, m):
    hi = x.astype(BF16)
    lo = (x - hi.astype(F32)).astype(BF16)
    return jnp.dot(hi, m, preferred_element_type=F32) + jnp.dot(lo, m, preferred_element_type=F32)


def pair_dot(a, b):
    return lax.dot_general(a, b, (((0,), (0,)), ((), ())), preferred_element_type=F32)


class Sizes:
    def __init__(self, mesh_shape, f_shape, n_blocks):
        self.nd, self.nt = mesh_shape["die"], mesh_shape["tile"]
        self.lz, self.rows, self.width = f_shape
        self.nb = n_blocks
        self.wc = self.width // self.nd
        self.we = self.wc + LN
        self.nz = self.nd * self.lz
        self.re = self.rows + 2 * HY
        self.r1 = self.re // 4
        self.c1 = self.wc // 4
        self.e1 = 2 * self.r1
        self.w1 = 2 * LN
        self.c2 = self.wc // 16
        self.chunk = self.lz
        assert self.rows == 16 and self.lz == 4 and self.c1 == LN
        assert self.nd * self.c2 == LN and self.nb % 8 == 0 and self.nt <= LN


def pack_kernel(s, idx, mat, material, conductance, blocks, f, *outs):
    d = idx[0]
    lane, sub = iota((8, LN), 1), iota((8, LN), 0)
    info = jnp.where(lane == 1, conductance[0], 0.0)
    for z in range(s.lz):
        info = jnp.where((lane == 0) & (sub == z), mat[material[z]], info)
    low = lax.broadcasted_iota(jnp.int32, (s.rows, LN), 1) < HX
    n = s.lz * s.rows
    for step, out in enumerate(outs):
        e = lax.rem(d + step, s.nd)
        right = lax.rem(e + 1, s.nd) * s.wc
        left = lax.rem(e + s.nd - 1, s.nd) * s.wc + (s.wc - LN)
        for z in range(s.lz):
            rows = slice(z * s.rows, (z + 1) * s.rows)
            out[rows, : s.wc] = f[z, :, pl.ds(pl.multiple_of(e * s.wc, LN), s.wc)]
            out[rows, s.wc :] = jnp.where(
                low,
                f[z, :, pl.ds(pl.multiple_of(right, LN), LN)],
                f[z, :, pl.ds(pl.multiple_of(left, LN), LN)],
            )
        out[n:, :] = jnp.zeros((8, s.we), F32)
        for k in range(s.nb // 8):
            out[n:, k * LN : k * LN + 4] = blocks[8 * k : 8 * k + 8, :].astype(F32)
        k = s.nb // 8
        out[n:, k * LN : (k + 1) * LN] = info


def assemble_kernel(s, idx, *refs):
    parts, (top, bot, prm) = refs[: s.nd], refs[s.nd :]
    d = idx[0]
    for step, part in enumerate(parts):
        e = lax.rem(d + s.nd - step, s.nd)
        for z in range(s.lz):
            top[s.lz * e + z] = part[z * s.rows : z * s.rows + HY, :]
            bot[s.lz * e + z] = part[z * s.rows + HY : (z + 1) * s.rows, :]
        prm[e] = part[s.lz * s.rows :, :]


def overlap(lo, size, first, past):
    return jnp.maximum(jnp.minimum(lo + size, past) - jnp.maximum(lo, first), 0.0)


def coeff_kernel(s, idx, prm, u0, d0, u1, d1, u2, l2, d2, c, c2):
    d, t = idx[0], idx[1]
    ny = s.rows * s.nt
    lane8, sub8 = iota((8, LN), 1), iota((8, LN), 0)

    def pick(tile, row, col):
        return jnp.sum(jnp.where((lane8 == col) & (sub8 == row), tile, 0.0), keepdims=True)

    info = [prm[g, :, s.nb // 8 * LN : (s.nb // 8 + 1) * LN] for g in range(s.nd)]
    cond = [pick(info[z // s.lz], z % s.lz, 0) for z in range(s.nz)]
    via = [pick(info[g], 0, 1) for g in range(s.nd)]
    vert = [
        2.0 * cond[z] * cond[min(z + 1, s.nz - 1)] / (cond[z] + cond[min(z + 1, s.nz - 1)])
        for z in range(s.nz)
    ]
    lane = iota((s.nb, LN), 1)
    blocks = []
    for g in range(s.nd):
        b = jnp.concatenate([prm[g, :, k * LN : (k + 1) * LN] for k in range(s.nb // 8)], axis=0)
        col = [jnp.sum(jnp.where(lane == j, b, 0.0), axis=1, keepdims=True) for j in range(4)]
        blocks.append((col[0], col[0] + col[2], col[1], col[1] + col[3]))

    p0 = iota((1, s.we), 1)
    col0 = d * s.wc + p0 - jnp.where(p0 >= s.wc + HX, s.we, 0)
    p1 = iota((1, s.w1), 1)
    col1 = d * s.c1 + p1 - jnp.where(p1 >= s.w1 - HX // 4, s.w1, 0)
    used1 = (p1 < s.c1 + HX // 4) | (p1 >= s.w1 - HX // 4)
    row0 = t * s.rows - HY + iota((1, LN), 1)
    row1 = t * (s.rows // 4) - (s.e1 - s.rows // 4) // 2 + iota((1, LN), 1)
    zero0 = jnp.zeros((s.re, s.we), F32)
    zero1 = jnp.zeros((s.e1, s.w1), F32)
    u0[0] = zero0
    u1[0] = zero1
    for z in range(s.nz):
        g = z // s.lz
        if z % s.lz == s.lz - 1:
            r0, r1, c0, c1 = blocks[g]
            a = overlap(row0.astype(F32), 1.0, r0, r1).astype(BF16)
            b = overlap(col0.astype(F32), 1.0, c0, c1).astype(BF16)
            u0[z + 1] = pair_dot(a, b)[: s.re] * via[g]
            a = overlap(row1.astype(F32) * 4.0, 4.0, r0, r1).astype(BF16)
            b = overlap(col1.astype(F32) * 4.0, 4.0, c0, c1).astype(BF16)
            u1[z + 1] = pair_dot(a, b)[: s.e1] * via[g]
        else:
            u0[z + 1] = zero0 + vert[z]
            u1[z + 1] = zero1 + vert[z] * 16.0
        c[z] = jnp.zeros((8, LN), F32) + cond[z]
    rr = t * s.rows - HY + iota((s.re, s.we), 0)
    pp = iota((s.re, s.we), 1)
    cc = d * s.wc + pp - jnp.where(pp >= s.wc + HX, s.we, 0)
    in0 = jnp.where((rr >= 0) & (rr < ny) & (cc >= 0) & (cc < s.width), OMEGA, 0.0)
    rr = t * (s.rows // 4) - (s.e1 - s.rows // 4) // 2 + iota((s.e1, s.w1), 0)
    pp = iota((s.e1, s.w1), 1)
    cc = d * s.c1 + pp - jnp.where(pp >= s.w1 - HX // 4, s.w1, 0)
    in1 = (rr >= 0) & (rr < ny // 4) & (cc >= 0) & (cc < s.width // 4)
    in1 = jnp.where(in1 & ((pp < s.c1 + HX // 4) | (pp >= s.w1 - HX // 4)), OMEGA, 0.0)
    for z in range(s.nz):
        d0[z] = in0 / (4.0 * cond[z] + u0[z + 1] + u0[z])
        d1[z] = in1 / (16.0 * cond[z] + u1[z + 1] + u1[z])

    group = iota((1, LN), 1) // s.c2
    xin = iota((1, LN), 1) % s.c2

    def by_group(values):
        out = jnp.zeros((1, LN), F32)
        for g in range(s.nd):
            out = jnp.where(group == g, values[g], out)
        return out

    cl = [by_group([cond[s.lz * g + a] for g in range(s.nd)]) * 16.0 for a in range(s.lz)]
    vl = [by_group([vert[s.lz * g + a] for g in range(s.nd)]) * 256.0 for a in range(s.lz)]
    vial = by_group(via)
    row2 = (iota((1, LN), 1) * 16).astype(F32)
    ra = jnp.concatenate([overlap(row2, 16.0, b[0], b[1]) for b in blocks], axis=0).astype(BF16)
    zero2 = jnp.zeros((s.nt, LN), F32)
    for a in range(s.lz):
        c2[a] = jnp.zeros((8, LN), F32) + cl[a]
    for e in range(s.nd):
        col2 = ((e * s.c2 + xin) * 16).astype(F32)
        cb = jnp.concatenate(
            [jnp.where(group == g, overlap(col2, 16.0, b[2], b[3]), 0.0) for g, b in enumerate(blocks)],
            axis=0,
        ).astype(BF16)
        v2 = pair_dot(ra, cb)[: s.nt] * vial
        ups = [zero2 + vl[a] for a in range(s.lz - 1)] + [v2]
        first = jnp.where(iota((s.nt, LN), 1) >= s.c2, pltpu.roll(v2, s.c2, 1), 0.0)
        lows = [first] + ups[:-1]
        for a in range(s.lz):
            q = e * s.lz + a
            u2[q] = ups[a]
            l2[q] = lows[a]
            d2[q] = OMEGA / (4.0 * cl[a] + ups[a] + lows[a])


def neighbours(v, c):
    rows, cols = v.shape
    side = (
        pltpu.roll(v, 1, 0) + pltpu.roll(v, rows - 1, 0) + (pltpu.roll(v, 1, 1) + pltpu.roll(v, cols - 1, 1))
    )
    return c * side


def off_diagonal(src, z, u, c, scale):
    v = src[z + 1]
    return v, neighbours(v, c[z, 0:1, 0:1] * scale) + u[z + 1] * src[z + 2] + u[z] * src[z]


def sweep(s, src, dst, f, u, dd, c, scale):
    def body(z, carry):
        v, g = off_diagonal(src, z, u, c, scale)
        dst[z + 1] = (1.0 - OMEGA) * v + dd[z] * (f[z] + g)
        return carry

    lax.fori_loop(0, s.nz, body, 0)


def residual(src, z, f, u, c, scale):
    v, g = off_diagonal(src, z, u, c, scale)
    return f[z] + g - (4.0 * scale * c[z, 0:1, 0:1] + u[z + 1] + u[z]) * v


def zero_ends(s, *bufs):
    for b in bufs:
        b[0] = jnp.zeros(b.shape[1:], F32)
        b[s.nz + 1] = jnp.zeros(b.shape[1:], F32)


def restrict(s, src, f, u, c, down, row_buf, sums, r1):
    def body(z, carry):
        r = residual(src, z, f, u, c, 1.0)
        at = pl.ds(pl.multiple_of(z * s.r1, 8), s.r1)
        for j in range(s.we // LN):
            row_buf[j * s.re : (j + 1) * s.re, :] = r[:, j * LN : (j + 1) * LN]
        for j in range(s.we // LN):
            part = [row_buf[pl.ds(j * s.re + k, s.r1, stride=4), :] for k in range(4)]
            sums[at, j * LN : (j + 1) * LN] = (part[0] + part[1]) + (part[2] + part[3])
        return carry

    lax.fori_loop(0, s.nz, body, 0)
    r1[...] = split_dot(sums[...], down[...]).reshape(s.nz, s.r1, s.w1)


def fine_first_kernel(s, above, top, bot, below, u0, d0, c, down, f, v2, r1, va, row_buf, sums):
    zero_ends(s, va, v2)

    def body(z, carry):
        for k, ref in enumerate((above, top, bot, below)):
            rows = slice(k * HY, (k + 1) * HY)
            x = ref[z]
            f[z, rows, :] = x
            va[z + 1, rows, :] = d0[z, rows, :] * x
        return carry

    lax.fori_loop(0, s.nz, body, 0)
    sweep(s, va, v2, f, u0, d0, c, 1.0)
    restrict(s, v2, f, u0, c, down, row_buf, sums, r1)


def middle_first_kernel(s, r1p, r1, r1n, u1, d1, c, down2, rx, w2, send, wa, gather):
    own = s.rows // 4
    pad = (s.e1 - own) // 2
    sub = iota((s.r1, s.w1), 0)
    zero_ends(s, wa, w2)

    def body(z, carry):
        mid = pltpu.roll(r1[z], s.r1 // 2, 0)
        up = jnp.where(sub >= pad, mid, r1p[z])
        down = jnp.where(sub < own - (s.r1 - pad), mid, r1n[z])
        rx[z, : s.r1, :] = up
        rx[z, s.r1 :, :] = down
        wa[z + 1, : s.r1, :] = d1[z, : s.r1, :] * up
        wa[z + 1, s.r1 :, :] = d1[z, s.r1 :, :] * down
        return carry

    lax.fori_loop(0, s.nz, body, 0)
    sweep(s, wa, w2, rx, u1, d1, c, 4.0)
    row = iota((s.e1, LN), 0)
    mine = (row >= pad) & (row < pad + own)
    for z in range(s.nz):
        r = residual(w2, z, rx, u1, c, 4.0)[:, :LN]
        total = jnp.sum(jnp.where(mine, r, 0.0), axis=0, keepdims=True)
        g, a = z // s.lz, z % s.lz
        gather[a : a + 1, g * LN : (g + 1) * LN] = total
        gather[a + s.lz : a + s.lz + 1, g * LN : (g + 1) * LN] = total
    tile = split_dot(gather[...], down2[...])
    for k in range(s.nd * s.nt * s.chunk // 8):
        send[8 * k : 8 * k + 8, :] = tile


def coarse(s, got, u2, l2, d2, c2, cs):
    lane = iota((s.nt, LN), 1)
    x, t = lane % s.c2, iota((s.nt, LN), 0)
    first_x, last_x = x == 0, x == s.c2 - 1
    slabs = s.nd * s.lz
    rhs, v = [], []
    for q in range(slabs):
        e, a = q // s.lz, q % s.lz
        r = got[pl.ds(e * s.nt * s.lz + a, s.nt, stride=s.lz), :]
        rhs.append(r)
        v.append(d2[q] * r)
    zero = jnp.zeros((s.nt, LN), F32)

    def body(_, v):
        new = []
        for q in range(slabs):
            e, a = q // s.lz, q % s.lz
            w = v[q]
            right = pltpu.roll(v[q + s.lz], s.c2 - 1, 1) if e < s.nd - 1 else zero
            left = pltpu.roll(v[q - s.lz], LN - (s.c2 - 1), 1) if e > 0 else zero
            side = jnp.where(last_x, right, pltpu.roll(w, LN - 1, 1))
            side += jnp.where(first_x, left, pltpu.roll(w, 1, 1))
            side += jnp.where(t == s.nt - 1, 0.0, pltpu.roll(w, s.nt - 1, 0))
            side += jnp.where(t == 0, 0.0, pltpu.roll(w, 1, 0))
            if a < s.lz - 1:
                up = v[q + 1]
            else:
                up = jnp.where(lane >= LN - s.c2, 0.0, pltpu.roll(v[q - a], LN - s.c2, 1))
            if a > 0:
                down = v[q - 1]
            else:
                down = jnp.where(lane < s.c2, 0.0, pltpu.roll(v[q + s.lz - 1], s.c2, 1))
            g = c2[a, 0:1, :] * side + u2[q] * up + l2[q] * down
            new.append((1.0 - OMEGA) * w + d2[q] * (rhs[q] + g))
        return tuple(new)

    v = lax.fori_loop(0, NC - 1, body, tuple(v))
    for q in range(slabs):
        cs[q, : HY, :] = jnp.zeros((HY, LN), F32)
        cs[q, HY + s.nt :, :] = jnp.zeros((HY, LN), F32)
        cs[q, HY : HY + s.nt, :] = v[q]


def middle_last(s, d, t, cs, spread2, w2, rx, u1, d1, c, comp, wa, wb):
    own = s.rows // 4
    pad = (s.e1 - own) // 2
    row = iota((s.e1, LN), 0)
    lane = iota((s.e1, LN), 1)
    after = lax.rem(d + 1, s.nd) * s.lz
    before = lax.rem(d + s.nd - 1, s.nd) * s.lz
    zero_ends(s, wa, wb)
    for a in range(s.lz):
        rows = []
        for base in (d * s.lz, after, before):
            out = jnp.zeros((s.e1, LN), F32)
            for k in range(-2, 3):
                lo = pad + own * k
                line = cs[base + a, pl.ds(HY + t + k, 1), :]
                out = jnp.where((row >= lo) & (row < lo + own), line, out)
            rows.append(out)
        for g in range(s.nd):
            turn = [pltpu.roll(r, (sh - g * s.c2) % LN, 1) if (sh - g * s.c2) % LN else r
                    for r, sh in zip(rows, (0, s.c2, LN - s.c2))]
            z = g * s.lz + a
            comp[z * s.e1 : (z + 1) * s.e1, :] = jnp.where(
                lane < s.c2, turn[0], jnp.where(lane < LN // 2, turn[1], turn[2])
            )
    wa[1 : s.nz + 1] = split_dot(comp[...], spread2[...]).reshape(s.nz, s.e1, s.w1)

    def body(z, carry):
        wa[z + 1] = jnp.where(d1[z] > 0.0, w2[z + 1] + wa[z + 1], 0.0)
        return carry

    lax.fori_loop(0, s.nz, body, 0)
    sweep(s, wa, wb, rx, u1, d1, c, 4.0)
    sweep(s, wb, wa, rx, u1, d1, c, 4.0)


def correct_fine(s, w, v, spread1, wide, dst):
    first = (s.e1 - s.r1) // 2
    lhs = w[1 : s.nz + 1, first : first + s.r1, :].reshape(s.nz * s.r1, s.w1)
    wide[...] = split_dot(lhs, spread1[...])
    zero_ends(s, dst)
    upper = iota((8, s.we), 0) < 4

    def body(z, carry):
        x = wide[pl.ds(pl.multiple_of(z * s.r1, 8), s.r1), :]
        for k in range(s.r1 // 2):
            rows = slice(8 * k, 8 * k + 8)
            step = jnp.where(upper, x[2 * k : 2 * k + 1, :], x[2 * k + 1 : 2 * k + 2, :])
            dst[z + 1, rows, :] = v[z + 1, rows, :] + step
        return carry

    lax.fori_loop(0, s.nz, body, 0)


def back_kernel(
    s, idx, got, u2, l2, d2, c2, w2, rx, u1, d1, c, v2, f, u0, d0, spread2, spread1, down,
    v, r1, cs, comp, wa, wb, va, wide, row_buf,
):
    d, t = idx[0], idx[1]
    coarse(s, got, u2, l2, d2, c2, cs)
    middle_last(s, d, t, cs, spread2, w2, rx, u1, d1, c, comp, wa, wb)
    correct_fine(s, wa, v2, spread1, wide, va)
    zero_ends(s, v)
    sweep(s, va, v, f, u0, d0, c, 1.0)
    sweep(s, v, va, f, u0, d0, c, 1.0)
    sweep(s, va, v, f, u0, d0, c, 1.0)
    sweep(s, v, va, f, u0, d0, c, 1.0)

    def body(z, carry):
        v[z + 1] = va[z + 1]
        return carry

    lax.fori_loop(0, s.nz, body, 0)
    restrict(s, va, f, u0, c, down, row_buf, wide, r1)


def last_kernel(
    s, idx, got, u2, l2, d2, c2, w2, rx, u1, d1, c, v2, f, u0, d0, spread2, spread1,
    *refs,
):
    outs, (cs, comp, wa, wb, va, vb, wide) = refs[: s.nd], refs[s.nd :]
    d, t = idx[0], idx[1]
    coarse(s, got, u2, l2, d2, c2, cs)
    middle_last(s, d, t, cs, spread2, w2, rx, u1, d1, c, comp, wa, wb)
    correct_fine(s, wa, v2, spread1, wide, va)
    zero_ends(s, vb)
    sweep(s, va, vb, f, u0, d0, c, 1.0)
    sweep(s, vb, va, f, u0, d0, c, 1.0)
    for step, out in enumerate(outs):
        e = lax.rem(d + step, s.nd)
        for a in range(s.lz):
            z = e * s.lz + a
            out[0, a] = va[z + 1, HY : HY + s.rows, : s.wc]
            out[1, a] = residual(va, z, f, u0, c, 1.0)[HY : HY + s.rows, : s.wc]


def unpack_kernel(s, idx, *refs):
    parts, outs = refs[: s.nd], refs[s.nd :]
    d = idx[0]
    for step, part in enumerate(parts):
        e = lax.rem(d + s.nd - step, s.nd)
        cols = pl.ds(pl.multiple_of(e * s.wc, LN), s.wc)
        for k, out in enumerate(outs):
            for a in range(s.lz):
                out[a, :, cols] = part[k, a]


def call(name, kernel, s, n_smem, outs, scratch=(), flops=0):
    shapes = [jax.ShapeDtypeStruct(o, F32) for o in outs]
    vm = pl.BlockSpec(memory_space=pltpu.VMEM)

    def run(*args):
        total = sum(int(np.prod(a.shape)) * 4 for a in args) + sum(int(np.prod(o)) * 4 for o in outs)
        return pl.pallas_call(
            functools.partial(kernel, s),
            name=name,
            out_shape=shapes,
            in_specs=[pl.BlockSpec(memory_space=pltpu.SMEM)] * n_smem + [vm] * (len(args) - n_smem),
            out_specs=[vm] * len(outs),
            scratch_shapes=[pltpu.VMEM(x, F32) for x in scratch],
            compiler_params=pltpu.CompilerParams(vmem_limit_bytes=32 << 20),
            cost_estimate=pl.CostEstimate(flops=flops, bytes_accessed=total, transcendentals=0),
        )(*args)

    return run


def shift(x, axis, by):
    n = lax.axis_size(axis)
    return lax.ppermute(x, axis, [(i, (i + by) % n) for i in range(n)])


def tables(s):
    p = np.arange(s.we)
    at = p // 4 + np.where(p >= s.wc + HX, s.w1 - s.we // 4, 0)
    down = (at[:, None] == np.arange(s.w1)[None, :])
    q = np.arange(s.w1)
    k = q // 4 + np.where(q >= s.w1 - HX // 4, LN - s.w1 // 4, 0)
    used = (q < s.c1 + HX // 4) | (q >= s.w1 - HX // 4)
    spread2 = (np.arange(LN)[:, None] == k[None, :]) & used[None, :]
    r = np.arange(s.nd * LN)
    down2 = ((r // LN) * s.c2 + (r % LN) // 4)[:, None] == np.arange(LN)[None, :]
    return [jnp.asarray(m, BF16) for m in (down, down.T, spread2, down2)]


def local(s, source_heating, material_thermal_values, layer_material, via_conductance, via_blocks):
    idx = jnp.stack([lax.axis_index("die"), lax.axis_index("tile")]).astype(jnp.int32)
    down, spread1, spread2, down2 = tables(s)
    packed = (s.lz * s.rows + 8, s.we)
    sends = call("pack", pack_kernel, s, 4, [packed] * s.nd)(
        idx, material_thermal_values, layer_material, via_conductance, via_blocks[0], source_heating
    )
    parts = [sends[0]] + [shift(sends[k], "die", k) for k in range(1, s.nd)]
    half = (s.nz, HY, s.we)
    top, bot, prm = call("assemble", assemble_kernel, s, 1, [half, half, (s.nd, 8, s.we)])(idx, *parts)
    above, below = shift(bot, "tile", 1), shift(top, "tile", -1)
    fine, fine_v = (s.nz, s.re, s.we), (s.nz + 2, s.re, s.we)
    mid, mid_v, mid_u = (s.nz, s.e1, s.w1), (s.nz + 2, s.e1, s.w1), (s.nz + 1, s.e1, s.w1)
    small = (s.nz, s.r1, s.w1)
    flat = (s.nz * s.r1, s.we)
    rows_buf = (s.re * s.we // LN, LN)
    slab = (s.nd * s.lz, s.nt, LN)
    u0, d0, u1, d1, u2, l2, d2, c, c2 = call(
        "coeff", coeff_kernel, s, 1,
        [(s.nz + 1, s.re, s.we), fine, mid_u, mid, slab, slab, slab, (s.nz, 8, LN), (s.lz, 8, LN)],
    )(idx, prm)
    f, v, r1 = call(
        "fine_first", fine_first_kernel, s, 0, [fine, fine_v, small], [fine_v, rows_buf, flat]
    )(above, top, bot, below, u0, d0, c, down)
    spaces = [(s.nd * s.lz, s.nt + 2 * HY, LN), (s.nz * s.e1, LN), mid_v, mid_v, fine_v]
    for cycle in range(2):
        rx, w2, send = call(
            "middle_first", middle_first_kernel, s, 0,
            [mid, mid_v, (s.nd * s.nt * s.chunk, LN)], [mid_v, (8, s.nd * LN)],
        )(shift(r1, "tile", 1), r1, shift(r1, "tile", -1), u1, d1, c, down2)
        got = lax.all_to_all(send, ("die", "tile"), 0, 0, tiled=True)
        args = (idx, got, u2, l2, d2, c2, w2, rx, u1, d1, c, v, f, u0, d0, spread2, spread1)
        if cycle == 0:
            v, r1 = call(
                "back", back_kernel, s, 1, [fine_v, small], spaces + [flat, rows_buf]
            )(*args, down)
    piece = (2, s.lz, s.rows, s.wc)
    sends = call("last", last_kernel, s, 1, [piece] * s.nd, spaces + [fine_v, flat])(*args)
    parts = [sends[0]] + [shift(sends[k], "die", k) for k in range(1, s.nd)]
    whole = (s.lz, s.rows, s.width)
    return tuple(call("unpack", unpack_kernel, s, 1, [whole, whole])(idx, *parts))


def solution(mesh):
    in_specs = (P("die", "tile", None), P(), P("die"), P("die"), P("die", None, None))
    out_specs = (P("die", "tile", None), P("die", "tile", None))

    def body(f, mat, material, conductance, blocks):
        s = Sizes(mesh.shape, f.shape, blocks.shape[1])
        return local(s, f, mat, material, conductance, blocks)

    return jax.shard_map(body, mesh=mesh, in_specs=in_specs, out_specs=out_specs, check_vma=False)
```

```python
import functools

import jax
import jax.numpy as jnp
import numpy as np
from jax import lax
from jax.experimental import pallas as pl
from jax.experimental.pallas import tpu as pltpu
from jax.sharding import PartitionSpec as P

OMEGA = 0.8
NC = 6
LN = 128
HX = 64
HY = 8
F32 = jnp.float32
BF16 = jnp.bfloat16


def iota(shape, axis):
    return lax.broadcasted_iota(jnp.int32, shape, axis)


def split_dot(x, m):
    hi = x.astype(BF16)
    lo = (x - hi.astype(F32)).astype(BF16)
    return jnp.dot(hi, m, preferred_element_type=F32) + jnp.dot(lo, m, preferred_element_type=F32)


def pair_dot(a, b):
    return lax.dot_general(a, b, (((0,), (0,)), ((), ())), preferred_element_type=F32)


class Sizes:
    def __init__(self, mesh_shape, f_shape, n_blocks):
        self.nd, self.nt = mesh_shape["die"], mesh_shape["tile"]
        self.lz, self.rows, self.width = f_shape
        self.nb = n_blocks
        self.wc = self.width // self.nd
        self.we = self.wc + LN
        self.j0 = self.we // LN
        self.nz = self.nd * self.lz
        self.re = self.rows + 2 * HY
        self.own1 = self.rows // 4
        self.r1 = self.re // 4
        self.c1 = self.wc // 4
        self.e1 = 2 * self.r1
        self.pad1 = (self.e1 - self.own1) // 2
        self.j1 = 2
        self.w1 = self.j1 * LN
        self.c2 = self.wc // 16
        self.part = self.lz * self.j0 * self.rows
        assert self.rows == 16 and self.lz == 4 and self.c1 == LN
        assert self.nd * self.c2 == LN and self.nb <= LN and self.nt <= LN and self.nt % 8 == 0


def place():
    return lax.axis_index("die"), lax.axis_index("tile")


def tiles(j):
    return slice(j * LN, (j + 1) * LN)


def windows(lo, hi):
    return [min(r, hi - 8) for r in range(lo, hi, 8)]


def pack_kernel(s, mat_h, material_h, conductance_h, blocks_h, f_h, *refs):
    outs, (mat, material, conductance, blocks, f, sem) = refs[: s.nd], refs[s.nd :]
    pairs = [(f_h, f), (mat_h, mat), (material_h, material), (conductance_h, conductance), (blocks_h, blocks)]
    copies = [pltpu.make_async_copy(a, b, sem.at[k]) for k, (a, b) in enumerate(pairs)]
    for c in copies:
        c.start()
    for c in copies[1:]:
        c.wait()
    d, _ = place()
    lane, sub = iota((8, LN), 1), iota((8, LN), 0)
    info = jnp.where((sub == 5) & (lane == 0), conductance[0], 0.0)
    for z in range(s.lz):
        info = jnp.where((sub == 4) & (lane == z), mat[material[z]], info)
    for out in outs:
        out[s.part :, :] = info
        out[s.part : s.part + 4, : s.nb] = blocks[...].astype(F32)
    copies[0].wait()
    low = iota((s.rows, LN), 1) < HX
    for step, out in enumerate(outs):
        e = lax.rem(d + step, s.nd)
        right = lax.rem(e + 1, s.nd) * s.wc
        left = lax.rem(e + s.nd - 1, s.nd) * s.wc + (s.wc - LN)

        def column(z, at):
            return f[z, :, pl.ds(pl.multiple_of(at, LN), LN)]

        for z in range(s.lz):
            for j in range(s.j0):
                at = (z * s.j0 + j) * s.rows
                if j < s.j0 - 1:
                    x = column(z, e * s.wc + j * LN)
                else:
                    x = jnp.where(low, column(z, right), column(z, left))
                out[at : at + s.rows, :] = x


def assemble_kernel(s, *refs):
    parts, (top, bot, prm) = refs[: s.nd], refs[s.nd :]
    d, _ = place()
    n = s.lz * s.j0
    for step, part in enumerate(parts):
        e = lax.rem(d + s.nd - step, s.nd)
        for q in range(n):
            top[n * e + q] = part[q * s.rows : q * s.rows + HY, :]
            bot[n * e + q] = part[q * s.rows + HY : (q + 1) * s.rows, :]
        prm[e] = part[s.part :, :]


def overlap(lo, size, first, past):
    return jnp.maximum(jnp.minimum(lo + size, past) - jnp.maximum(lo, first), 0.0)


def coeff_kernel(s, prm, via0, d0, via1, d1, u2, l2, d2, c, u, c2):
    d, t = place()
    ny = s.rows * s.nt
    lane8, sub8 = iota((8, LN), 1), iota((8, LN), 0)

    def pick(tile, row, col):
        return jnp.sum(jnp.where((lane8 == col) & (sub8 == row), tile, 0.0), keepdims=True)

    info = [prm[g] for g in range(s.nd)]
    cond = [pick(info[z // s.lz], 4, z % s.lz) for z in range(s.nz)]
    via = [pick(info[g], 5, 0) for g in range(s.nd)]
    vert = [
        2.0 * cond[z] * cond[min(z + 1, s.nz - 1)] / (cond[z] + cond[min(z + 1, s.nz - 1)])
        for z in range(s.nz)
    ]
    blocks = []
    for g in range(s.nd):
        b = jnp.transpose(info[g])
        lane = iota((LN, 8), 1)
        col = [jnp.sum(jnp.where(lane == k, b, 0.0), axis=1, keepdims=True) for k in range(4)]
        col = [x[: s.nb] for x in col]
        blocks.append((col[0], col[0] + col[2], col[1], col[1] + col[3]))

    def columns(n, own, shape, axis):
        p = iota(shape, axis)
        return p, jnp.where(p >= n - own // 8, p - n, p)

    row0 = t * s.rows - HY + iota((1, LN), 1)
    row1 = t * s.own1 - s.pad1 + iota((1, LN), 1)
    _, col0 = columns(s.we, s.wc, (1, s.we), 1)
    _, col1 = columns(s.w1, s.c1, (1, s.w1), 1)
    col0 += d * s.wc
    col1 += d * s.c1
    via0[0] = jnp.zeros(via0.shape[1:], F32)
    via1[0] = jnp.zeros(via1.shape[1:], F32)
    for g in range(s.nd):
        r0, r1, c0, c1 = blocks[g]
        a = overlap(row0.astype(F32), 1.0, r0, r1).astype(BF16)
        b = overlap(col0.astype(F32), 1.0, c0, c1).astype(BF16)
        m = pair_dot(a, b)[: s.re] * via[g]
        for j in range(s.j0):
            via0[g + 1, j] = m[:, tiles(j)]
        a = overlap(row1.astype(F32) * 4.0, 4.0, r0, r1).astype(BF16)
        b = overlap(col1.astype(F32) * 4.0, 4.0, c0, c1).astype(BF16)
        m = pair_dot(a, b)[: s.e1] * via[g]
        for j in range(s.j1):
            via1[g + 1, j] = m[:, tiles(j)]
    for z in range(s.nz):
        c[z] = jnp.zeros((8, LN), F32) + cond[z]
        u[z] = jnp.zeros((8, LN), F32) + vert[z]

    rr = t * s.rows - HY + iota((s.re, s.we), 0)
    _, cc = columns(s.we, s.wc, (s.re, s.we), 1)
    cc += d * s.wc
    in0 = jnp.where((rr >= 0) & (rr < ny) & (cc >= 0) & (cc < s.width), OMEGA, 0.0)
    rr = t * s.own1 - s.pad1 + iota((s.e1, s.w1), 0)
    pp, cc = columns(s.w1, s.c1, (s.e1, s.w1), 1)
    cc += d * s.c1
    in1 = (rr >= 0) & (rr < ny // 4) & (cc >= 0) & (cc < s.width // 4)
    in1 = jnp.where(in1 & ((pp < s.c1 + HX // 4) | (pp >= s.w1 - HX // 4)), OMEGA, 0.0)
    for level, (inside, nj, vp, out) in enumerate(((in0, s.j0, via0, d0), (in1, s.j1, via1, d1))):
        for z in range(s.nz):
            g, a = z // s.lz, z % s.lz
            const = 4.0 * cond[z] * 4.0**level
            if a < s.lz - 1:
                const = const + vert[z] * 16.0**level
            if a > 0:
                const = const + vert[z - 1] * 16.0**level
            for j in range(nj):
                diag = const
                if a == s.lz - 1:
                    diag = diag + vp[g + 1, j]
                if a == 0:
                    diag = diag + vp[g, j]
                out[z, j] = inside[:, tiles(j)] / diag

    group = iota((1, LN), 1) // s.c2
    xin = iota((1, LN), 1) % s.c2

    def by_group(values):
        out = jnp.zeros((1, LN), F32)
        for g in range(s.nd):
            out = jnp.where(group == g, values[g], out)
        return out

    cl = [by_group([cond[s.lz * g + a] for g in range(s.nd)]) * 16.0 for a in range(s.lz)]
    vl = [by_group([vert[s.lz * g + a] for g in range(s.nd)]) * 256.0 for a in range(s.lz)]
    vial = by_group(via)
    row2 = (iota((1, LN), 1) * 16).astype(F32)
    ra = jnp.concatenate([overlap(row2, 16.0, b[0], b[1]) for b in blocks], axis=0).astype(BF16)
    zero2 = jnp.zeros((s.nt, LN), F32)
    for a in range(s.lz):
        c2[a] = jnp.zeros((8, LN), F32) + cl[a]
    for e in range(s.nd):
        col2 = ((e * s.c2 + xin) * 16).astype(F32)
        cb = jnp.concatenate(
            [jnp.where(group == g, overlap(col2, 16.0, b[2], b[3]), 0.0) for g, b in enumerate(blocks)],
            axis=0,
        ).astype(BF16)
        v2 = pair_dot(ra, cb)[: s.nt] * vial
        ups = [zero2 + vl[a] for a in range(s.lz - 1)] + [v2]
        first = jnp.where(iota((s.nt, LN), 1) >= s.c2, pltpu.roll(v2, s.c2, 1), 0.0)
        lows = [first] + ups[:-1]
        for a in range(s.lz):
            q = e * s.lz + a
            u2[q] = ups[a]
            l2[q] = lows[a]
            d2[q] = OMEGA / (4.0 * cl[a] + ups[a] + lows[a])


class Level:
    def __init__(self, s, level, via, inv, c, u):
        self.s, self.via, self.inv, self.c, self.u = s, via, inv, c, u
        self.nj = (s.j0, s.j1)[level]
        self.cs, self.us = 4.0**level, 16.0**level

    def layers(self, body):
        s = self.s

        def group(g, carry):
            for a in range(s.lz):
                z = g * s.lz + a
                if a < s.lz - 1:
                    const_up = self.u[z] * self.us
                    up = lambda j, rows, k=const_up: k
                else:
                    up = lambda j, rows: self.via[g + 1, j, rows, :]
                if a > 0:
                    const_down = self.u[z - 1] * self.us
                    down = lambda j, rows, k=const_down: k
                else:
                    down = lambda j, rows: self.via[g, j, rows, :]
                body(z, self.c[z] * self.cs, up, down)
            return carry

        lax.fori_loop(0, s.nd, group, 0)

    def off_diagonal(self, src, z, r, c, up, down, count=None):
        n = self.nj
        lane = iota((8, LN), 1)
        first, last = lane == 0, lane == LN - 1
        rows = pl.ds(r, 8)
        v = [src[z + 1, j, rows, :] for j in range(n)]
        ahead = [pltpu.roll(x, LN - 1, 1) for x in v]
        behind = [pltpu.roll(x, 1, 1) for x in v]
        out = []
        for j in range(n if count is None else count):
            x = jnp.where(last, ahead[(j + 1) % n], ahead[j]) + jnp.where(first, behind[j - 1], behind[j])
            y = src[z + 1, j, pl.ds(r - 1, 8), :] + src[z + 1, j, pl.ds(r + 1, 8), :]
            k_up, k_down = up(j, rows), down(j, rows)
            g = c * (x + y) + (k_up * src[z + 2, j, rows, :] + k_down * src[z, j, rows, :])
            out.append((j, v[j], g, k_up, k_down))
        return out

    def sweep(self, src, dst, f, lo, hi):
        def body(z, c, up, down):
            for r in windows(lo, hi):
                rows = pl.ds(r, 8)
                for j, v, g, _, _ in self.off_diagonal(src, z, r, c, up, down):
                    dst[z + 1, j, rows, :] = (1.0 - OMEGA) * v + self.inv[z, j, rows, :] * (f[z, j, rows, :] + g)

        self.layers(body)

    def residual(self, src, f, lo, hi, put, count=None):
        def body(z, c, up, down):
            four = 4.0 * c
            for r in windows(lo, hi):
                for j, v, g, k_up, k_down in self.off_diagonal(src, z, r, c, up, down, count):
                    put(z, j, r, (f[z, j, pl.ds(r, 8), :] + g) - (four + k_up + k_down) * v)

        self.layers(body)


def zero_ends(s, *bufs):
    for b in bufs:
        b[0] = jnp.zeros(b.shape[1:], F32)
        b[s.nz + 1] = jnp.zeros(b.shape[1:], F32)


def restrict(s, level, src, f, lo, hi, down, rbuf, sums, r1):
    n = s.nz * s.j0 * s.re
    for k in range(0, s.nz * s.j0):
        if lo > 0:
            rbuf[k * s.re : k * s.re + lo, :] = jnp.zeros((lo, LN), F32)
            rbuf[k * s.re + hi : (k + 1) * s.re, :] = jnp.zeros((s.re - hi, LN), F32)

    def put(z, j, r, x):
        rbuf[pl.ds((z * s.j0 + j) * s.re + r, 8), :] = x

    level.residual(src, f, lo, hi, put)

    def body(z, carry):
        for j in range(s.j0):
            part = [rbuf[pl.ds((z * s.j0 + j) * s.re + k, s.r1, stride=4), :] for k in range(4)]
            sums[z, :, tiles(j)] = (part[0] + part[1]) + (part[2] + part[3])
        return carry

    lax.fori_loop(0, s.nz, body, 0)
    out = split_dot(sums[...].reshape(s.nz * s.r1, s.we), down[...])
    for z in range(s.nz):
        for j in range(s.j1):
            r1[z, j] = out[z * s.r1 : (z + 1) * s.r1, tiles(j)]


def fine_first_kernel(s, above, top, bot, below, via0, d0, c, u, down, f, v2, r1, va, rbuf, sums):
    level = Level(s, 0, via0, d0, c, u)
    zero_ends(s, va, v2)

    def body(z, carry):
        for j in range(s.j0):
            for k, ref in enumerate((above, top, bot, below)):
                rows = slice(k * HY, (k + 1) * HY)
                x = ref[z * s.j0 + j]
                f[z, j, rows, :] = x
                va[z + 1, j, rows, :] = d0[z, j, rows, :] * x
        return carry

    lax.fori_loop(0, s.nz, body, 0)
    level.sweep(va, v2, f, 1, s.re - 1)
    restrict(s, level, v2, f, HY - 4, s.re - HY + 4, down, rbuf, sums, r1)


def middle_first_kernel(s, r1p, r1, r1n, via1, d1, c, u, down2, rx, w2, send, wa, buf):
    level = Level(s, 1, via1, d1, c, u)
    half, own, pad = s.r1, s.own1, s.pad1
    sub = iota((half, LN), 0)
    zero_ends(s, wa, w2)

    def body(z, carry):
        for j in range(s.j1):
            mid = pltpu.roll(r1[z, j], half // 2, 0)
            up = jnp.where(sub >= pad, mid, r1p[z, j])
            down = jnp.where(sub < own - (half - pad), mid, r1n[z, j])
            rx[z, j, :half, :] = up
            rx[z, j, half:, :] = down
            wa[z + 1, j, :half, :] = d1[z, j, :half, :] * up
            wa[z + 1, j, half:, :] = d1[z, j, half:, :] * down
        return carry

    lax.fori_loop(0, s.nz, body, 0)
    level.sweep(wa, w2, rx, pad - 4, pad + own + 4)

    def put(z, j, r, x):
        buf[pl.ds(pl.multiple_of(z * 8, 8), 8), :] = x

    level.residual(w2, rx, pad - 2, pad + own + 2, put, 1)
    sub8, group = iota((8, LN), 0), iota((8, LN), 1) // s.c2
    tile = jnp.zeros((8, LN), F32)
    for h in range(s.nz // 8):
        part = [buf[pl.ds(64 * h + 2 + k, 8, stride=8), :] for k in range(own)]
        x = split_dot((part[0] + part[1]) + (part[2] + part[3]), down2[...])
        y = pltpu.roll(x, 4, 0)
        for g in (2 * h, 2 * h + 1):
            tile = jnp.where(group == g, jnp.where((sub8 < 4) == (g % 2 == 0), x, y), tile)
    for k in range(s.nd * s.nt * s.lz // 8):
        send[8 * k : 8 * k + 8, :] = tile


def coarse(s, got, u2, l2, d2, c2, cs):
    lane = iota((s.nt, LN), 1)
    x, t = lane % s.c2, iota((s.nt, LN), 0)
    first_x, last_x = x == 0, x == s.c2 - 1
    slabs = s.nd * s.lz
    rhs, v = [], []
    for q in range(slabs):
        e, a = q // s.lz, q % s.lz
        r = got[pl.ds(e * s.nt * s.lz + a, s.nt, stride=s.lz), :]
        rhs.append(r)
        v.append(d2[q] * r)
    zero = jnp.zeros((s.nt, LN), F32)

    def body(_, v):
        new = []
        for q in range(slabs):
            e, a = q // s.lz, q % s.lz
            w = v[q]
            right = pltpu.roll(v[q + s.lz], s.c2 - 1, 1) if e < s.nd - 1 else zero
            left = pltpu.roll(v[q - s.lz], LN - (s.c2 - 1), 1) if e > 0 else zero
            side = jnp.where(last_x, right, pltpu.roll(w, LN - 1, 1))
            side += jnp.where(first_x, left, pltpu.roll(w, 1, 1))
            side += jnp.where(t == s.nt - 1, 0.0, pltpu.roll(w, s.nt - 1, 0))
            side += jnp.where(t == 0, 0.0, pltpu.roll(w, 1, 0))
            if a < s.lz - 1:
                up = v[q + 1]
            else:
                up = jnp.where(lane >= LN - s.c2, 0.0, pltpu.roll(v[q - a], LN - s.c2, 1))
            if a > 0:
                down = v[q - 1]
            else:
                down = jnp.where(lane < s.c2, 0.0, pltpu.roll(v[q + s.lz - 1], s.c2, 1))
            g = c2[a, 0:1, :] * side + u2[q] * up + l2[q] * down
            new.append((1.0 - OMEGA) * w + d2[q] * (rhs[q] + g))
        return tuple(new)

    v = lax.fori_loop(0, NC - 1, body, tuple(v))
    for q in range(slabs):
        cs[q, :HY, :] = jnp.zeros((HY, LN), F32)
        cs[q, HY + s.nt :, :] = jnp.zeros((HY, LN), F32)
        cs[q, HY : HY + s.nt, :] = v[q]


def middle_last(s, level, cs, spread2, w2, rx, comp, wide, wa, wb):
    d, t = place()
    lane, upper = iota((8, LN), 1), iota((8, LN), 0) < 4
    after = lax.rem(d + 1, s.nd) * s.lz
    before = lax.rem(d + s.nd - 1, s.nd) * s.lz
    zero_ends(s, wa, wb)
    for a in range(s.lz):
        rows = [cs[base + a, pl.ds(HY - 1 + t, 8), :] for base in (d * s.lz, after, before)]
        for g in range(s.nd):
            turn = []
            for r, by in zip(rows, (0, s.c2, LN - s.c2)):
                by = (by - g * s.c2) % LN
                turn.append(pltpu.roll(r, by, 1) if by else r)
            z = g * s.lz + a
            comp[8 * z : 8 * z + 8, :] = jnp.where(
                lane < s.c2, turn[0], jnp.where(lane < LN // 2, turn[1], turn[2])
            )
    wide[...] = split_dot(comp[...], spread2[...]).reshape(wide.shape)

    def body(z, carry):
        for j in range(s.j1):
            x = [wide[z, k : k + 1, tiles(j)] for k in range(3)]
            for k in range(2):
                rows = slice(s.pad1 - 4 + 4 * k, s.pad1 + 4 + 4 * k)
                y = w2[z + 1, j, rows, :] + jnp.where(upper, x[k], x[k + 1])
                wa[z + 1, j, rows, :] = jnp.where(level.inv[z, j, rows, :] > 0.0, y, 0.0)
        return carry

    lax.fori_loop(0, s.nz, body, 0)
    level.sweep(wa, wb, rx, s.pad1 - 3, s.pad1 + s.own1 + 3)
    level.sweep(wb, wa, rx, s.pad1 - 2, s.pad1 + s.own1 + 2)


def correct_fine(s, w, v, spread1, wide, dst):
    rows = slice(s.pad1 - 2, s.pad1 + s.own1 + 2)
    lhs = jnp.concatenate([w[1 : s.nz + 1, j, rows, :].reshape(s.nz * s.r1, LN) for j in range(s.j1)], axis=1)
    wide[...] = split_dot(lhs, spread1[...]).reshape(wide.shape)
    zero_ends(s, dst)
    upper = iota((8, LN), 0) < 4

    def body(z, carry):
        for j in range(s.j0):
            for k in range(s.r1 // 2):
                rows = slice(8 * k, 8 * k + 8)
                x = [wide[z, 2 * k + i : 2 * k + i + 1, tiles(j)] for i in range(2)]
                dst[z + 1, j, rows, :] = v[z + 1, j, rows, :] + jnp.where(upper, x[0], x[1])
        return carry

    lax.fori_loop(0, s.nz, body, 0)


def back_kernel(
    s, got, u2, l2, d2, c2, w2, rx, via1, d1, c, u, v2, f, via0, d0, spread2, spread1, down,
    v, r1, cs, comp, wide2, wa, wb, va, wide, rbuf,
):
    fine, middle = Level(s, 0, via0, d0, c, u), Level(s, 1, via1, d1, c, u)
    coarse(s, got, u2, l2, d2, c2, cs)
    middle_last(s, middle, cs, spread2, w2, rx, comp, wide2, wa, wb)
    correct_fine(s, wa, v2, spread1, wide, va)
    zero_ends(s, v)
    fine.sweep(va, v, f, 2, s.re - 2)
    fine.sweep(v, va, f, 3, s.re - 3)
    fine.sweep(va, v, f, 4, s.re - 4)
    fine.sweep(v, va, f, 5, s.re - 5)
    restrict(s, fine, va, f, HY, HY + s.rows, down, rbuf, wide, r1)

    def body(z, carry):
        for j in range(s.j0):
            for r in windows(5, s.re - 5):
                v[z + 1, j, r : r + 8, :] = va[z + 1, j, r : r + 8, :]
        return carry

    lax.fori_loop(0, s.nz, body, 0)


def last_kernel(
    s, got, u2, l2, d2, c2, w2, rx, via1, d1, c, u, v2, f, via0, d0, spread2, spread1, *refs,
):
    outs, (cs, comp, wide2, wa, wb, va, wide, vb, rbuf) = refs[: s.nd], refs[s.nd :]
    fine, middle = Level(s, 0, via0, d0, c, u), Level(s, 1, via1, d1, c, u)
    d, _ = place()
    coarse(s, got, u2, l2, d2, c2, cs)
    middle_last(s, middle, cs, spread2, w2, rx, comp, wide2, wa, wb)
    correct_fine(s, wa, v2, spread1, wide, va)
    zero_ends(s, vb)
    fine.sweep(va, vb, f, HY - 2, HY + s.rows + 2)
    fine.sweep(vb, va, f, HY - 1, HY + s.rows + 1)

    def put(z, j, r, x):
        rbuf[pl.ds(pl.multiple_of((z * (s.j0 - 1) + j) * s.rows + (r - HY), 8), 8), :] = x

    fine.residual(va, f, HY, HY + s.rows, put, s.j0 - 1)
    for step, out in enumerate(outs):
        e = lax.rem(d + step, s.nd)
        for a in range(s.lz):
            z = e * s.lz + a
            for j in range(s.j0 - 1):
                out[0, a, :, tiles(j)] = va[z + 1, j, HY : HY + s.rows, :]
                at = pl.multiple_of((z * (s.j0 - 1) + j) * s.rows, 8)
                out[1, a, :, tiles(j)] = rbuf[pl.ds(at, s.rows), :]


def unpack_kernel(s, *refs):
    parts, outs, sem = refs[: s.nd], refs[s.nd : -1], refs[-1]
    d, _ = place()
    copies = []
    for step, part in enumerate(parts):
        e = lax.rem(d + s.nd - step, s.nd)
        cols = pl.ds(pl.multiple_of(e * s.wc, LN), s.wc)
        for k, out in enumerate(outs):
            copies.append(pltpu.make_async_copy(part.at[k], out.at[:, :, cols], sem.at[len(outs) * step + k]))
    for c in copies:
        c.start()
    for c in copies:
        c.wait()


def call(name, kernel, s, outs, scratch=(), host_in=False, host_out=False):
    shapes = [jax.ShapeDtypeStruct(o, F32) for o in outs]
    spaces = [pl.BlockSpec(memory_space=m) for m in (pltpu.VMEM, pltpu.HBM)]

    def run(*args):
        total = sum(int(np.prod(a.shape)) * 4 for a in args) + sum(int(np.prod(o)) * 4 for o in outs)
        return pl.pallas_call(
            functools.partial(kernel, s),
            name=name,
            out_shape=shapes,
            in_specs=[spaces[host_in]] * len(args),
            out_specs=[spaces[host_out]] * len(outs),
            scratch_shapes=[pltpu.VMEM(x, F32) if isinstance(x, tuple) else x for x in scratch],
            compiler_params=pltpu.CompilerParams(vmem_limit_bytes=32 << 20),
            cost_estimate=pl.CostEstimate(flops=4 * total, bytes_accessed=total, transcendentals=0),
        )(*args)

    return run


def shift(x, axis, by):
    n = lax.axis_size(axis)
    return lax.ppermute(x, axis, [(i, (i + by) % n) for i in range(n)])


def tables(s):
    p = np.arange(s.we)
    at = p // 4 + np.where(p >= s.wc + HX, s.w1 - s.we // 4, 0)
    down = at[:, None] == np.arange(s.w1)[None, :]
    q = np.arange(s.w1)
    k = q // 4 + np.where(q >= s.w1 - HX // 4, LN - s.w1 // 4, 0)
    used = (q < s.c1 + HX // 4) | (q >= s.w1 - HX // 4)
    spread2 = (np.arange(LN)[:, None] == k[None, :]) & used[None, :]
    r = np.arange(LN)
    down2 = (r // 4)[:, None] == (r % s.c2)[None, :]
    return [jnp.asarray(m, BF16) for m in (down, down.T, spread2, down2)]


def local(s, source_heating, material_thermal_values, layer_material, via_conductance, via_blocks):
    down, spread1, spread2, down2 = tables(s)
    dma, smem = pltpu.SemaphoreType.DMA, pltpu.SMEM
    packed = (s.part + 8, LN)
    sends = call(
        "pack", pack_kernel, s, [packed] * s.nd,
        [
            smem(material_thermal_values.shape, F32), smem(layer_material.shape, jnp.int32),
            smem(via_conductance.shape, F32), pltpu.VMEM((4, s.nb), jnp.int32),
            pltpu.VMEM(source_heating.shape, F32), dma((5,)),
        ],
        host_in=True,
    )(material_thermal_values, layer_material, via_conductance, via_blocks[0].T, source_heating)
    parts = [sends[0]] + [shift(sends[k], "die", k) for k in range(1, s.nd)]
    half = (s.nz * s.j0, HY, LN)
    top, bot, prm = call("assemble", assemble_kernel, s, [half, half, (s.nd, 8, LN)])(*parts)
    above, below = shift(bot, "tile", 1), shift(top, "tile", -1)
    f0, f1, small = (s.j0, s.re, LN), (s.j1, s.e1, LN), (s.nz, s.j1, s.r1, LN)
    fine, fine_v = (s.nz, *f0), (s.nz + 2, *f0)
    mid, mid_v = (s.nz, *f1), (s.nz + 2, *f1)
    slab = (s.nd * s.lz, s.nt, LN)
    via0, d0, via1, d1, u2, l2, d2, c, u, c2 = call(
        "coeff", coeff_kernel, s,
        [(s.nd + 1, *f0), fine, (s.nd + 1, *f1), mid, slab, slab, slab, (s.nz, 8, LN), (s.nz, 8, LN), (s.lz, 8, LN)],
    )(prm)
    flat, rbuf = (s.nz, s.r1, s.we), (s.nz * s.j0 * s.re, LN)
    f, v, r1 = call("fine_first", fine_first_kernel, s, [fine, fine_v, small], [fine_v, rbuf, flat])(
        above, top, bot, below, via0, d0, c, u, down
    )
    spaces = [(s.nd * s.lz, s.nt + 2 * HY, LN), (s.nz * 8, LN), (s.nz, 8, s.w1), mid_v, mid_v, fine_v, flat]
    for cycle in range(2):
        rx, w2, send = call(
            "middle_first", middle_first_kernel, s,
            [mid, mid_v, (s.nd * s.nt * s.lz, LN)], [mid_v, (s.nz * 8, LN)],
        )(shift(r1, "tile", 1), r1, shift(r1, "tile", -1), via1, d1, c, u, down2)
        got = lax.all_to_all(send, ("die", "tile"), 0, 0, tiled=True)
        args = (got, u2, l2, d2, c2, w2, rx, via1, d1, c, u, v, f, via0, d0, spread2, spread1)
        if cycle == 0:
            v, r1 = call("back", back_kernel, s, [fine_v, small], spaces + [rbuf])(*args, down)
    piece = (2, s.lz, s.rows, s.wc)
    sends = call(
        "last", last_kernel, s, [piece] * s.nd, spaces + [fine_v, (s.nz * (s.j0 - 1) * s.rows, LN)]
    )(*args)
    parts = [sends[0]] + [shift(sends[k], "die", k) for k in range(1, s.nd)]
    whole = (s.lz, s.rows, s.width)
    return tuple(call("unpack", unpack_kernel, s, [whole] * 2, [dma((2 * s.nd,))], host_out=True)(*parts))


def solution(mesh):
    in_specs = (P("die", "tile", None), P(), P("die"), P("die"), P("die", None, None))
    out_specs = (P("die", "tile", None), P("die", "tile", None))

    def body(f, mat, material, conductance, blocks):
        s = Sizes(mesh.shape, f.shape, blocks.shape[1])
        return local(s, f, mat, material, conductance, blocks)

    return jax.shard_map(body, mesh=mesh, in_specs=in_specs, out_specs=out_specs, check_vma=False)
```

```python
import functools

import jax
import jax.numpy as jnp
import numpy as np
from jax import lax
from jax.experimental import pallas as pl
from jax.experimental.pallas import tpu as pltpu
from jax.sharding import PartitionSpec as P

OMEGA = 0.8
NC = 6
LN = 128
HX = 64
VMEM = 67_043_328
HY = 8
F32 = jnp.float32
BF16 = jnp.bfloat16


def iota(shape, axis):
    return lax.broadcasted_iota(jnp.int32, shape, axis)


def split_dot(x, m):
    hi = x.astype(BF16)
    lo = (x - hi.astype(F32)).astype(BF16)
    return jnp.dot(hi, m, preferred_element_type=F32) + jnp.dot(lo, m, preferred_element_type=F32)


def pair_dot(a, b):
    return lax.dot_general(a, b, (((0,), (0,)), ((), ())), preferred_element_type=F32)


class Sizes:
    def __init__(self, mesh_shape, f_shape, n_blocks):
        self.nd, self.nt = mesh_shape["die"], mesh_shape["tile"]
        self.lz, self.rows, self.width = f_shape
        self.nb = n_blocks
        self.wc = self.width // self.nd
        self.we = self.wc + LN
        self.j0 = self.we // LN
        self.nz = self.nd * self.lz
        self.re = self.rows + 2 * HY
        self.own1 = self.rows // 4
        self.r1 = self.re // 4
        self.c1 = self.wc // 4
        self.e1 = 2 * self.r1
        self.pad1 = (self.e1 - self.own1) // 2
        self.j1 = 2
        self.w1 = self.j1 * LN
        self.c2 = self.wc // 16
        self.part = self.lz * self.j0 * self.rows
        assert self.rows == 16 and self.lz == 4 and self.c1 == LN
        assert self.nd * self.c2 == LN and self.nb <= LN and self.nt <= LN and self.nt % 8 == 0


def place():
    return lax.axis_index("die"), lax.axis_index("tile")


def tiles(j):
    return slice(j * LN, (j + 1) * LN)


def windows(lo, hi):
    return [min(r, hi - 8) for r in range(lo, hi, 8)]


def pack_kernel(s, mat_h, material_h, conductance_h, blocks_h, f_h, *refs):
    outs, (mat, material, conductance, blocks, f, sem) = refs[: s.nd], refs[s.nd :]
    pairs = [(f_h, f), (mat_h, mat), (material_h, material), (conductance_h, conductance), (blocks_h, blocks)]
    copies = [pltpu.make_async_copy(a, b, sem.at[k]) for k, (a, b) in enumerate(pairs)]
    for c in copies:
        c.start()
    for c in copies[1:]:
        c.wait()
    d, _ = place()
    lane, sub = iota((8, LN), 1), iota((8, LN), 0)
    info = jnp.where((sub == 5) & (lane == 0), conductance[0, 0], 0.0)
    for z in range(s.lz):
        info = jnp.where((sub == 4) & (lane == z), mat[material[z]], info)
    for out in outs:
        out[s.part :, :] = info
        out[s.part : s.part + 4, : s.nb] = blocks[...].astype(F32)
    copies[0].wait()
    low = iota((s.rows, LN), 1) < HX
    for step, out in enumerate(outs):
        e = lax.rem(d + step, s.nd)
        right = lax.rem(e + 1, s.nd) * s.wc
        left = lax.rem(e + s.nd - 1, s.nd) * s.wc + (s.wc - LN)

        def column(z, at):
            return f[z, :, pl.ds(pl.multiple_of(at, LN), LN)]

        for z in range(s.lz):
            for j in range(s.j0):
                at = (z * s.j0 + j) * s.rows
                if j < s.j0 - 1:
                    x = column(z, e * s.wc + j * LN)
                else:
                    x = jnp.where(low, column(z, right), column(z, left))
                out[at : at + s.rows, :] = x


def assemble_kernel(s, *refs):
    parts, (top, bot, prm) = refs[: s.nd], refs[s.nd :]
    d, _ = place()
    n = s.lz * s.j0
    for step, part in enumerate(parts):
        e = lax.rem(d + s.nd - step, s.nd)
        for q in range(n):
            top[n * e + q] = part[q * s.rows : q * s.rows + HY, :]
            bot[n * e + q] = part[q * s.rows + HY : (q + 1) * s.rows, :]
        prm[e] = part[s.part :, :]


def overlap(lo, size, first, past):
    return jnp.maximum(jnp.minimum(lo + size, past) - jnp.maximum(lo, first), 0.0)


def die_values(s, prm):
    lane8, sub8 = iota((8, LN), 1), iota((8, LN), 0)

    def pick(tile, row, col):
        return jnp.sum(jnp.where((lane8 == col) & (sub8 == row), tile, 0.0), keepdims=True)

    info = [prm[g] for g in range(s.nd)]
    cond = [pick(info[z // s.lz], 4, z % s.lz) for z in range(s.nz)]
    via = [pick(info[g], 5, 0) for g in range(s.nd)]
    vert = [2.0 * p * q / (p + q) for p, q in zip(cond, cond[1:] + cond[-1:])]
    blocks = []
    for g in range(s.nd):
        b = jnp.transpose(info[g])
        lane = iota((LN, 8), 1)
        col = [jnp.sum(jnp.where(lane == k, b, 0.0), axis=1, keepdims=True) for k in range(4)]
        col = [x[: s.nb] for x in col]
        blocks.append((col[0], col[0] + col[2], col[1], col[1] + col[3]))
    return cond, vert, via, blocks


def level_coeffs(s, level, values, via_up, via_down, scale):
    cond, vert, via, blocks = values
    d, t = place()
    size = 4**level
    n, own = (s.we, s.wc) if level == 0 else (s.w1, s.c1)
    height, nj = (s.re, s.j0) if level == 0 else (s.e1, s.j1)
    pad = HY if level == 0 else s.pad1
    halo = HX // size

    def columns(shape, axis):
        p = iota(shape, axis)
        return p, d * own + jnp.where(p >= n - halo, p - n, p)

    first = t * (s.rows // size) - pad
    row = ((first + iota((1, LN), 1)) * size).astype(F32)
    col = (columns((1, n), 1)[1] * size).astype(F32)
    rr = first + iota((height, n), 0)
    pp, cc = columns((height, n), 1)
    inside = (rr >= 0) & (rr < s.rows * s.nt // size) & (cc >= 0) & (cc < s.width // size)
    inside = jnp.where(inside & ((pp < own + halo) | (pp >= n - halo)), OMEGA, 0.0)
    via_down[0] = jnp.zeros(via_down.shape[1:], F32)
    for g in range(s.nd):
        r0, r1, c0, c1 = blocks[g]
        m = pair_dot(
            overlap(row, float(size), r0, r1).astype(BF16), overlap(col, float(size), c0, c1).astype(BF16)
        )[:height]
        top = (g + 1) * s.lz - 1
        m = m * (via[g] * (0.25**level))
        for j in range(nj):
            via_up[g, j] = m[:, tiles(j)] / cond[top]
            if g + 1 < s.nd:
                via_down[g + 1, j] = m[:, tiles(j)] / cond[top + 1]
    for z in range(s.nz):
        g, a = z // s.lz, z % s.lz
        const = 4.0
        if a < s.lz - 1:
            const = const + vert[z] * (4.0**level) / cond[z]
        if a > 0:
            const = const + vert[z - 1] * (4.0**level) / cond[z]
        for j in range(nj):
            diag = const
            if a == s.lz - 1:
                diag = diag + via_up[g, j]
            if a == 0:
                diag = diag + via_down[g, j]
            scale[z, j] = inside[:, tiles(j)] / diag


def coeff_fine_kernel(s, prm, up0, down0, e0, c, ic, cu, cd):
    values = die_values(s, prm)
    cond, vert = values[:2]
    for z in range(s.nz):
        c[z] = jnp.zeros((8, LN), F32) + cond[z]
        ic[z] = jnp.zeros((8, LN), F32) + 1.0 / cond[z]
        cu[z] = jnp.zeros((8, LN), F32) + vert[z] / cond[z]
        cd[z] = jnp.zeros((8, LN), F32) + vert[max(z - 1, 0)] / cond[z]
    level_coeffs(s, 0, values, up0, down0, e0)


def coeff_coarse_kernel(s, prm, up1, down1, e1, u2, l2, e2):
    values = die_values(s, prm)
    cond, vert, via, blocks = values
    level_coeffs(s, 1, values, up1, down1, e1)
    group = iota((1, LN), 1) // s.c2
    xin = iota((1, LN), 1) % s.c2

    def by_group(values):
        out = jnp.zeros((1, LN), F32)
        for g in range(s.nd):
            out = jnp.where(group == g, values[g], out)
        return out

    cl = [by_group([cond[s.lz * g + a] for g in range(s.nd)]) * 16.0 for a in range(s.lz)]
    vl = [by_group([vert[s.lz * g + a] for g in range(s.nd)]) * 256.0 for a in range(s.lz)]
    vial = by_group(via)
    row2 = (iota((1, LN), 1) * 16).astype(F32)
    ra = jnp.concatenate([overlap(row2, 16.0, b[0], b[1]) for b in blocks], axis=0).astype(BF16)
    zero2 = jnp.zeros((s.nt, LN), F32)
    for e in range(s.nd):
        col2 = ((e * s.c2 + xin) * 16).astype(F32)
        cb = jnp.concatenate(
            [jnp.where(group == g, overlap(col2, 16.0, b[2], b[3]), 0.0) for g, b in enumerate(blocks)],
            axis=0,
        ).astype(BF16)
        v2 = pair_dot(ra, cb)[: s.nt] * vial
        ups = [zero2 + vl[a] for a in range(s.lz - 1)] + [v2]
        first = jnp.where(iota((s.nt, LN), 1) >= s.c2, pltpu.roll(v2, s.c2, 1), 0.0)
        lows = [first] + ups[:-1]
        for a in range(s.lz):
            q = e * s.lz + a
            u2[q] = ups[a] / cl[a]
            l2[q] = lows[a] / cl[a]
            e2[q] = OMEGA * cl[a] / (4.0 * cl[a] + ups[a] + lows[a])


class Level:
    def __init__(self, s, level, up, down, scale, cu, cd):
        self.s, self.up, self.down, self.scale, self.cu, self.cd = s, up, down, scale, cu, cd
        self.nj = (s.j0, s.j1)[level]
        self.us = 4.0**level

    def layers(self, body):
        s = self.s

        def group(g, carry):
            for a in range(s.lz):
                z = g * s.lz + a
                if a < s.lz - 1:
                    const_up = self.cu[z] * self.us
                    up = lambda j, rows, k=const_up: k
                else:
                    up = lambda j, rows: self.up[g, j, rows, :]
                if a > 0:
                    const_down = self.cd[z] * self.us
                    down = lambda j, rows, k=const_down: k
                else:
                    down = lambda j, rows: self.down[g, j, rows, :]
                body(z, up, down)
            return carry

        lax.fori_loop(0, s.nd, group, 0)

    def sums(self, v, to, z, rows):
        n = len(v)
        lane = iota((8, LN), 1)
        ahead = [pltpu.roll(x, LN - 1, 1) for x in v]
        behind = [pltpu.roll(x, 1, 1) for x in v]
        for j in range(n):
            x = jnp.where(lane == LN - 1, ahead[(j + 1) % n], ahead[j])
            to[z, j, rows, :] = x + jnp.where(lane == 0, behind[j - 1], behind[j])

    def right(self, src, side, f, z, j, r, k_up, k_down):
        rows = pl.ds(r, 8)
        y = src[z + 1, j, pl.ds(r - 1, 8), :] + src[z + 1, j, pl.ds(r + 1, 8), :]
        x = f[z, j, rows, :] + side[z, j, rows, :]
        return (x + y) + (k_up * src[z + 2, j, rows, :] + k_down * src[z, j, rows, :])

    def sweep(self, src, side, dst, to, f, lo, hi):
        def body(z, up, down):
            for r in windows(lo, hi):
                rows = pl.ds(r, 8)
                new = []
                for j in range(self.nj):
                    g = self.right(src, side, f, z, j, r, up(j, rows), down(j, rows))
                    new.append((1.0 - OMEGA) * src[z + 1, j, rows, :] + self.scale[z, j, rows, :] * g)
                    dst[z + 1, j, rows, :] = new[-1]
                if to is not None:
                    self.sums(new, to, z, rows)

        self.layers(body)

    def residual(self, src, side, f, lo, hi, put, count=None):
        def body(z, up, down):
            for r in windows(lo, hi):
                rows = pl.ds(r, 8)
                for j in range(count or self.nj):
                    k_up, k_down = up(j, rows), down(j, rows)
                    g = self.right(src, side, f, z, j, r, k_up, k_down)
                    put(z, j, r, g - (4.0 + k_up + k_down) * src[z + 1, j, rows, :])

        self.layers(body)


def zero_ends(s, *bufs):
    for b in bufs:
        b[0] = jnp.zeros(b.shape[1:], F32)
        b[s.nz + 1] = jnp.zeros(b.shape[1:], F32)


def restrict(s, level, src, side, f, lo, hi, down, rbuf, sums, r1):
    for k in range(s.nz * s.j0):
        rbuf[k * s.re : k * s.re + 8, :] = jnp.zeros((8, LN), F32)
        rbuf[(k + 1) * s.re - 8 : (k + 1) * s.re, :] = jnp.zeros((8, LN), F32)

    def put(z, j, r, x):
        rbuf[pl.ds((z * s.j0 + j) * s.re + r, 8), :] = x

    level.residual(src, side, f, lo, hi, put)

    def body(z, carry):
        for j in range(s.j0):
            part = [rbuf[pl.ds((z * s.j0 + j) * s.re + k, s.r1, stride=4), :] for k in range(4)]
            sums[z, :, tiles(j)] = (part[0] + part[1]) + (part[2] + part[3])
        return carry

    lax.fori_loop(0, s.nz, body, 0)
    out = split_dot(sums[...].reshape(s.nz * s.r1, s.we), down[...])
    for z in range(s.nz):
        for j in range(s.j1):
            r1[z, j] = out[z * s.r1 : (z + 1) * s.r1, tiles(j)]


def fine_own_kernel(s, top, bot, up0, down0, e0, ic, cu, cd, down, r1, fore, aft, f, va, xa, vb, xb, rbuf, sums):
    level = Level(s, 0, up0, down0, e0, cu, cd)
    zero_ends(s, va, vb)
    zero = jnp.zeros((8, LN), F32)

    def body(z, carry):
        for k in range(s.re // 8):
            rows = slice(8 * k, 8 * k + 8)
            v = []
            for j in range(s.j0):
                if HY <= 8 * k < HY + s.rows:
                    x = (top, bot)[k - HY // 8][z * s.j0 + j] * ic[z]
                    v.append(e0[z, j, rows, :] * x)
                    f[z, j, rows, :] = x
                    va[z + 1, j, rows, :] = v[-1]
                else:
                    for b in (f, xa, xb):
                        b[z, j, rows, :] = zero
                    va[z + 1, j, rows, :] = zero
                    vb[z + 1, j, rows, :] = zero
            if v:
                level.sums(v, xa, z, rows)
        return carry

    lax.fori_loop(0, s.nz, body, 0)
    level.sweep(va, xa, vb, xb, f, HY - 1, HY + s.rows + 1)
    restrict(s, level, vb, xb, f, HY - 2, HY + s.rows + 2, down, rbuf, sums, r1)
    low = iota((s.r1, LN), 0) < s.r1 // 2

    def halves(z, carry):
        a, b = r1[z, 0], r1[z, 1]
        fore[z] = jnp.where(low, pltpu.roll(a, s.r1 // 2, 0), b)
        aft[z] = jnp.where(low, a, pltpu.roll(b, s.r1 // 2, 0))
        return carry

    lax.fori_loop(0, s.nz, halves, 0)


def middle_first_kernel(s, r1p, r1, r1n, up1, down1, e1, cu, cd, down2, *refs):
    far, (rx, w2, send, wa, xa, xb, buf) = refs[:-7], refs[-7:]
    level = Level(s, 1, up1, down1, e1, cu, cd)
    half, own, pad = s.r1, s.own1, s.pad1
    sub = iota((half, LN), 0)
    _, t = place()
    from_p, from_n = (t >= 1).astype(F32), (t < s.nt - 1).astype(F32)
    from_pp, from_nn = (t >= 2).astype(F32), (t < s.nt - 2).astype(F32)
    zero_ends(s, wa, w2)

    def body(z, carry):
        new = []
        for j in range(s.j1):
            mid = pltpu.roll(r1[z, j], half // 2, 0)
            up = from_p * r1p[z, j] + jnp.where(sub >= half // 2, mid, 0.0)
            down = from_n * r1n[z, j] + jnp.where(sub < half // 2, mid, 0.0)
            if far:
                fore, aft = far[0][z], far[1][z]
                fore = pltpu.roll(fore, half // 2, 0) if j == 1 else fore
                aft = pltpu.roll(aft, half // 2, 0) if j == 0 else aft
                up += from_pp * jnp.where(sub < half // 2, fore, 0.0)
                down += from_nn * jnp.where(sub >= half // 2, aft, 0.0)
            rx[z, j, :half, :] = up
            rx[z, j, half:, :] = down
            new.append((e1[z, j, :half, :] * up, e1[z, j, half:, :] * down))
            wa[z + 1, j, :half, :] = new[-1][0]
            wa[z + 1, j, half:, :] = new[-1][1]
        level.sums([x[0] for x in new], xa, z, slice(0, half))
        level.sums([x[1] for x in new], xa, z, slice(half, 2 * half))
        return carry

    lax.fori_loop(0, s.nz, body, 0)
    level.sweep(wa, xa, w2, xb, rx, pad - 4, pad + own + 4)

    def put(z, j, r, x):
        buf[pl.ds(pl.multiple_of(z * 8, 8), 8), :] = x

    level.residual(w2, xb, rx, pad - 2, pad + own + 2, put, 1)
    sub8, group = iota((8, LN), 0), iota((8, LN), 1) // s.c2
    tile = jnp.zeros((8, LN), F32)
    for h in range(s.nz // 8):
        part = [buf[pl.ds(64 * h + 2 + k, 8, stride=8), :] for k in range(own)]
        x = split_dot((part[0] + part[1]) + (part[2] + part[3]), down2[...])
        y = pltpu.roll(x, 4, 0)
        for g in (2 * h, 2 * h + 1):
            tile = jnp.where(group == g, jnp.where((sub8 < 4) == (g % 2 == 0), x, y), tile)
    for k in range(s.nd * s.nt * s.lz // 8):
        send[8 * k : 8 * k + 8, :] = tile


def coarse(s, got, u2, l2, e2, cs):
    lane = iota((s.nt, LN), 1)
    x, t = lane % s.c2, iota((s.nt, LN), 0)
    first_x, last_x = x == 0, x == s.c2 - 1
    slabs = s.nd * s.lz
    rhs, v = [], []
    for q in range(slabs):
        e, a = q // s.lz, q % s.lz
        r = got[pl.ds(e * s.nt * s.lz + a, s.nt, stride=s.lz), :]
        rhs.append(r)
        v.append(e2[q] * r)
    zero = jnp.zeros((s.nt, LN), F32)

    def body(_, v):
        new = []
        for q in range(slabs):
            e, a = q // s.lz, q % s.lz
            w = v[q]
            right = pltpu.roll(v[q + s.lz], s.c2 - 1, 1) if e < s.nd - 1 else zero
            left = pltpu.roll(v[q - s.lz], LN - (s.c2 - 1), 1) if e > 0 else zero
            side = jnp.where(last_x, right, pltpu.roll(w, LN - 1, 1))
            side += jnp.where(first_x, left, pltpu.roll(w, 1, 1))
            side += jnp.where(t == s.nt - 1, 0.0, pltpu.roll(w, s.nt - 1, 0))
            side += jnp.where(t == 0, 0.0, pltpu.roll(w, 1, 0))
            if a < s.lz - 1:
                up = v[q + 1]
            else:
                up = jnp.where(lane >= LN - s.c2, 0.0, pltpu.roll(v[q - a], LN - s.c2, 1))
            if a > 0:
                down = v[q - 1]
            else:
                down = jnp.where(lane < s.c2, 0.0, pltpu.roll(v[q + s.lz - 1], s.c2, 1))
            g = (rhs[q] + side) + (u2[q] * up + l2[q] * down)
            new.append((1.0 - OMEGA) * w + e2[q] * g)
        return tuple(new)

    v = lax.fori_loop(0, NC - 1, body, tuple(v))
    for q in range(slabs):
        cs[q, :HY, :] = jnp.zeros((HY, LN), F32)
        cs[q, HY + s.nt :, :] = jnp.zeros((HY, LN), F32)
        cs[q, HY : HY + s.nt, :] = v[q]


def middle_last(s, level, cs, spread2, start, rx, comp, wide, wa, xa, wb, xb):
    d, t = place()
    lane, upper = iota((8, LN), 1), iota((8, LN), 0) < 4
    after = lax.rem(d + 1, s.nd) * s.lz
    before = lax.rem(d + s.nd - 1, s.nd) * s.lz
    zero_ends(s, wa, wb)
    for a in range(s.lz):
        rows = [cs[base + a, pl.ds(HY - 1 + t, 8), :] for base in (d * s.lz, after, before)]
        for g in range(s.nd):
            turn = []
            for r, by in zip(rows, (0, s.c2, LN - s.c2)):
                by = (by - g * s.c2) % LN
                turn.append(pltpu.roll(r, by, 1) if by else r)
            z = g * s.lz + a
            comp[8 * z : 8 * z + 8, :] = jnp.where(
                lane < s.c2, turn[0], jnp.where(lane < LN // 2, turn[1], turn[2])
            )
    wide[...] = split_dot(comp[...], spread2[...]).reshape(wide.shape)

    def body(z, carry):
        x = [[wide[z, k : k + 1, tiles(j)] for k in range(3)] for j in range(s.j1)]
        for k in range(2):
            rows = slice(s.pad1 - 4 + 4 * k, s.pad1 + 4 + 4 * k)
            new = []
            for j in range(s.j1):
                y = start(z, j, k, rows) + jnp.where(upper, x[j][k], x[j][k + 1])
                new.append(jnp.where(level.scale[z, j, rows, :] > 0.0, y, 0.0))
                wa[z + 1, j, rows, :] = new[-1]
            level.sums(new, xa, z, rows)
        return carry

    lax.fori_loop(0, s.nz, body, 0)
    level.sweep(wa, xa, wb, xb, rx, s.pad1 - 3, s.pad1 + s.own1 + 3)
    level.sweep(wb, xb, wa, None, rx, s.pad1 - 2, s.pad1 + s.own1 + 2)


def correct_fine(s, level, w, v, spread1, wide, dst, to):
    rows = slice(s.pad1 - 2, s.pad1 + s.own1 + 2)
    lhs = jnp.concatenate([w[1 : s.nz + 1, j, rows, :].reshape(s.nz * s.r1, LN) for j in range(s.j1)], axis=1)
    wide[...] = split_dot(lhs, spread1[...]).reshape(wide.shape)
    upper = iota((8, s.we), 0) < 4

    def body(z, carry):
        for k in range(s.r1 // 2):
            rows = slice(8 * k, 8 * k + 8)
            new = []
            for j in range(s.j0):
                x = [wide[z, 2 * k + i : 2 * k + i + 1, tiles(j)] for i in range(2)]
                new.append(v[z + 1, j, rows, :] + jnp.where(upper[:, tiles(j)], x[0], x[1]))
                dst[z + 1, j, rows, :] = new[-1]
            level.sums(new, to, z, rows)
        return carry

    lax.fori_loop(0, s.nz, body, 0)


def back_kernel(
    s, got, above, top, bot, below, w2, rx,
    u2, l2, e2, up1, down1, e1, up0, down0, e0, ic, cu, cd, spread2, spread1, down,
    f, v, r1, cs, comp, wide2, wa, xwa, wb, xwb, va, xa, vb, xb, wide, rbuf,
):
    fine = Level(s, 0, up0, down0, e0, cu, cd)
    middle = Level(s, 1, up1, down1, e1, cu, cd)
    zero_ends(s, va, vb, v)

    def body(z, carry):
        for k, ref in enumerate((above, top, bot, below)):
            rows = slice(k * HY, (k + 1) * HY)
            new = []
            for j in range(s.j0):
                x = ref[z * s.j0 + j] * ic[z]
                f[z, j, rows, :] = x
                new.append(e0[z, j, rows, :] * x)
                va[z + 1, j, rows, :] = new[-1]
            fine.sums(new, xa, z, rows)
        return carry

    lax.fori_loop(0, s.nz, body, 0)
    fine.sweep(va, xa, vb, None, f, 1, s.re - 1)
    coarse(s, got, u2, l2, e2, cs)
    start = lambda z, j, k, rows: w2[z + 1, j, rows, :]
    middle_last(s, middle, cs, spread2, start, rx, comp, wide2, wa, xwa, wb, xwb)
    correct_fine(s, fine, wa, vb, spread1, wide, va, xa)
    fine.sweep(va, xa, vb, xb, f, 2, s.re - 2)
    fine.sweep(vb, xb, va, xa, f, 3, s.re - 3)
    fine.sweep(va, xa, vb, xb, f, 4, s.re - 4)
    fine.sweep(vb, xb, v, xa, f, 5, s.re - 5)
    restrict(s, fine, v, xa, f, HY, HY + s.rows, down, rbuf, wide, r1)


def last_kernel(
    s, got, w2, rx, v2, f, u2, l2, e2, up1, down1, e1, up0, down0, e0, c, cu, cd, spread2, spread1, *refs,
):
    outs, (cs, comp, wide2, wa, xwa, wb, xwb, va, xa, vb, xb, wide, rbuf) = refs[: s.nd], refs[s.nd :]
    fine = Level(s, 0, up0, down0, e0, cu, cd)
    middle = Level(s, 1, up1, down1, e1, cu, cd)
    d, _ = place()
    zero_ends(s, va, vb)
    coarse(s, got, u2, l2, e2, cs)
    start = lambda z, j, k, rows: w2[z + 1, j, rows, :]
    middle_last(s, middle, cs, spread2, start, rx, comp, wide2, wa, xwa, wb, xwb)
    correct_fine(s, fine, wa, v2, spread1, wide, va, xa)
    fine.sweep(va, xa, vb, xb, f, HY - 2, HY + s.rows + 2)
    fine.sweep(vb, xb, va, xa, f, HY - 1, HY + s.rows + 1)

    def put(z, j, r, x):
        rbuf[pl.ds(pl.multiple_of((z * (s.j0 - 1) + j) * s.rows + (r - HY), 8), 8), :] = x * c[z]

    fine.residual(va, xa, f, HY, HY + s.rows, put, s.j0 - 1)
    for step, out in enumerate(outs):
        e = lax.rem(d + step, s.nd)
        for a in range(s.lz):
            z = e * s.lz + a
            for j in range(s.j0 - 1):
                out[0, a, :, tiles(j)] = va[z + 1, j, HY : HY + s.rows, :]
                at = pl.multiple_of((z * (s.j0 - 1) + j) * s.rows, 8)
                out[1, a, :, tiles(j)] = rbuf[pl.ds(at, s.rows), :]


def unpack_kernel(s, *refs):
    parts, outs, sem = refs[: s.nd], refs[s.nd : -1], refs[-1]
    d, _ = place()
    copies = []
    for step, part in enumerate(parts):
        e = lax.rem(d + s.nd - step, s.nd)
        cols = pl.ds(pl.multiple_of(e * s.wc, LN), s.wc)
        for k, out in enumerate(outs):
            copies.append(pltpu.make_async_copy(part.at[k], out.at[:, :, cols], sem.at[len(outs) * step + k]))
    for c in copies:
        c.start()
    for c in copies:
        c.wait()


def call(name, kernel, s, outs, scratch=(), to_hbm=False, from_hbm=False, in_vmem=False, limit=32 << 20):
    shapes = [pltpu.VMEM(o, F32) if in_vmem else jax.ShapeDtypeStruct(o, F32) for o in outs]
    spaces = [pl.BlockSpec(memory_space=m) for m in (pltpu.VMEM, pltpu.HBM)]

    def run(*args):
        total = sum(int(np.prod(a.shape)) * 4 for a in args) + sum(int(np.prod(o)) * 4 for o in outs)
        return pl.pallas_call(
            functools.partial(kernel, s),
            name=name,
            out_shape=shapes,
            in_specs=[spaces[from_hbm]] * len(args),
            out_specs=[spaces[to_hbm]] * len(outs),
            scratch_shapes=[pltpu.VMEM(x, F32) if isinstance(x, tuple) else x for x in scratch],
            compiler_params=pltpu.CompilerParams(vmem_limit_bytes=limit),
            cost_estimate=pl.CostEstimate(flops=4 * total, bytes_accessed=total, transcendentals=0),
        )(*args)

    return run


def shift(x, axis, by):
    n = lax.axis_size(axis)
    return lax.ppermute(x, axis, [(i, (i + by) % n) for i in range(n)])


def tables(s):
    p = np.arange(s.we)
    at = p // 4 + np.where(p >= s.wc + HX, s.w1 - s.we // 4, 0)
    down = at[:, None] == np.arange(s.w1)[None, :]
    q = np.arange(s.w1)
    k = q // 4 + np.where(q >= s.w1 - HX // 4, LN - s.w1 // 4, 0)
    used = (q < s.c1 + HX // 4) | (q >= s.w1 - HX // 4)
    spread2 = (np.arange(LN)[:, None] == k[None, :]) & used[None, :]
    r = np.arange(LN)
    down2 = (r // 4)[:, None] == (r % s.c2)[None, :]
    return [jnp.asarray(m, BF16) for m in (down * 0.25, down.T, spread2, down2 * 0.25)]


def local(s, source_heating, material_thermal_values, layer_material, via_conductance, via_blocks):
    down, spread1, spread2, down2 = tables(s)
    smem, packed = pltpu.SMEM, (s.part + 8, LN)
    sends = call(
        "pack", pack_kernel, s, [packed] * s.nd,
        [
            smem(material_thermal_values.shape, F32), smem(layer_material.shape, jnp.int32),
            smem((1, 1), F32), pltpu.VMEM((4, s.nb), jnp.int32),
            pltpu.VMEM(source_heating.shape, F32), pltpu.SemaphoreType.DMA((5,)),
        ],
        from_hbm=True, in_vmem=True, limit=VMEM - 4 * s.nd * packed[0] * packed[1],
    )(material_thermal_values, layer_material, via_conductance[None], via_blocks[0].T, source_heating)
    parts = [sends[0]] + [shift(sends[k], "die", k) for k in range(1, s.nd)]
    half = (s.nz * s.j0, HY, LN)
    top, bot, prm = call("assemble", assemble_kernel, s, [half, half, (s.nd, 8, LN)])(*parts)
    f0, f1, small = (s.j0, s.re, LN), (s.j1, s.e1, LN), (s.nz, s.j1, s.r1, LN)
    fine, fine_v = (s.nz, *f0), (s.nz + 2, *f0)
    mid, mid_v = (s.nz, *f1), (s.nz + 2, *f1)
    slab, table = (s.nd * s.lz, s.nt, LN), (s.nz, 8, LN)
    up0, down0, e0, c, ic, cu, cd = call(
        "coeff_fine", coeff_fine_kernel, s, [(s.nd, *f0), (s.nd, *f0), fine, table, table, table, table]
    )(prm)
    flat, rbuf = (s.nz, s.r1, s.we), (s.nz * s.j0 * s.re, LN)
    r1, fore, aft = call("fine_own", fine_own_kernel, s, [small, table, table], [fine, fine_v, fine, fine_v, fine, rbuf, flat])(
        top, bot, up0, down0, e0, ic, cu, cd, down
    )
    up1, down1, e1, u2, l2, e2 = call(
        "coeff_coarse", coeff_coarse_kernel, s, [(s.nd, *f1), (s.nd, *f1), mid, slab, slab, slab]
    )(prm)

    def middle_first(r1, *far):
        return call(
            "middle_first", middle_first_kernel, s,
            [mid, mid_v, (s.nd * s.nt * s.lz, LN)], [mid_v, mid, mid, (s.nz * 8, LN)],
        )(shift(r1, "tile", 1), r1, shift(r1, "tile", -1), up1, down1, e1, cu, cd, down2, *far)

    def everywhere(send):
        return lax.all_to_all(send, ("die", "tile"), 0, 0, tiled=True)

    spaces = [(s.nd * s.lz, s.nt + 2 * HY, LN), (s.nz * 8, LN), (s.nz, 8, s.w1), mid_v, mid, mid_v, mid]
    spaces += [fine_v, fine, fine_v, fine, flat]
    above, below = shift(bot, "tile", 1), shift(top, "tile", -1)
    rx, w2, send = middle_first(r1, shift(fore, "tile", 2), shift(aft, "tile", -2))
    above, below, send = lax.optimization_barrier((above, below, send))
    levels = (u2, l2, e2, up1, down1, e1, up0, down0, e0)
    f, v, r1 = call("back", back_kernel, s, [fine, fine_v, small], spaces + [rbuf])(
        everywhere(send), above, top, bot, below, w2, rx,
        *levels, ic, cu, cd, spread2, spread1, down,
    )
    rx, w2, send = middle_first(r1)
    piece = (2, s.lz, s.rows, s.wc)
    sends = call(
        "last", last_kernel, s, [piece] * s.nd, spaces + [(s.nz * (s.j0 - 1) * s.rows, LN)]
    )(everywhere(send), w2, rx, v, f, *levels, c, cu, cd, spread2, spread1)
    parts = [sends[0]] + [shift(sends[k], "die", k) for k in range(1, s.nd)]
    whole = (s.lz, s.rows, s.width)
    return tuple(call("unpack", unpack_kernel, s, [whole] * 2, [pltpu.SemaphoreType.DMA((2 * s.nd,))], True)(*parts))


def solution(mesh):
    in_specs = (P("die", "tile", None), P(), P("die"), P("die"), P("die", None, None))
    out_specs = (P("die", "tile", None), P("die", "tile", None))

    def body(f, mat, material, conductance, blocks):
        s = Sizes(mesh.shape, f.shape, blocks.shape[1])
        return local(s, f, mat, material, conductance, blocks)

    return jax.shard_map(body, mesh=mesh, in_specs=in_specs, out_specs=out_specs, check_vma=False)
```

```python
import functools

import jax
import jax.numpy as jnp
import numpy as np
from jax import lax
from jax.experimental import pallas as pl
from jax.experimental.pallas import tpu as pltpu
from jax.sharding import PartitionSpec as P


OMEGA = 0.8
NC = 6
LN = 128
HX = 64
VMEM = 67_043_328
HY = 8
F32 = jnp.float32
BF16 = jnp.bfloat16


def iota(shape, axis):
    return lax.broadcasted_iota(jnp.int32, shape, axis)


def split_dot(x, m):
    hi = x.astype(BF16)
    lo = (x - hi.astype(F32)).astype(BF16)
    return jnp.dot(hi, m, preferred_element_type=F32) + jnp.dot(lo, m, preferred_element_type=F32)


def pair_dot(a, b):
    return lax.dot_general(a, b, (((0,), (0,)), ((), ())), preferred_element_type=F32)


class Sizes:
    def __init__(self, mesh_shape, f_shape, n_blocks):
        self.nd, self.nt = mesh_shape["die"], mesh_shape["tile"]
        self.lz, self.rows, self.width = f_shape
        self.nb = n_blocks
        self.wc = self.width // self.nd
        self.we = self.wc + LN
        self.j0 = self.we // LN
        self.nz = self.nd * self.lz
        self.re = self.rows + 2 * HY
        self.own1 = self.rows // 4
        self.r1 = self.re // 4
        self.c1 = self.wc // 4
        self.e1 = 2 * self.r1
        self.pad1 = (self.e1 - self.own1) // 2
        self.j1 = 2
        self.w1 = self.j1 * LN
        self.c2 = self.wc // 16
        self.part = self.lz * self.j0 * self.rows
        assert self.rows == 16 and self.lz == 4 and self.c1 == LN
        assert self.nd * self.c2 == LN and self.nb <= LN and self.nt <= LN and self.nt % 8 == 0


def place():
    return lax.axis_index("die"), lax.axis_index("tile")


def tiles(j):
    return slice(j * LN, (j + 1) * LN)


def windows(lo, hi):
    return [min(r, hi - 8) for r in range(lo, hi, 8)]


def pack_kernel(s, mat_h, material_h, conductance_h, blocks_h, f_h, *refs):
    outs, (mat, material, conductance, blocks, f, sem) = refs[: s.nd], refs[s.nd :]
    pairs = [(f_h, f), (mat_h, mat), (material_h, material), (conductance_h, conductance), (blocks_h, blocks)]
    copies = [pltpu.make_async_copy(a, b, sem.at[k]) for k, (a, b) in enumerate(pairs)]
    for c in copies:
        c.start()
    for c in copies[1:]:
        c.wait()
    d, _ = place()
    lane, sub = iota((8, LN), 1), iota((8, LN), 0)
    info = jnp.where((sub == 5) & (lane == 0), conductance[0, 0], 0.0)
    for z in range(s.lz):
        info = jnp.where((sub == 4) & (lane == z), mat[material[z]], info)
    for out in outs:
        out[s.part :, :] = info
        out[s.part : s.part + 4, : s.nb] = blocks[...].astype(F32)
    copies[0].wait()
    low = iota((s.rows, LN), 1) < HX
    for step, out in enumerate(outs):
        e = lax.rem(d + step, s.nd)
        right = lax.rem(e + 1, s.nd) * s.wc
        left = lax.rem(e + s.nd - 1, s.nd) * s.wc + (s.wc - LN)

        def column(z, at):
            return f[z, :, pl.ds(pl.multiple_of(at, LN), LN)]

        for z in range(s.lz):
            for j in range(s.j0):
                at = (z * s.j0 + j) * s.rows
                if j < s.j0 - 1:
                    x = column(z, e * s.wc + j * LN)
                else:
                    x = jnp.where(low, column(z, right), column(z, left))
                out[at : at + s.rows, :] = x


def assemble_kernel(s, *refs):
    parts, (top, bot, prm) = refs[: s.nd], refs[s.nd :]
    d, _ = place()
    n = s.lz * s.j0
    for step, part in enumerate(parts):
        e = lax.rem(d + s.nd - step, s.nd)
        for q in range(n):
            top[n * e + q] = part[q * s.rows : q * s.rows + HY, :]
            bot[n * e + q] = part[q * s.rows + HY : (q + 1) * s.rows, :]
        prm[e] = part[s.part :, :]


def overlap(lo, size, first, past):
    return jnp.maximum(jnp.minimum(lo + size, past) - jnp.maximum(lo, first), 0.0)


def die_values(s, prm):
    lane8, sub8 = iota((8, LN), 1), iota((8, LN), 0)

    def pick(tile, row, col):
        return jnp.sum(jnp.where((lane8 == col) & (sub8 == row), tile, 0.0), keepdims=True)

    info = [prm[g] for g in range(s.nd)]
    cond = [pick(info[z // s.lz], 4, z % s.lz) for z in range(s.nz)]
    via = [pick(info[g], 5, 0) for g in range(s.nd)]
    vert = [2.0 * p * q / (p + q) for p, q in zip(cond, cond[1:] + cond[-1:])]
    blocks = []
    for g in range(s.nd):
        b = jnp.transpose(info[g])
        lane = iota((LN, 8), 1)
        col = [jnp.sum(jnp.where(lane == k, b, 0.0), axis=1, keepdims=True) for k in range(4)]
        col = [x[: s.nb] for x in col]
        blocks.append((col[0], col[0] + col[2], col[1], col[1] + col[3]))
    return cond, vert, via, blocks


def level_coeffs(s, level, values, via_up, via_down, scale):
    cond, vert, via, blocks = values
    d, t = place()
    size = 4**level
    n, own = (s.we, s.wc) if level == 0 else (s.w1, s.c1)
    height, nj = (s.re, s.j0) if level == 0 else (s.e1, s.j1)
    pad = HY if level == 0 else s.pad1
    halo = HX // size

    def columns(shape, axis):
        p = iota(shape, axis)
        return p, d * own + jnp.where(p >= n - halo, p - n, p)

    first = t * (s.rows // size) - pad
    row = ((first + iota((1, LN), 1)) * size).astype(F32)
    col = (columns((1, n), 1)[1] * size).astype(F32)
    rr = first + iota((height, n), 0)
    pp, cc = columns((height, n), 1)
    inside = (rr >= 0) & (rr < s.rows * s.nt // size) & (cc >= 0) & (cc < s.width // size)
    inside = jnp.where(inside & ((pp < own + halo) | (pp >= n - halo)), OMEGA, 0.0)
    via_down[0] = jnp.zeros(via_down.shape[1:], F32)
    for g in range(s.nd):
        r0, r1, c0, c1 = blocks[g]
        m = pair_dot(
            overlap(row, float(size), r0, r1).astype(BF16), overlap(col, float(size), c0, c1).astype(BF16)
        )[:height]
        top = (g + 1) * s.lz - 1
        m = m * (via[g] * (0.25**level))
        for j in range(nj):
            via_up[g, j] = m[:, tiles(j)] / cond[top]
            if g + 1 < s.nd:
                via_down[g + 1, j] = m[:, tiles(j)] / cond[top + 1]
    for z in range(s.nz):
        g, a = z // s.lz, z % s.lz
        const = 4.0
        if a < s.lz - 1:
            const = const + vert[z] * (4.0**level) / cond[z]
        if a > 0:
            const = const + vert[z - 1] * (4.0**level) / cond[z]
        for j in range(nj):
            diag = const
            if a == s.lz - 1:
                diag = diag + via_up[g, j]
            if a == 0:
                diag = diag + via_down[g, j]
            scale[z, j] = inside[:, tiles(j)] / diag


def coeff_fine_kernel(s, prm, up0, down0, e0, c, ic, cu, cd):
    values = die_values(s, prm)
    cond, vert = values[:2]
    for z in range(s.nz):
        c[z] = jnp.zeros((8, LN), F32) + cond[z]
        ic[z] = jnp.zeros((8, LN), F32) + 1.0 / cond[z]
        cu[z] = jnp.zeros((8, LN), F32) + vert[z] / cond[z]
        cd[z] = jnp.zeros((8, LN), F32) + vert[max(z - 1, 0)] / cond[z]
    level_coeffs(s, 0, values, up0, down0, e0)


def coeff_coarse_kernel(s, prm, up1, down1, e1, u2, l2, e2):
    values = die_values(s, prm)
    cond, vert, via, blocks = values
    level_coeffs(s, 1, values, up1, down1, e1)
    group = iota((1, LN), 1) // s.c2
    xin = iota((1, LN), 1) % s.c2

    def by_group(values):
        out = jnp.zeros((1, LN), F32)
        for g in range(s.nd):
            out = jnp.where(group == g, values[g], out)
        return out

    cl = [by_group([cond[s.lz * g + a] for g in range(s.nd)]) * 16.0 for a in range(s.lz)]
    vl = [by_group([vert[s.lz * g + a] for g in range(s.nd)]) * 256.0 for a in range(s.lz)]
    vial = by_group(via)
    row2 = (iota((1, LN), 1) * 16).astype(F32)
    ra = jnp.concatenate([overlap(row2, 16.0, b[0], b[1]) for b in blocks], axis=0).astype(BF16)
    zero2 = jnp.zeros((s.nt, LN), F32)
    for e in range(s.nd):
        col2 = ((e * s.c2 + xin) * 16).astype(F32)
        cb = jnp.concatenate(
            [jnp.where(group == g, overlap(col2, 16.0, b[2], b[3]), 0.0) for g, b in enumerate(blocks)],
            axis=0,
        ).astype(BF16)
        v2 = pair_dot(ra, cb)[: s.nt] * vial
        ups = [zero2 + vl[a] for a in range(s.lz - 1)] + [v2]
        first = jnp.where(iota((s.nt, LN), 1) >= s.c2, pltpu.roll(v2, s.c2, 1), 0.0)
        lows = [first] + ups[:-1]
        for a in range(s.lz):
            q = e * s.lz + a
            u2[q] = ups[a] / cl[a]
            l2[q] = lows[a] / cl[a]
            e2[q] = OMEGA * cl[a] / (4.0 * cl[a] + ups[a] + lows[a])


class Level:
    def __init__(self, s, level, up, down, scale, cu, cd):
        self.s, self.up, self.down, self.scale, self.cu, self.cd = s, up, down, scale, cu, cd
        self.nj = (s.j0, s.j1)[level]
        self.us = 4.0**level

    def walk(self, src, f, lo, hi, emit, count=None):
        s, n = self.s, self.nj
        lane = iota((8, LN), 1)
        first, last = lane == 0, lane == LN - 1

        def group(g, carry):
            for a in range(s.lz):
                z = g * s.lz + a
                for r in windows(lo, hi):
                    rows = pl.ds(r, 8)
                    v = [src[z + 1, j, rows, :] for j in range(n)]
                    ahead = [pltpu.roll(x, LN - 1, 1) for x in v]
                    behind = [pltpu.roll(x, 1, 1) for x in v]
                    for j in range(count or n):
                        k_up = self.cu[z] * self.us if a < s.lz - 1 else self.up[g, j, rows, :]
                        k_down = self.cd[z] * self.us if a > 0 else self.down[g, j, rows, :]
                        x = jnp.where(last, ahead[(j + 1) % n], ahead[j]) + jnp.where(first, behind[j - 1], behind[j])
                        y = src[z + 1, j, pl.ds(r - 1, 8), :] + src[z + 1, j, pl.ds(r + 1, 8), :]
                        x = (f[z, j, rows, :] + x) + y
                        x = x + (k_up * src[z + 2, j, rows, :] + k_down * src[z, j, rows, :])
                        emit(z, j, rows, v[j], x, k_up, k_down)
            return carry

        lax.fori_loop(0, s.nd, group, 0)

    def sweep(self, src, dst, f, lo, hi):
        def emit(z, j, rows, v, g, *_):
            dst[z + 1, j, rows, :] = (1.0 - OMEGA) * v + self.scale[z, j, rows, :] * g

        self.walk(src, f, lo, hi, emit)

    def residual(self, src, f, lo, hi, put, count=None):
        def emit(z, j, rows, v, g, k_up, k_down):
            put(z, j, rows, g - (4.0 + k_up + k_down) * v)

        self.walk(src, f, lo, hi, emit, count)


def zero_ends(s, *bufs):
    for b in bufs:
        b[0] = jnp.zeros(b.shape[1:], F32)
        b[s.nz + 1] = jnp.zeros(b.shape[1:], F32)


def restrict(s, level, src, f, lo, hi, down, rbuf, sums, r1):
    for k in range(s.nz * s.j0):
        rbuf[k * s.re : k * s.re + 8, :] = jnp.zeros((8, LN), F32)
        rbuf[(k + 1) * s.re - 8 : (k + 1) * s.re, :] = jnp.zeros((8, LN), F32)

    def put(z, j, rows, x):
        rbuf[pl.ds((z * s.j0 + j) * s.re + rows.start, 8), :] = x

    level.residual(src, f, lo, hi, put)

    def body(z, carry):
        for j in range(s.j0):
            part = [rbuf[pl.ds((z * s.j0 + j) * s.re + k, s.r1, stride=4), :] for k in range(4)]
            sums[z, :, tiles(j)] = (part[0] + part[1]) + (part[2] + part[3])
        return carry

    lax.fori_loop(0, s.nz, body, 0)
    out = split_dot(sums[...].reshape(s.nz * s.r1, s.we), down[...])
    for z in range(s.nz):
        for j in range(s.j1):
            r1[z, j] = out[z * s.r1 : (z + 1) * s.r1, tiles(j)]


def down_kernel(s, out):
    p, q = iota((s.we, s.w1), 0), iota((s.we, s.w1), 1)
    at = p // 4 + jnp.where(p >= s.wc + HX, s.w1 - s.we // 4, 0)
    out[...] = jnp.where(at == q, 0.25, 0.0).astype(BF16)


def fine_own_kernel(s, top, bot, up0, down0, e0, ic, cu, cd, down, r1, fore, aft, f, va, vb, rbuf, sums):
    level = Level(s, 0, up0, down0, e0, cu, cd)
    zero_ends(s, va, vb)
    zero = jnp.zeros((8, LN), F32)

    def body(z, carry):
        for k in range(s.re // 8):
            rows = slice(8 * k, 8 * k + 8)
            for j in range(s.j0):
                if HY <= 8 * k < HY + s.rows:
                    x = (top, bot)[k - HY // 8][z * s.j0 + j] * ic[z]
                    f[z, j, rows, :] = x
                    va[z + 1, j, rows, :] = e0[z, j, rows, :] * x
                else:
                    f[z, j, rows, :] = zero
                    va[z + 1, j, rows, :] = zero
                    vb[z + 1, j, rows, :] = zero
        return carry

    lax.fori_loop(0, s.nz, body, 0)
    level.sweep(va, vb, f, HY - 1, HY + s.rows + 1)
    restrict(s, level, vb, f, HY - 2, HY + s.rows + 2, down, rbuf, sums, r1)
    low = iota((s.r1, LN), 0) < s.r1 // 2

    def halves(z, carry):
        a, b = r1[z, 0], r1[z, 1]
        fore[z] = jnp.where(low, pltpu.roll(a, s.r1 // 2, 0), b)
        aft[z] = jnp.where(low, a, pltpu.roll(b, s.r1 // 2, 0))
        return carry

    lax.fori_loop(0, s.nz, halves, 0)


def middle_first_kernel(s, r1p, r1, r1n, up1, down1, e1, cu, cd, down2, *refs):
    far, (rx, w2, send, wa, buf) = refs[:-5], refs[-5:]
    level = Level(s, 1, up1, down1, e1, cu, cd)
    half, own, pad = s.r1, s.own1, s.pad1
    sub = iota((half, LN), 0)
    _, t = place()
    from_p, from_n = (t >= 1).astype(F32), (t < s.nt - 1).astype(F32)
    from_pp, from_nn = (t >= 2).astype(F32), (t < s.nt - 2).astype(F32)
    zero_ends(s, wa, w2)

    def body(z, carry):
        for j in range(s.j1):
            mid = pltpu.roll(r1[z, j], half // 2, 0)
            up = from_p * r1p[z, j] + jnp.where(sub >= half // 2, mid, 0.0)
            down = from_n * r1n[z, j] + jnp.where(sub < half // 2, mid, 0.0)
            if far:
                fore, aft = far[0][z], far[1][z]
                fore = pltpu.roll(fore, half // 2, 0) if j == 1 else fore
                aft = pltpu.roll(aft, half // 2, 0) if j == 0 else aft
                up += from_pp * jnp.where(sub < half // 2, fore, 0.0)
                down += from_nn * jnp.where(sub >= half // 2, aft, 0.0)
            rx[z, j, :half, :] = up
            rx[z, j, half:, :] = down
            wa[z + 1, j, :half, :] = e1[z, j, :half, :] * up
            wa[z + 1, j, half:, :] = e1[z, j, half:, :] * down
        return carry

    lax.fori_loop(0, s.nz, body, 0)
    level.sweep(wa, w2, rx, pad - 4, pad + own + 4)

    def put(z, j, rows, x):
        buf[pl.ds(pl.multiple_of(z * 8, 8), 8), :] = x

    level.residual(w2, rx, pad - 2, pad + own + 2, put, 1)
    sub8, group = iota((8, LN), 0), iota((8, LN), 1) // s.c2
    tile = jnp.zeros((8, LN), F32)
    for h in range(s.nz // 8):
        part = [buf[pl.ds(64 * h + 2 + k, 8, stride=8), :] for k in range(own)]
        x = split_dot((part[0] + part[1]) + (part[2] + part[3]), down2[...])
        y = pltpu.roll(x, 4, 0)
        for g in (2 * h, 2 * h + 1):
            tile = jnp.where(group == g, jnp.where((sub8 < 4) == (g % 2 == 0), x, y), tile)
    for k in range(s.nd * s.nt * s.lz // 8):
        send[8 * k : 8 * k + 8, :] = tile


def coarse(s, got, u2, l2, e2, cs):
    lane = iota((s.nt, LN), 1)
    x, t = lane % s.c2, iota((s.nt, LN), 0)
    first_x, last_x = x == 0, x == s.c2 - 1
    slabs = s.nd * s.lz
    rhs, v = [], []
    for q in range(slabs):
        e, a = q // s.lz, q % s.lz
        r = got[pl.ds(e * s.nt * s.lz + a, s.nt, stride=s.lz), :]
        rhs.append(r)
        v.append(e2[q] * r)
    zero = jnp.zeros((s.nt, LN), F32)

    def body(_, v):
        new = []
        for q in range(slabs):
            e, a = q // s.lz, q % s.lz
            w = v[q]
            right = pltpu.roll(v[q + s.lz], s.c2 - 1, 1) if e < s.nd - 1 else zero
            left = pltpu.roll(v[q - s.lz], LN - (s.c2 - 1), 1) if e > 0 else zero
            side = jnp.where(last_x, right, pltpu.roll(w, LN - 1, 1))
            side += jnp.where(first_x, left, pltpu.roll(w, 1, 1))
            side += jnp.where(t == s.nt - 1, 0.0, pltpu.roll(w, s.nt - 1, 0))
            side += jnp.where(t == 0, 0.0, pltpu.roll(w, 1, 0))
            if a < s.lz - 1:
                up = v[q + 1]
            else:
                up = jnp.where(lane >= LN - s.c2, 0.0, pltpu.roll(v[q - a], LN - s.c2, 1))
            if a > 0:
                down = v[q - 1]
            else:
                down = jnp.where(lane < s.c2, 0.0, pltpu.roll(v[q + s.lz - 1], s.c2, 1))
            g = (rhs[q] + side) + (u2[q] * up + l2[q] * down)
            new.append((1.0 - OMEGA) * w + e2[q] * g)
        return tuple(new)

    v = lax.fori_loop(0, NC - 1, body, tuple(v))
    for q in range(slabs):
        cs[q, :HY, :] = jnp.zeros((HY, LN), F32)
        cs[q, HY + s.nt :, :] = jnp.zeros((HY, LN), F32)
        cs[q, HY : HY + s.nt, :] = v[q]


def middle_last(s, level, cs, spread2, w2, rx, comp, wide, wa, wb):
    d, t = place()
    lane, upper = iota((8, LN), 1), iota((8, LN), 0) < 4
    after = lax.rem(d + 1, s.nd) * s.lz
    before = lax.rem(d + s.nd - 1, s.nd) * s.lz
    zero_ends(s, wa, wb)
    for a in range(s.lz):
        rows = [cs[base + a, pl.ds(HY - 1 + t, 8), :] for base in (d * s.lz, after, before)]
        for g in range(s.nd):
            turn = []
            for r, by in zip(rows, (0, s.c2, LN - s.c2)):
                by = (by - g * s.c2) % LN
                turn.append(pltpu.roll(r, by, 1) if by else r)
            z = g * s.lz + a
            comp[8 * z : 8 * z + 8, :] = jnp.where(
                lane < s.c2, turn[0], jnp.where(lane < LN // 2, turn[1], turn[2])
            )
    wide[...] = split_dot(comp[...], spread2[...]).reshape(wide.shape)

    def body(z, carry):
        x = [[wide[z, k : k + 1, tiles(j)] for k in range(3)] for j in range(s.j1)]
        for k in range(2):
            rows = slice(s.pad1 - 4 + 4 * k, s.pad1 + 4 + 4 * k)
            for j in range(s.j1):
                y = w2[z + 1, j, rows, :] + jnp.where(upper, x[j][k], x[j][k + 1])
                wa[z + 1, j, rows, :] = jnp.where(level.scale[z, j, rows, :] > 0.0, y, 0.0)
        return carry

    lax.fori_loop(0, s.nz, body, 0)
    level.sweep(wa, wb, rx, s.pad1 - 3, s.pad1 + s.own1 + 3)
    level.sweep(wb, wa, rx, s.pad1 - 2, s.pad1 + s.own1 + 2)


def correct_fine(s, w, v, spread1, wide, dst):
    rows = slice(s.pad1 - 2, s.pad1 + s.own1 + 2)
    lhs = jnp.concatenate([w[1 : s.nz + 1, j, rows, :].reshape(s.nz * s.r1, LN) for j in range(s.j1)], axis=1)
    wide[...] = split_dot(lhs, spread1[...]).reshape(wide.shape)
    upper = iota((8, LN), 0) < 4

    def body(z, carry):
        for k in range(s.r1 // 2):
            rows = slice(8 * k, 8 * k + 8)
            for j in range(s.j0):
                x = [wide[z, 2 * k + i : 2 * k + i + 1, tiles(j)] for i in range(2)]
                dst[z + 1, j, rows, :] = v[z + 1, j, rows, :] + jnp.where(upper, x[0], x[1])
        return carry

    lax.fori_loop(0, s.nz, body, 0)


def back_kernel(
    s, got, above, top, bot, below, w2, rx,
    u2, l2, e2, up1, down1, e1, up0, down0, e0, ic, cu, cd, spread2, spread1, down,
    f, v, r1, cs, comp, wide2, wa, wb, va, vb, wide, rbuf,
):
    fine = Level(s, 0, up0, down0, e0, cu, cd)
    middle = Level(s, 1, up1, down1, e1, cu, cd)
    zero_ends(s, va, vb, v)

    def body(z, carry):
        for k, ref in enumerate((above, top, bot, below)):
            rows = slice(k * HY, (k + 1) * HY)
            for j in range(s.j0):
                x = ref[z * s.j0 + j] * ic[z]
                f[z, j, rows, :] = x
                va[z + 1, j, rows, :] = e0[z, j, rows, :] * x
        return carry

    lax.fori_loop(0, s.nz, body, 0)
    fine.sweep(va, vb, f, 1, s.re - 1)
    coarse(s, got, u2, l2, e2, cs)
    middle_last(s, middle, cs, spread2, w2, rx, comp, wide2, wa, wb)
    correct_fine(s, wa, vb, spread1, wide, va)
    fine.sweep(va, vb, f, 2, s.re - 2)
    fine.sweep(vb, va, f, 3, s.re - 3)
    fine.sweep(va, vb, f, 4, s.re - 4)
    fine.sweep(vb, v, f, 5, s.re - 5)
    restrict(s, fine, v, f, HY, HY + s.rows, down, rbuf, wide, r1)


def last_kernel(
    s, got, w2, rx, v2, f, u2, l2, e2, up1, down1, e1, up0, down0, e0, c, cu, cd, spread2, spread1, *refs,
):
    outs, (cs, comp, wide2, wa, wb, va, vb, wide, rbuf) = refs[: s.nd], refs[s.nd :]
    fine = Level(s, 0, up0, down0, e0, cu, cd)
    middle = Level(s, 1, up1, down1, e1, cu, cd)
    d, _ = place()
    zero_ends(s, va, vb)
    coarse(s, got, u2, l2, e2, cs)
    middle_last(s, middle, cs, spread2, w2, rx, comp, wide2, wa, wb)
    correct_fine(s, wa, v2, spread1, wide, va)
    fine.sweep(va, vb, f, HY - 2, HY + s.rows + 2)
    fine.sweep(vb, va, f, HY - 1, HY + s.rows + 1)

    def put(z, j, rows, x):
        at = (z * (s.j0 - 1) + j) * s.rows + rows.start - HY
        rbuf[pl.ds(pl.multiple_of(at, 8), 8), :] = x * c[z]

    fine.residual(va, f, HY, HY + s.rows, put, s.j0 - 1)
    for step, out in enumerate(outs):
        e = lax.rem(d + step, s.nd)
        for a in range(s.lz):
            z = e * s.lz + a
            for j in range(s.j0 - 1):
                out[0, a, :, tiles(j)] = va[z + 1, j, HY : HY + s.rows, :]
                at = pl.multiple_of((z * (s.j0 - 1) + j) * s.rows, 8)
                out[1, a, :, tiles(j)] = rbuf[pl.ds(at, s.rows), :]


def unpack_kernel(s, *refs):
    parts, outs, sem = refs[: s.nd], refs[s.nd : -1], refs[-1]
    d, _ = place()
    copies = []
    for step, part in enumerate(parts):
        e = lax.rem(d + s.nd - step, s.nd)
        cols = pl.ds(pl.multiple_of(e * s.wc, LN), s.wc)
        for k, out in enumerate(outs):
            copies.append(pltpu.make_async_copy(part.at[k], out.at[:, :, cols], sem.at[len(outs) * step + k]))
    for c in copies:
        c.start()
    for c in copies:
        c.wait()


def call(kernel, s, outs, scratch=(), to_hbm=False, from_hbm=False, in_vmem=False, limit=32 << 20):
    shapes = [pltpu.VMEM(o, F32) if in_vmem else jax.ShapeDtypeStruct(o, F32) for o in outs]
    spaces = [pl.BlockSpec(memory_space=m) for m in (pltpu.VMEM, pltpu.HBM)]

    def run(*args):
        total = sum(int(np.prod(a.shape)) * 4 for a in args) + sum(int(np.prod(o)) * 4 for o in outs)
        return pl.pallas_call(
            functools.partial(kernel, s),
            out_shape=shapes,
            in_specs=[spaces[from_hbm]] * len(args),
            out_specs=[spaces[to_hbm]] * len(outs),
            scratch_shapes=[pltpu.VMEM(x, F32) if isinstance(x, tuple) else x for x in scratch],
            compiler_params=pltpu.CompilerParams(vmem_limit_bytes=limit),
            cost_estimate=pl.CostEstimate(flops=4 * total, bytes_accessed=total, transcendentals=0),
        )(*args)

    return run


def shift(x, axis, by):
    n = lax.axis_size(axis)
    return lax.ppermute(x, axis, [(i, (i + by) % n) for i in range(n)])


def tables(s):
    p = np.arange(s.we)
    at = p // 4 + np.where(p >= s.wc + HX, s.w1 - s.we // 4, 0)
    down = at[:, None] == np.arange(s.w1)[None, :]
    q = np.arange(s.w1)
    k = q // 4 + np.where(q >= s.w1 - HX // 4, LN - s.w1 // 4, 0)
    used = (q < s.c1 + HX // 4) | (q >= s.w1 - HX // 4)
    spread2 = (np.arange(LN)[:, None] == k[None, :]) & used[None, :]
    r = np.arange(LN)
    down2 = (r // 4)[:, None] == (r % s.c2)[None, :]
    return [jnp.asarray(m, BF16) for m in (down.T, spread2, down2 * 0.25)]


def local(s, source_heating, material_thermal_values, layer_material, via_conductance, via_blocks):
    spread1, spread2, down2 = tables(s)
    down = pl.pallas_call(
        functools.partial(down_kernel, s),
        name="down",
        out_shape=jax.ShapeDtypeStruct((s.we, s.w1), BF16),
        compiler_params=pltpu.CompilerParams(vmem_limit_bytes=4 << 20),
        cost_estimate=pl.CostEstimate(flops=1 << 20, bytes_accessed=1 << 20, transcendentals=0),
    )()
    smem, packed = pltpu.SMEM, (s.part + 8, LN)
    sends = call(
        pack_kernel, s, [packed] * s.nd,
        [
            smem(material_thermal_values.shape, F32), smem(layer_material.shape, jnp.int32),
            smem((1, 1), F32), pltpu.VMEM((4, s.nb), jnp.int32),
            pltpu.VMEM(source_heating.shape, F32), pltpu.SemaphoreType.DMA((5,)),
        ],
        from_hbm=True, in_vmem=True, limit=VMEM - 4 * s.nd * packed[0] * packed[1],
    )(material_thermal_values, layer_material, via_conductance[None], via_blocks[0].T, source_heating)
    parts = [sends[0]] + [shift(sends[k], "die", k) for k in range(1, s.nd)]
    half = (s.nz * s.j0, HY, LN)
    top, bot, prm = call(assemble_kernel, s, [half, half, (s.nd, 8, LN)])(*parts)
    f0, f1, small = (s.j0, s.re, LN), (s.j1, s.e1, LN), (s.nz, s.j1, s.r1, LN)
    fine, fine_v = (s.nz, *f0), (s.nz + 2, *f0)
    mid, mid_v = (s.nz, *f1), (s.nz + 2, *f1)
    slab, table = (s.nd * s.lz, s.nt, LN), (s.nz, 8, LN)
    up0, down0, e0, c, ic, cu, cd = call(
        coeff_fine_kernel, s, [(s.nd, *f0), (s.nd, *f0), fine, table, table, table, table]
    )(prm)
    flat, rbuf = (s.nz, s.r1, s.we), (s.nz * s.j0 * s.re, LN)
    r1, fore, aft = call(fine_own_kernel, s, [small, table, table], [fine, fine_v, fine_v, rbuf, flat])(
        top, bot, up0, down0, e0, ic, cu, cd, down
    )
    up1, down1, e1, u2, l2, e2 = call(coeff_coarse_kernel, s, [(s.nd, *f1), (s.nd, *f1), mid, slab, slab, slab])(prm)

    def middle_first(r1, *far):
        return call(
            middle_first_kernel, s,
            [mid, mid_v, (s.nd * s.nt * s.lz, LN)], [mid_v, (s.nz * 8, LN)],
        )(shift(r1, "tile", 1), r1, shift(r1, "tile", -1), up1, down1, e1, cu, cd, down2, *far)

    def everywhere(send):
        return lax.all_to_all(send, ("die", "tile"), 0, 0, tiled=True)

    spaces = [(s.nd * s.lz, s.nt + 2 * HY, LN), (s.nz * 8, LN), (s.nz, 8, s.w1), mid_v, mid_v]
    spaces += [fine_v, fine_v, flat]
    rx, w2, send = middle_first(r1, shift(fore, "tile", 2), shift(aft, "tile", -2))
    above, below = shift(bot, "tile", 1), shift(top, "tile", -1)
    above, below, send = lax.optimization_barrier((above, below, send))
    levels = (u2, l2, e2, up1, down1, e1, up0, down0, e0)
    f, v, r1 = call(back_kernel, s, [fine, fine_v, small], spaces + [rbuf])(
        everywhere(send), above, top, bot, below, w2, rx,
        *levels, ic, cu, cd, spread2, spread1, down,
    )
    rx, w2, send = middle_first(r1)
    piece = (2, s.lz, s.rows, s.wc)
    sends = call(
        last_kernel, s, [piece] * s.nd, spaces + [(s.nz * (s.j0 - 1) * s.rows, LN)]
    )(everywhere(send), w2, rx, v, f, *levels, c, cu, cd, spread2, spread1)
    parts = [sends[0]] + [shift(sends[k], "die", k) for k in range(1, s.nd)]
    whole = (s.lz, s.rows, s.width)
    return tuple(call(unpack_kernel, s, [whole] * 2, [pltpu.SemaphoreType.DMA((2 * s.nd,))], True)(*parts))


def solution(mesh):
    in_specs = (P("die", "tile", None), P(), P("die"), P("die"), P("die", None, None))
    out_specs = (P("die", "tile", None), P("die", "tile", None))

    def body(f, mat, material, conductance, blocks):
        s = Sizes(mesh.shape, f.shape, blocks.shape[1])
        return local(s, f, mat, material, conductance, blocks)

    return jax.shard_map(body, mesh=mesh, in_specs=in_specs, out_specs=out_specs, check_vma=False)
```

```python
import functools

import jax
import jax.numpy as jnp
import numpy as np
from jax import lax
from jax.experimental import pallas as pl
from jax.experimental.pallas import tpu as pltpu
from jax.sharding import PartitionSpec as P

OMEGA = 0.8
NC = 6
LN = 128
HX = 64
VMEM = 67_043_328
HY = 8
F32 = jnp.float32
BF16 = jnp.bfloat16


def iota(shape, axis):
    return lax.broadcasted_iota(jnp.int32, shape, axis)


def split_dot(x, m):
    hi = x.astype(BF16)
    lo = (x - hi.astype(F32)).astype(BF16)
    return jnp.dot(hi, m, preferred_element_type=F32) + jnp.dot(lo, m, preferred_element_type=F32)


def pair_dot(a, b):
    return lax.dot_general(a, b, (((0,), (0,)), ((), ())), preferred_element_type=F32)


class Sizes:
    def __init__(self, mesh_shape, f_shape, n_blocks):
        self.nd, self.nt = mesh_shape["die"], mesh_shape["tile"]
        self.lz, self.rows, self.width = f_shape
        self.nb = n_blocks
        self.wc = self.width // self.nd
        self.we = self.wc + LN
        self.j0 = self.we // LN
        self.nz = self.nd * self.lz
        self.re = self.rows + 2 * HY
        self.own1 = self.rows // 4
        self.r1 = self.re // 4
        self.c1 = self.wc // 4
        self.e1 = 2 * self.r1
        self.pad1 = (self.e1 - self.own1) // 2
        self.j1 = 2
        self.w1 = self.j1 * LN
        self.c2 = self.wc // 16
        self.part = self.lz * self.j0 * self.rows
        assert self.rows == 16 and self.lz == 4 and self.c1 == LN
        assert self.nd * self.c2 == LN and self.nb <= LN and self.nt <= LN and self.nt % 8 == 0


def place():
    return lax.axis_index("die"), lax.axis_index("tile")


def even(stride):
    _, t = place()
    return lax.rem(t // stride, 2) == 0


def tiles(j):
    return slice(j * LN, (j + 1) * LN)


def windows(lo, hi):
    return [min(r, hi - 8) for r in range(lo, hi, 8)]


def pack_kernel(s, mat_h, material_h, conductance_h, blocks_h, f_h, *refs):
    outs, (mat, material, conductance, blocks, f, sem) = refs[: s.nd], refs[s.nd :]
    pairs = [(f_h, f), (mat_h, mat), (material_h, material), (conductance_h, conductance), (blocks_h, blocks)]
    copies = [pltpu.make_async_copy(a, b, sem.at[k]) for k, (a, b) in enumerate(pairs)]
    for c in copies:
        c.start()
    for c in copies[1:]:
        c.wait()
    d, _ = place()
    lane, sub = iota((8, LN), 1), iota((8, LN), 0)
    info = jnp.where((sub == 5) & (lane == 0), conductance[0, 0], 0.0)
    for z in range(s.lz):
        info = jnp.where((sub == 4) & (lane == z), mat[material[z]], info)
    for out in outs:
        out[s.part :, :] = info
        out[s.part : s.part + 4, : s.nb] = blocks[...].astype(F32)
    copies[0].wait()
    low = iota((s.rows, LN), 1) < HX
    for step, out in enumerate(outs):
        e = lax.rem(d + step, s.nd)
        right = lax.rem(e + 1, s.nd) * s.wc
        left = lax.rem(e + s.nd - 1, s.nd) * s.wc + (s.wc - LN)

        def column(z, at):
            return f[z, :, pl.ds(pl.multiple_of(at, LN), LN)]

        for z in range(s.lz):
            for j in range(s.j0):
                at = (z * s.j0 + j) * s.rows
                if j < s.j0 - 1:
                    x = column(z, e * s.wc + j * LN)
                else:
                    x = jnp.where(low, column(z, right), column(z, left))
                out[at : at + s.rows, :] = x


def assemble_kernel(s, *refs):
    parts, (one, two, prm) = refs[: s.nd], refs[s.nd :]
    d, _ = place()
    n = s.lz * s.j0
    lower = even(1)
    for step, part in enumerate(parts):
        e = lax.rem(d + s.nd - step, s.nd)
        for q in range(n):
            top = part[q * s.rows : q * s.rows + HY, :]
            bot = part[q * s.rows + HY : (q + 1) * s.rows, :]
            one[n * e + q] = jnp.where(lower, bot, top)
            two[n * e + q] = jnp.where(lower, top, bot)
        prm[e] = part[s.part :, :]


def overlap(lo, size, first, past):
    return jnp.maximum(jnp.minimum(lo + size, past) - jnp.maximum(lo, first), 0.0)


def die_values(s, prm):
    lane8, sub8 = iota((8, LN), 1), iota((8, LN), 0)

    def pick(tile, row, col):
        return jnp.sum(jnp.where((lane8 == col) & (sub8 == row), tile, 0.0), keepdims=True)

    info = [prm[g] for g in range(s.nd)]
    cond = [pick(info[z // s.lz], 4, z % s.lz) for z in range(s.nz)]
    via = [pick(info[g], 5, 0) for g in range(s.nd)]
    vert = [2.0 * p * q / (p + q) for p, q in zip(cond, cond[1:] + cond[-1:])]
    blocks = []
    for g in range(s.nd):
        b = jnp.transpose(info[g])
        lane = iota((LN, 8), 1)
        col = [jnp.sum(jnp.where(lane == k, b, 0.0), axis=1, keepdims=True) for k in range(4)]
        col = [x[: s.nb] for x in col]
        blocks.append((col[0], col[0] + col[2], col[1], col[1] + col[3]))
    return cond, vert, via, blocks


def level_coeffs(s, level, values, via_up, via_down, scale):
    cond, vert, via, blocks = values
    d, t = place()
    size = 4**level
    n, own = (s.we, s.wc) if level == 0 else (s.w1, s.c1)
    height, nj = (s.re, s.j0) if level == 0 else (s.e1, s.j1)
    pad = HY if level == 0 else s.pad1
    halo = HX // size

    def columns(shape, axis):
        p = iota(shape, axis)
        return p, d * own + jnp.where(p >= n - halo, p - n, p)

    first = t * (s.rows // size) - pad
    row = ((first + iota((1, LN), 1)) * size).astype(F32)
    col = (columns((1, n), 1)[1] * size).astype(F32)
    rr = first + iota((height, n), 0)
    pp, cc = columns((height, n), 1)
    inside = (rr >= 0) & (rr < s.rows * s.nt // size) & (cc >= 0) & (cc < s.width // size)
    inside = jnp.where(inside & ((pp < own + halo) | (pp >= n - halo)), OMEGA, 0.0)
    via_down[0] = jnp.zeros(via_down.shape[1:], F32)
    for g in range(s.nd):
        r0, r1, c0, c1 = blocks[g]
        m = pair_dot(
            overlap(row, float(size), r0, r1).astype(BF16), overlap(col, float(size), c0, c1).astype(BF16)
        )[:height]
        top = (g + 1) * s.lz - 1
        m = m * (via[g] * (0.25**level))
        for j in range(nj):
            via_up[g, j] = m[:, tiles(j)] / cond[top]
            if g + 1 < s.nd:
                via_down[g + 1, j] = m[:, tiles(j)] / cond[top + 1]
    for z in range(s.nz):
        g, a = z // s.lz, z % s.lz
        const = 4.0
        if a < s.lz - 1:
            const = const + vert[z] * (4.0**level) / cond[z]
        if a > 0:
            const = const + vert[z - 1] * (4.0**level) / cond[z]
        for j in range(nj):
            diag = const
            if a == s.lz - 1:
                diag = diag + via_up[g, j]
            if a == 0:
                diag = diag + via_down[g, j]
            scale[z, j] = inside[:, tiles(j)] / diag


def coeff_fine_kernel(s, prm, up0, down0, e0, c, ic, cu, cd):
    values = die_values(s, prm)
    cond, vert = values[:2]
    for z in range(s.nz):
        c[z] = jnp.zeros((8, LN), F32) + cond[z]
        ic[z] = jnp.zeros((8, LN), F32) + 1.0 / cond[z]
        cu[z] = jnp.zeros((8, LN), F32) + vert[z] / cond[z]
        cd[z] = jnp.zeros((8, LN), F32) + vert[max(z - 1, 0)] / cond[z]
    level_coeffs(s, 0, values, up0, down0, e0)


def coeff_coarse_kernel(s, prm, up1, down1, e1, u2, l2, e2):
    values = die_values(s, prm)
    cond, vert, via, blocks = values
    level_coeffs(s, 1, values, up1, down1, e1)
    group = iota((1, LN), 1) // s.c2
    xin = iota((1, LN), 1) % s.c2

    def by_group(values):
        out = jnp.zeros((1, LN), F32)
        for g in range(s.nd):
            out = jnp.where(group == g, values[g], out)
        return out

    cl = [by_group([cond[s.lz * g + a] for g in range(s.nd)]) * 16.0 for a in range(s.lz)]
    vl = [by_group([vert[s.lz * g + a] for g in range(s.nd)]) * 256.0 for a in range(s.lz)]
    vial = by_group(via)
    row2 = (iota((1, LN), 1) * 16).astype(F32)
    ra = jnp.concatenate([overlap(row2, 16.0, b[0], b[1]) for b in blocks], axis=0).astype(BF16)
    zero2 = jnp.zeros((s.nt, LN), F32)
    for e in range(s.nd):
        col2 = ((e * s.c2 + xin) * 16).astype(F32)
        cb = jnp.concatenate(
            [jnp.where(group == g, overlap(col2, 16.0, b[2], b[3]), 0.0) for g, b in enumerate(blocks)],
            axis=0,
        ).astype(BF16)
        v2 = pair_dot(ra, cb)[: s.nt] * vial
        ups = [zero2 + vl[a] for a in range(s.lz - 1)] + [v2]
        first = jnp.where(iota((s.nt, LN), 1) >= s.c2, pltpu.roll(v2, s.c2, 1), 0.0)
        lows = [first] + ups[:-1]
        for a in range(s.lz):
            q = e * s.lz + a
            u2[q] = ups[a] / cl[a]
            l2[q] = lows[a] / cl[a]
            e2[q] = OMEGA * cl[a] / (4.0 * cl[a] + ups[a] + lows[a])


class Level:
    def __init__(self, s, level, up, down, scale, cu, cd):
        self.s, self.up, self.down, self.scale, self.cu, self.cd = s, up, down, scale, cu, cd
        self.nj = (s.j0, s.j1)[level]
        self.us = 4.0**level

    def walk(self, src, f, lo, hi, emit, count=None):
        s, n = self.s, self.nj
        lane = iota((8, LN), 1)
        first, last = lane == 0, lane == LN - 1

        def group(g, carry):
            for a in range(s.lz):
                z = g * s.lz + a
                for r in windows(lo, hi):
                    rows = pl.ds(r, 8)
                    v = [src[z + 1, j, rows, :] for j in range(n)]
                    ahead = [pltpu.roll(x, LN - 1, 1) for x in v]
                    behind = [pltpu.roll(x, 1, 1) for x in v]
                    for j in range(count or n):
                        k_up = self.cu[z] * self.us if a < s.lz - 1 else self.up[g, j, rows, :]
                        k_down = self.cd[z] * self.us if a > 0 else self.down[g, j, rows, :]
                        x = jnp.where(last, ahead[(j + 1) % n], ahead[j]) + jnp.where(first, behind[j - 1], behind[j])
                        y = src[z + 1, j, pl.ds(r - 1, 8), :] + src[z + 1, j, pl.ds(r + 1, 8), :]
                        x = (f[z, j, rows, :] + x) + y
                        x = x + (k_up * src[z + 2, j, rows, :] + k_down * src[z, j, rows, :])
                        emit(z, j, rows, v[j], x, k_up, k_down)
            return carry

        lax.fori_loop(0, s.nd, group, 0)

    def sweep(self, src, dst, f, lo, hi):
        def emit(z, j, rows, v, g, *_):
            dst[z + 1, j, rows, :] = (1.0 - OMEGA) * v + self.scale[z, j, rows, :] * g

        self.walk(src, f, lo, hi, emit)

    def residual(self, src, f, lo, hi, put, count=None):
        def emit(z, j, rows, v, g, k_up, k_down):
            put(z, j, rows, g - (4.0 + k_up + k_down) * v)

        self.walk(src, f, lo, hi, emit, count)


def zero_ends(s, *bufs):
    for b in bufs:
        b[0] = jnp.zeros(b.shape[1:], F32)
        b[s.nz + 1] = jnp.zeros(b.shape[1:], F32)


def restrict(s, level, src, f, lo, hi, down, rbuf, sums, r1):
    for k in range(s.nz * s.j0):
        rbuf[k * s.re : k * s.re + 8, :] = jnp.zeros((8, LN), F32)
        rbuf[(k + 1) * s.re - 8 : (k + 1) * s.re, :] = jnp.zeros((8, LN), F32)

    def put(z, j, rows, x):
        rbuf[pl.ds((z * s.j0 + j) * s.re + rows.start, 8), :] = x

    level.residual(src, f, lo, hi, put)

    def body(z, carry):
        for j in range(s.j0):
            part = [rbuf[pl.ds((z * s.j0 + j) * s.re + k, s.r1, stride=4), :] for k in range(4)]
            sums[z, :, tiles(j)] = (part[0] + part[1]) + (part[2] + part[3])
        return carry

    lax.fori_loop(0, s.nz, body, 0)
    out = split_dot(sums[...].reshape(s.nz * s.r1, s.we), down[...])
    for z in range(s.nz):
        for j in range(s.j1):
            r1[z, j] = out[z * s.r1 : (z + 1) * s.r1, tiles(j)]


def down_kernel(s, out):
    p, q = iota((s.we, s.w1), 0), iota((s.we, s.w1), 1)
    at = p // 4 + jnp.where(p >= s.wc + HX, s.w1 - s.we // 4, 0)
    out[...] = jnp.where(at == q, 0.25, 0.0).astype(BF16)


def fine_own_kernel(s, one, two, up0, down0, e0, ic, cu, cd, down, r1, fore, aft, f, va, vb, rbuf, sums):
    level = Level(s, 0, up0, down0, e0, cu, cd)
    zero_ends(s, va, vb)
    zero = jnp.zeros((8, LN), F32)
    lower = even(1)

    def body(z, carry):
        for k in range(s.re // 8):
            rows = slice(8 * k, 8 * k + 8)
            for j in range(s.j0):
                if HY <= 8 * k < HY + s.rows:
                    q = z * s.j0 + j
                    x = one[q], two[q]
                    x = jnp.where(lower == (k > HY // 8), x[0], x[1]) * ic[z]
                    f[z, j, rows, :] = x
                    va[z + 1, j, rows, :] = e0[z, j, rows, :] * x
                else:
                    f[z, j, rows, :] = zero
                    va[z + 1, j, rows, :] = zero
                    vb[z + 1, j, rows, :] = zero
        return carry

    lax.fori_loop(0, s.nz, body, 0)
    level.sweep(va, vb, f, HY - 1, HY + s.rows + 1)
    restrict(s, level, vb, f, HY - 2, HY + s.rows + 2, down, rbuf, sums, r1)
    ahead = even(2)
    low = iota((s.r1, LN), 0) < s.r1 // 2

    def halves(z, carry):
        a, b = r1[z, 0], r1[z, 1]
        x = jnp.where(low, pltpu.roll(a, s.r1 // 2, 0), b)
        y = jnp.where(low, a, pltpu.roll(b, s.r1 // 2, 0))
        fore[z] = jnp.where(ahead, x, y)
        aft[z] = jnp.where(ahead, y, x)
        return carry

    lax.fori_loop(0, s.nz, halves, 0)


def middle_first_kernel(s, r1a, r1, r1b, up1, down1, e1, cu, cd, down2, *refs):
    far, (rx, w2, send, wa, buf) = refs[:-5], refs[-5:]
    level = Level(s, 1, up1, down1, e1, cu, cd)
    half, own, pad = s.r1, s.own1, s.pad1
    sub = iota((half, LN), 0)
    _, t = place()
    lower, ahead = even(1), even(2)
    from_p, from_n = (t >= 1).astype(F32), (t < s.nt - 1).astype(F32)
    from_pp, from_nn = (t >= 2).astype(F32), (t < s.nt - 2).astype(F32)
    zero_ends(s, wa, w2)

    def body(z, carry):
        for j in range(s.j1):
            mid = pltpu.roll(r1[z, j], half // 2, 0)
            up = from_p * jnp.where(lower, r1b[z, j], r1a[z, j]) + jnp.where(sub >= half // 2, mid, 0.0)
            down = from_n * jnp.where(lower, r1a[z, j], r1b[z, j]) + jnp.where(sub < half // 2, mid, 0.0)
            if far:
                a, b = far[0][z], far[1][z]
                fore, aft = jnp.where(ahead, b, a), jnp.where(ahead, a, b)
                fore = pltpu.roll(fore, half // 2, 0) if j == 1 else fore
                aft = pltpu.roll(aft, half // 2, 0) if j == 0 else aft
                up += from_pp * jnp.where(sub < half // 2, fore, 0.0)
                down += from_nn * jnp.where(sub >= half // 2, aft, 0.0)
            rx[z, j, :half, :] = up
            rx[z, j, half:, :] = down
            wa[z + 1, j, :half, :] = e1[z, j, :half, :] * up
            wa[z + 1, j, half:, :] = e1[z, j, half:, :] * down
        return carry

    lax.fori_loop(0, s.nz, body, 0)
    level.sweep(wa, w2, rx, pad - 4, pad + own + 4)

    def put(z, j, rows, x):
        buf[pl.ds(pl.multiple_of(z * 8, 8), 8), :] = x

    level.residual(w2, rx, pad - 2, pad + own + 2, put, 1)
    sub8, group = iota((8, LN), 0), iota((8, LN), 1) // s.c2
    tile = jnp.zeros((8, LN), F32)
    for h in range(s.nz // 8):
        part = [buf[pl.ds(64 * h + 2 + k, 8, stride=8), :] for k in range(own)]
        x = split_dot((part[0] + part[1]) + (part[2] + part[3]), down2[...])
        y = pltpu.roll(x, 4, 0)
        for g in (2 * h, 2 * h + 1):
            tile = jnp.where(group == g, jnp.where((sub8 < 4) == (g % 2 == 0), x, y), tile)
    for k in range(s.nd * s.nt * s.lz // 8):
        send[8 * k : 8 * k + 8, :] = tile


def coarse(s, got, u2, l2, e2, cs):
    lane = iota((s.nt, LN), 1)
    x, t = lane % s.c2, iota((s.nt, LN), 0)
    first_x, last_x = x == 0, x == s.c2 - 1
    slabs = s.nd * s.lz
    rhs, v = [], []
    for q in range(slabs):
        e, a = q // s.lz, q % s.lz
        r = got[pl.ds(e * s.nt * s.lz + a, s.nt, stride=s.lz), :]
        rhs.append(r)
        v.append(e2[q] * r)
    zero = jnp.zeros((s.nt, LN), F32)

    def body(_, v):
        new = []
        for q in range(slabs):
            e, a = q // s.lz, q % s.lz
            w = v[q]
            right = pltpu.roll(v[q + s.lz], s.c2 - 1, 1) if e < s.nd - 1 else zero
            left = pltpu.roll(v[q - s.lz], LN - (s.c2 - 1), 1) if e > 0 else zero
            side = jnp.where(last_x, right, pltpu.roll(w, LN - 1, 1))
            side += jnp.where(first_x, left, pltpu.roll(w, 1, 1))
            side += jnp.where(t == s.nt - 1, 0.0, pltpu.roll(w, s.nt - 1, 0))
            side += jnp.where(t == 0, 0.0, pltpu.roll(w, 1, 0))
            if a < s.lz - 1:
                up = v[q + 1]
            else:
                up = jnp.where(lane >= LN - s.c2, 0.0, pltpu.roll(v[q - a], LN - s.c2, 1))
            if a > 0:
                down = v[q - 1]
            else:
                down = jnp.where(lane < s.c2, 0.0, pltpu.roll(v[q + s.lz - 1], s.c2, 1))
            g = (rhs[q] + side) + (u2[q] * up + l2[q] * down)
            new.append((1.0 - OMEGA) * w + e2[q] * g)
        return tuple(new)

    v = lax.fori_loop(0, NC - 1, body, tuple(v))
    for q in range(slabs):
        cs[q, :HY, :] = jnp.zeros((HY, LN), F32)
        cs[q, HY + s.nt :, :] = jnp.zeros((HY, LN), F32)
        cs[q, HY : HY + s.nt, :] = v[q]


def middle_last(s, level, cs, spread2, w2, rx, comp, wide, wa, wb):
    d, t = place()
    lane, upper = iota((8, LN), 1), iota((8, LN), 0) < 4
    after = lax.rem(d + 1, s.nd) * s.lz
    before = lax.rem(d + s.nd - 1, s.nd) * s.lz
    zero_ends(s, wa, wb)
    for a in range(s.lz):
        rows = [cs[base + a, pl.ds(HY - 1 + t, 8), :] for base in (d * s.lz, after, before)]
        for g in range(s.nd):
            turn = []
            for r, by in zip(rows, (0, s.c2, LN - s.c2)):
                by = (by - g * s.c2) % LN
                turn.append(pltpu.roll(r, by, 1) if by else r)
            z = g * s.lz + a
            comp[8 * z : 8 * z + 8, :] = jnp.where(
                lane < s.c2, turn[0], jnp.where(lane < LN // 2, turn[1], turn[2])
            )
    wide[...] = split_dot(comp[...], spread2[...]).reshape(wide.shape)

    def body(z, carry):
        x = [[wide[z, k : k + 1, tiles(j)] for k in range(3)] for j in range(s.j1)]
        for k in range(2):
            rows = slice(s.pad1 - 4 + 4 * k, s.pad1 + 4 + 4 * k)
            for j in range(s.j1):
                y = w2[z + 1, j, rows, :] + jnp.where(upper, x[j][k], x[j][k + 1])
                wa[z + 1, j, rows, :] = jnp.where(level.scale[z, j, rows, :] > 0.0, y, 0.0)
        return carry

    lax.fori_loop(0, s.nz, body, 0)
    level.sweep(wa, wb, rx, s.pad1 - 3, s.pad1 + s.own1 + 3)
    level.sweep(wb, wa, rx, s.pad1 - 2, s.pad1 + s.own1 + 2)


def correct_fine(s, w, v, spread1, wide, dst):
    rows = slice(s.pad1 - 2, s.pad1 + s.own1 + 2)
    lhs = jnp.concatenate([w[1 : s.nz + 1, j, rows, :].reshape(s.nz * s.r1, LN) for j in range(s.j1)], axis=1)
    wide[...] = split_dot(lhs, spread1[...]).reshape(wide.shape)
    upper = iota((8, LN), 0) < 4

    def body(z, carry):
        for k in range(s.r1 // 2):
            rows = slice(8 * k, 8 * k + 8)
            for j in range(s.j0):
                x = [wide[z, 2 * k + i : 2 * k + i + 1, tiles(j)] for i in range(2)]
                dst[z + 1, j, rows, :] = v[z + 1, j, rows, :] + jnp.where(upper, x[0], x[1])
        return carry

    lax.fori_loop(0, s.nz, body, 0)


def back_kernel(
    s, got, from_one, from_two, one, two, w2, rx,
    u2, l2, e2, up1, down1, e1, up0, down0, e0, ic, cu, cd, spread2, spread1, down,
    f, v, r1, cs, comp, wide2, wa, wb, va, vb, wide, rbuf,
):
    fine = Level(s, 0, up0, down0, e0, cu, cd)
    middle = Level(s, 1, up1, down1, e1, cu, cd)
    zero_ends(s, va, vb, v)
    lower = even(1)

    def body(z, carry):
        for k, (a, b) in enumerate(((from_two, from_one), (two, one), (one, two), (from_one, from_two))):
            rows = slice(k * HY, (k + 1) * HY)
            for j in range(s.j0):
                q = z * s.j0 + j
                x = jnp.where(lower, a[q], b[q]) * ic[z]
                f[z, j, rows, :] = x
                va[z + 1, j, rows, :] = e0[z, j, rows, :] * x
        return carry

    lax.fori_loop(0, s.nz, body, 0)
    fine.sweep(va, vb, f, 1, s.re - 1)
    coarse(s, got, u2, l2, e2, cs)
    middle_last(s, middle, cs, spread2, w2, rx, comp, wide2, wa, wb)
    correct_fine(s, wa, vb, spread1, wide, va)
    fine.sweep(va, vb, f, 2, s.re - 2)
    fine.sweep(vb, va, f, 3, s.re - 3)
    fine.sweep(va, vb, f, 4, s.re - 4)
    fine.sweep(vb, v, f, 5, s.re - 5)
    restrict(s, fine, v, f, HY, HY + s.rows, down, rbuf, wide, r1)


def last_kernel(
    s, got, w2, rx, v2, f, u2, l2, e2, up1, down1, e1, up0, down0, e0, c, cu, cd, spread2, spread1, *refs,
):
    outs, (cs, comp, wide2, wa, wb, va, vb, wide, rbuf) = refs[: s.nd], refs[s.nd :]
    fine = Level(s, 0, up0, down0, e0, cu, cd)
    middle = Level(s, 1, up1, down1, e1, cu, cd)
    d, _ = place()
    zero_ends(s, va, vb)
    coarse(s, got, u2, l2, e2, cs)
    middle_last(s, middle, cs, spread2, w2, rx, comp, wide2, wa, wb)
    correct_fine(s, wa, v2, spread1, wide, va)
    fine.sweep(va, vb, f, HY - 2, HY + s.rows + 2)
    fine.sweep(vb, va, f, HY - 1, HY + s.rows + 1)

    def put(z, j, rows, x):
        at = (z * (s.j0 - 1) + j) * s.rows + rows.start - HY
        rbuf[pl.ds(pl.multiple_of(at, 8), 8), :] = x * c[z]

    fine.residual(va, f, HY, HY + s.rows, put, s.j0 - 1)
    for step, out in enumerate(outs):
        e = lax.rem(d + step, s.nd)
        for a in range(s.lz):
            z = e * s.lz + a
            for j in range(s.j0 - 1):
                out[0, a, :, tiles(j)] = va[z + 1, j, HY : HY + s.rows, :]
                at = pl.multiple_of((z * (s.j0 - 1) + j) * s.rows, 8)
                out[1, a, :, tiles(j)] = rbuf[pl.ds(at, s.rows), :]


def unpack_kernel(s, *refs):
    parts, outs, sem = refs[: s.nd], refs[s.nd : -1], refs[-1]
    d, _ = place()
    copies = []
    for step, part in enumerate(parts):
        e = lax.rem(d + s.nd - step, s.nd)
        cols = pl.ds(pl.multiple_of(e * s.wc, LN), s.wc)
        for k, out in enumerate(outs):
            copies.append(pltpu.make_async_copy(part.at[k], out.at[:, :, cols], sem.at[len(outs) * step + k]))
    for c in copies:
        c.start()
    for c in copies:
        c.wait()


def call(name, kernel, s, outs, scratch=(), to_hbm=False, from_hbm=False, in_vmem=False, limit=32 << 20):
    shapes = [pltpu.VMEM(o, F32) if in_vmem else jax.ShapeDtypeStruct(o, F32) for o in outs]
    spaces = [pl.BlockSpec(memory_space=m) for m in (pltpu.VMEM, pltpu.HBM)]

    def run(*args):
        total = sum(int(np.prod(a.shape)) * 4 for a in args) + sum(int(np.prod(o)) * 4 for o in outs)
        return pl.pallas_call(
            functools.partial(kernel, s),
            name=name,
            out_shape=shapes,
            in_specs=[spaces[from_hbm]] * len(args),
            out_specs=[spaces[to_hbm]] * len(outs),
            scratch_shapes=[pltpu.VMEM(x, F32) if isinstance(x, tuple) else x for x in scratch],
            compiler_params=pltpu.CompilerParams(vmem_limit_bytes=limit),
            cost_estimate=pl.CostEstimate(flops=4 * total, bytes_accessed=total, transcendentals=0),
        )(*args)

    return run


def shift(x, axis, by):
    n = lax.axis_size(axis)
    return lax.ppermute(x, axis, [(i, (i + by) % n) for i in range(n)])


def swap(x, odd, stride=1):
    n = lax.axis_size("tile") // stride
    to = [((q - odd) ^ 1) + odd for q in range(n)]
    to = [q if 0 <= q < n else k for k, q in enumerate(to)]
    return lax.ppermute(x, "tile", [(q * stride + i, to[q] * stride + i) for q in range(n) for i in range(stride)])


def tables(s):
    p = np.arange(s.we)
    at = p // 4 + np.where(p >= s.wc + HX, s.w1 - s.we // 4, 0)
    down = at[:, None] == np.arange(s.w1)[None, :]
    q = np.arange(s.w1)
    k = q // 4 + np.where(q >= s.w1 - HX // 4, LN - s.w1 // 4, 0)
    used = (q < s.c1 + HX // 4) | (q >= s.w1 - HX // 4)
    spread2 = (np.arange(LN)[:, None] == k[None, :]) & used[None, :]
    r = np.arange(LN)
    down2 = (r // 4)[:, None] == (r % s.c2)[None, :]
    return [jnp.asarray(m, BF16) for m in (down.T, spread2, down2 * 0.25)]


def local(s, source_heating, material_thermal_values, layer_material, via_conductance, via_blocks):
    spread1, spread2, down2 = tables(s)
    down = pl.pallas_call(
        functools.partial(down_kernel, s),
        name="down",
        out_shape=jax.ShapeDtypeStruct((s.we, s.w1), BF16),
        compiler_params=pltpu.CompilerParams(vmem_limit_bytes=4 << 20),
        cost_estimate=pl.CostEstimate(flops=1 << 20, bytes_accessed=1 << 20, transcendentals=0),
    )()
    smem, packed = pltpu.SMEM, (s.part + 8, LN)
    sends = call(
        "pack", pack_kernel, s, [packed] * s.nd,
        [
            smem(material_thermal_values.shape, F32), smem(layer_material.shape, jnp.int32),
            smem((1, 1), F32), pltpu.VMEM((4, s.nb), jnp.int32),
            pltpu.VMEM(source_heating.shape, F32), pltpu.SemaphoreType.DMA((5,)),
        ],
        from_hbm=True, in_vmem=True, limit=VMEM - 4 * s.nd * packed[0] * packed[1],
    )(material_thermal_values, layer_material, via_conductance[None], via_blocks[0].T, source_heating)
    parts = [sends[0]] + [shift(sends[k], "die", k) for k in range(1, s.nd)]
    half = (s.nz * s.j0, HY, LN)
    one, two, prm = call("assemble", assemble_kernel, s, [half, half, (s.nd, 8, LN)])(*parts)
    f0, f1, small = (s.j0, s.re, LN), (s.j1, s.e1, LN), (s.nz, s.j1, s.r1, LN)
    fine, fine_v = (s.nz, *f0), (s.nz + 2, *f0)
    mid, mid_v = (s.nz, *f1), (s.nz + 2, *f1)
    slab, table = (s.nd * s.lz, s.nt, LN), (s.nz, 8, LN)
    up0, down0, e0, c, ic, cu, cd = call(
        "coeff_fine", coeff_fine_kernel, s, [(s.nd, *f0), (s.nd, *f0), fine, table, table, table, table]
    )(prm)
    flat, rbuf = (s.nz, s.r1, s.we), (s.nz * s.j0 * s.re, LN)
    r1, fore, aft = call("fine_own", fine_own_kernel, s, [small, table, table], [fine, fine_v, fine_v, rbuf, flat])(
        one, two, up0, down0, e0, ic, cu, cd, down
    )
    up1, down1, e1, u2, l2, e2 = call(
        "coeff_coarse", coeff_coarse_kernel, s, [(s.nd, *f1), (s.nd, *f1), mid, slab, slab, slab]
    )(prm)

    def middle_first(r1, *far):
        return call(
            "middle_first", middle_first_kernel, s,
            [mid, mid_v, (s.nd * s.nt * s.lz, LN)], [mid_v, (s.nz * 8, LN)],
        )(swap(r1, 0), r1, swap(r1, 1), up1, down1, e1, cu, cd, down2, *far)

    def everywhere(send):
        return lax.all_to_all(send, ("die", "tile"), 0, 0, tiled=True)

    spaces = [(s.nd * s.lz, s.nt + 2 * HY, LN), (s.nz * 8, LN), (s.nz, 8, s.w1), mid_v, mid_v]
    spaces += [fine_v, fine_v, flat]
    from_one, from_two = swap(one, 0), swap(two, 1)
    rx, w2, send = middle_first(r1, swap(fore, 0, 2), swap(aft, 1, 2))
    from_one, from_two, send = lax.optimization_barrier((from_one, from_two, send))
    levels = (u2, l2, e2, up1, down1, e1, up0, down0, e0)
    f, v, r1 = call("back", back_kernel, s, [fine, fine_v, small], spaces + [rbuf])(
        everywhere(send), from_one, from_two, one, two, w2, rx,
        *levels, ic, cu, cd, spread2, spread1, down,
    )
    rx, w2, send = middle_first(r1)
    piece = (2, s.lz, s.rows, s.wc)
    sends = call(
        "last", last_kernel, s, [piece] * s.nd, spaces + [(s.nz * (s.j0 - 1) * s.rows, LN)]
    )(everywhere(send), w2, rx, v, f, *levels, c, cu, cd, spread2, spread1)
    parts = [sends[0]] + [shift(sends[k], "die", k) for k in range(1, s.nd)]
    whole = (s.lz, s.rows, s.width)
    return tuple(call("unpack", unpack_kernel, s, [whole] * 2, [pltpu.SemaphoreType.DMA((2 * s.nd,))], True)(*parts))


def solution(mesh):
    in_specs = (P("die", "tile", None), P(), P("die"), P("die"), P("die", None, None))
    out_specs = (P("die", "tile", None), P("die", "tile", None))

    def body(f, mat, material, conductance, blocks):
        s = Sizes(mesh.shape, f.shape, blocks.shape[1])
        return local(s, f, mat, material, conductance, blocks)

    return jax.shard_map(body, mesh=mesh, in_specs=in_specs, out_specs=out_specs, check_vma=False)
```

```python
import functools

import jax
import jax.numpy as jnp
import numpy as np
from jax import lax
from jax.experimental import pallas as pl
from jax.experimental.pallas import tpu as pltpu
from jax.sharding import PartitionSpec as P


OMEGA = 0.8
NC = 6
LN = 128
HX = 64
VMEM = 67_043_328
HY = 8
F32 = jnp.float32
BF16 = jnp.bfloat16


def iota(shape, axis):
    return lax.broadcasted_iota(jnp.int32, shape, axis)


def split_dot(x, m):
    hi = x.astype(BF16)
    lo = (x - hi.astype(F32)).astype(BF16)
    return jnp.dot(hi, m, preferred_element_type=F32) + jnp.dot(lo, m, preferred_element_type=F32)


def pair_dot(a, b):
    return lax.dot_general(a, b, (((0,), (0,)), ((), ())), preferred_element_type=F32)


class Sizes:
    def __init__(self, mesh_shape, f_shape, n_blocks):
        self.nd, self.nt = mesh_shape["die"], mesh_shape["tile"]
        self.lz, self.rows, self.width = f_shape
        self.nb = n_blocks
        self.wc = self.width // self.nd
        self.we = self.wc + LN
        self.j0 = self.we // LN
        self.nz = self.nd * self.lz
        self.re = self.rows + 2 * HY
        self.own1 = self.rows // 4
        self.r1 = self.re // 4
        self.c1 = self.wc // 4
        self.e1 = 2 * self.r1
        self.pad1 = (self.e1 - self.own1) // 2
        self.j1 = 2
        self.w1 = self.j1 * LN
        self.c2 = self.wc // 16
        self.part = self.lz * self.j0 * self.rows
        assert self.rows == 16 and self.lz == 4 and self.c1 == LN
        assert self.nd * self.c2 == LN and self.nb <= LN and self.nt <= LN and self.nt % 8 == 0


def place():
    return lax.axis_index("die"), lax.axis_index("tile")


def even(stride):
    _, t = place()
    return lax.rem(t // stride, 2) == 0


def tiles(j):
    return slice(j * LN, (j + 1) * LN)


def windows(lo, hi):
    return [min(r, hi - 8) for r in range(lo, hi, 8)]


def pack_kernel(s, mat_h, material_h, conductance_h, blocks_h, f_h, *refs):
    outs, (one, two), (mat, material, conductance, blocks, f, sem) = refs[: s.nd], refs[s.nd : -6], refs[-6:]
    pairs = [(f_h, f), (mat_h, mat), (material_h, material), (conductance_h, conductance), (blocks_h, blocks)]
    copies = [pltpu.make_async_copy(a, b, sem.at[k]) for k, (a, b) in enumerate(pairs)]
    for c in copies:
        c.start()
    for c in copies[1:]:
        c.wait()
    lane, sub = iota((8, LN), 1), iota((8, LN), 0)
    info = jnp.where((sub == 5) & (lane == 0), conductance[0, 0], 0.0)
    for z in range(s.lz):
        info = jnp.where((sub == 4) & (lane == z), mat[material[z]], info)
    for out in outs:
        out[s.part :, :] = info
        out[s.part : s.part + 4, : s.nb] = blocks[...].astype(F32)
    copies[0].wait()
    for step, out in enumerate(outs):
        spread_columns(s, step, out, lambda z, at: f[z, :, pl.ds(at, LN)])
    lower = even(1)
    for z in range(s.lz):
        for j in range(s.width // LN):
            top, bot = f[z, :HY, tiles(j)], f[z, s.rows - HY :, tiles(j)]
            one[z, :, tiles(j)] = jnp.where(lower, bot, top)
            two[z, :, tiles(j)] = jnp.where(lower, top, bot)


def spread_columns(s, step, out, column):
    d, _ = place()
    low = iota((s.rows, LN), 1) < HX
    e = lax.rem(d + step, s.nd)
    right = lax.rem(e + 1, s.nd) * s.wc
    left = lax.rem(e + s.nd - 1, s.nd) * s.wc + (s.wc - LN)
    tile = lambda z, at: column(z, pl.multiple_of(at, LN))
    for z in range(s.lz):
        for j in range(s.j0):
            at = (z * s.j0 + j) * s.rows
            if j < s.j0 - 1:
                x = tile(z, e * s.wc + j * LN)
            else:
                x = jnp.where(low, tile(z, right), tile(z, left))
            out[at : at + s.rows, :] = x


def assemble_kernel(s, from_one, from_two, *refs):
    parts, outs, (own, prm) = refs[: s.nd], refs[s.nd : -2], refs[-2:]
    d, _ = place()
    n = s.lz * s.j0
    lower = even(1)

    def column(z, at):
        a, b = from_one[z, :, pl.ds(at, LN)], from_two[z, :, pl.ds(at, LN)]
        return jnp.concatenate([jnp.where(lower, b, a), jnp.where(lower, a, b)], axis=0)

    for step, out in enumerate(outs):
        spread_columns(s, step, out, column)
    for step, part in enumerate(parts):
        e = lax.rem(d + s.nd - step, s.nd)
        for q in range(n):
            own[n * e + q] = part[q * s.rows : (q + 1) * s.rows, :]
        prm[e] = part[s.part :, :]


def overlap(lo, size, first, past):
    return jnp.maximum(jnp.minimum(lo + size, past) - jnp.maximum(lo, first), 0.0)


def die_values(s, prm):
    lane8, sub8 = iota((8, LN), 1), iota((8, LN), 0)

    def pick(tile, row, col):
        return jnp.sum(jnp.where((lane8 == col) & (sub8 == row), tile, 0.0), keepdims=True)

    info = [prm[g] for g in range(s.nd)]
    cond = [pick(info[z // s.lz], 4, z % s.lz) for z in range(s.nz)]
    via = [pick(info[g], 5, 0) for g in range(s.nd)]
    vert = [2.0 * p * q / (p + q) for p, q in zip(cond, cond[1:] + cond[-1:])]
    blocks = []
    for g in range(s.nd):
        b = jnp.transpose(info[g])
        lane = iota((LN, 8), 1)
        col = [jnp.sum(jnp.where(lane == k, b, 0.0), axis=1, keepdims=True) for k in range(4)]
        col = [x[: s.nb] for x in col]
        blocks.append((col[0], col[0] + col[2], col[1], col[1] + col[3]))
    return cond, vert, via, blocks


def level_coeffs(s, level, values, via_up, via_down, scale):
    cond, vert, via, blocks = values
    d, t = place()
    size = 4**level
    n, own = (s.we, s.wc) if level == 0 else (s.w1, s.c1)
    height, nj = (s.re, s.j0) if level == 0 else (s.e1, s.j1)
    pad = HY if level == 0 else s.pad1
    halo = HX // size

    def columns(shape, axis):
        p = iota(shape, axis)
        return p, d * own + jnp.where(p >= n - halo, p - n, p)

    first = t * (s.rows // size) - pad
    row = ((first + iota((1, LN), 1)) * size).astype(F32)
    col = (columns((1, n), 1)[1] * size).astype(F32)
    rr = first + iota((height, n), 0)
    pp, cc = columns((height, n), 1)
    inside = (rr >= 0) & (rr < s.rows * s.nt // size) & (cc >= 0) & (cc < s.width // size)
    inside = jnp.where(inside & ((pp < own + halo) | (pp >= n - halo)), OMEGA, 0.0)
    via_down[0] = jnp.zeros(via_down.shape[1:], F32)
    for g in range(s.nd):
        r0, r1, c0, c1 = blocks[g]
        m = pair_dot(
            overlap(row, float(size), r0, r1).astype(BF16), overlap(col, float(size), c0, c1).astype(BF16)
        )[:height]
        top = (g + 1) * s.lz - 1
        m = m * (via[g] * (0.25**level))
        for j in range(nj):
            via_up[g, j] = m[:, tiles(j)] / cond[top]
            if g + 1 < s.nd:
                via_down[g + 1, j] = m[:, tiles(j)] / cond[top + 1]
    for z in range(s.nz):
        g, a = z // s.lz, z % s.lz
        const = 4.0
        if a < s.lz - 1:
            const = const + vert[z] * (4.0**level) / cond[z]
        if a > 0:
            const = const + vert[z - 1] * (4.0**level) / cond[z]
        for j in range(nj):
            diag = const
            if a == s.lz - 1:
                diag = diag + via_up[g, j]
            if a == 0:
                diag = diag + via_down[g, j]
            scale[z, j] = inside[:, tiles(j)] / diag


def coeff_fine_kernel(s, prm, up0, down0, e0, c, ic, cu, cd):
    values = die_values(s, prm)
    cond, vert = values[:2]
    for z in range(s.nz):
        c[z] = jnp.zeros((8, LN), F32) + cond[z]
        ic[z] = jnp.zeros((8, LN), F32) + 1.0 / cond[z]
        cu[z] = jnp.zeros((8, LN), F32) + vert[z] / cond[z]
        cd[z] = jnp.zeros((8, LN), F32) + vert[max(z - 1, 0)] / cond[z]
    level_coeffs(s, 0, values, up0, down0, e0)


def coeff_coarse_kernel(s, prm, up1, down1, e1, u2, l2, e2):
    values = die_values(s, prm)
    cond, vert, via, blocks = values
    level_coeffs(s, 1, values, up1, down1, e1)
    group = iota((1, LN), 1) // s.c2
    xin = iota((1, LN), 1) % s.c2

    def by_group(values):
        out = jnp.zeros((1, LN), F32)
        for g in range(s.nd):
            out = jnp.where(group == g, values[g], out)
        return out

    cl = [by_group([cond[s.lz * g + a] for g in range(s.nd)]) * 16.0 for a in range(s.lz)]
    vl = [by_group([vert[s.lz * g + a] for g in range(s.nd)]) * 256.0 for a in range(s.lz)]
    vial = by_group(via)
    row2 = (iota((1, LN), 1) * 16).astype(F32)
    ra = jnp.concatenate([overlap(row2, 16.0, b[0], b[1]) for b in blocks], axis=0).astype(BF16)
    zero2 = jnp.zeros((s.nt, LN), F32)
    for e in range(s.nd):
        col2 = ((e * s.c2 + xin) * 16).astype(F32)
        cb = jnp.concatenate(
            [jnp.where(group == g, overlap(col2, 16.0, b[2], b[3]), 0.0) for g, b in enumerate(blocks)],
            axis=0,
        ).astype(BF16)
        v2 = pair_dot(ra, cb)[: s.nt] * vial
        ups = [zero2 + vl[a] for a in range(s.lz - 1)] + [v2]
        first = jnp.where(iota((s.nt, LN), 1) >= s.c2, pltpu.roll(v2, s.c2, 1), 0.0)
        lows = [first] + ups[:-1]
        for a in range(s.lz):
            q = e * s.lz + a
            u2[q] = ups[a] / cl[a]
            l2[q] = lows[a] / cl[a]
            e2[q] = OMEGA * cl[a] / (4.0 * cl[a] + ups[a] + lows[a])


class Level:
    def __init__(self, s, level, up, down, scale, cu, cd):
        self.s, self.up, self.down, self.scale, self.cu, self.cd = s, up, down, scale, cu, cd
        self.nj = (s.j0, s.j1)[level]
        self.us = 4.0**level

    def walk(self, src, f, lo, hi, emit, count=None):
        s, n = self.s, self.nj
        lane = iota((8, LN), 1)
        first, last = lane == 0, lane == LN - 1

        def group(g, carry):
            for a in range(s.lz):
                z = g * s.lz + a
                for r in windows(lo, hi):
                    rows = pl.ds(r, 8)
                    v = [src[z + 1, j, rows, :] for j in range(n)]
                    ahead = [pltpu.roll(x, LN - 1, 1) for x in v]
                    behind = [pltpu.roll(x, 1, 1) for x in v]
                    for j in range(count or n):
                        k_up = self.cu[z] * self.us if a < s.lz - 1 else self.up[g, j, rows, :]
                        k_down = self.cd[z] * self.us if a > 0 else self.down[g, j, rows, :]
                        x = jnp.where(last, ahead[(j + 1) % n], ahead[j]) + jnp.where(first, behind[j - 1], behind[j])
                        y = src[z + 1, j, pl.ds(r - 1, 8), :] + src[z + 1, j, pl.ds(r + 1, 8), :]
                        x = (f[z, j, rows, :] + x) + y
                        x = x + (k_up * src[z + 2, j, rows, :] + k_down * src[z, j, rows, :])
                        emit(z, j, rows, v[j], x, k_up, k_down)
            return carry

        lax.fori_loop(0, s.nd, group, 0)

    def sweep(self, src, dst, f, lo, hi):
        def emit(z, j, rows, v, g, *_):
            dst[z + 1, j, rows, :] = (1.0 - OMEGA) * v + self.scale[z, j, rows, :] * g

        self.walk(src, f, lo, hi, emit)

    def residual(self, src, f, lo, hi, put, count=None):
        def emit(z, j, rows, v, g, k_up, k_down):
            put(z, j, rows, g - (4.0 + k_up + k_down) * v)

        self.walk(src, f, lo, hi, emit, count)


def zero_ends(s, *bufs):
    for b in bufs:
        b[0] = jnp.zeros(b.shape[1:], F32)
        b[s.nz + 1] = jnp.zeros(b.shape[1:], F32)


def restrict(s, level, src, f, lo, hi, down, rbuf, sums, r1):
    for k in range(s.nz * s.j0):
        rbuf[k * s.re : k * s.re + 8, :] = jnp.zeros((8, LN), F32)
        rbuf[(k + 1) * s.re - 8 : (k + 1) * s.re, :] = jnp.zeros((8, LN), F32)

    def put(z, j, rows, x):
        rbuf[pl.ds((z * s.j0 + j) * s.re + rows.start, 8), :] = x

    level.residual(src, f, lo, hi, put)

    def body(z, carry):
        for j in range(s.j0):
            part = [rbuf[pl.ds((z * s.j0 + j) * s.re + k, s.r1, stride=4), :] for k in range(4)]
            sums[z, :, tiles(j)] = (part[0] + part[1]) + (part[2] + part[3])
        return carry

    lax.fori_loop(0, s.nz, body, 0)
    out = split_dot(sums[...].reshape(s.nz * s.r1, s.we), down[...])
    for z in range(s.nz):
        for j in range(s.j1):
            r1[z, j] = out[z * s.r1 : (z + 1) * s.r1, tiles(j)]


def down_kernel(s, out):
    p, q = iota((s.we, s.w1), 0), iota((s.we, s.w1), 1)
    at = p // 4 + jnp.where(p >= s.wc + HX, s.w1 - s.we // 4, 0)
    out[...] = jnp.where(at == q, 0.25, 0.0).astype(BF16)


def fine_own_kernel(s, own, up0, down0, e0, ic, cu, cd, down, r1, fore, aft, f, va, vb, rbuf, sums):
    level = Level(s, 0, up0, down0, e0, cu, cd)
    zero_ends(s, va, vb)
    zero = jnp.zeros((8, LN), F32)

    def body(z, carry):
        for k in range(s.re // 8):
            rows = slice(8 * k, 8 * k + 8)
            for j in range(s.j0):
                if HY <= 8 * k < HY + s.rows:
                    x = own[z * s.j0 + j, 8 * k - HY : 8 * k - HY + 8, :] * ic[z]
                    f[z, j, rows, :] = x
                    va[z + 1, j, rows, :] = e0[z, j, rows, :] * x
                else:
                    f[z, j, rows, :] = zero
                    va[z + 1, j, rows, :] = zero
                    vb[z + 1, j, rows, :] = zero
        return carry

    lax.fori_loop(0, s.nz, body, 0)
    level.sweep(va, vb, f, HY - 1, HY + s.rows + 1)
    restrict(s, level, vb, f, HY - 2, HY + s.rows + 2, down, rbuf, sums, r1)
    ahead = even(2)
    low = iota((s.r1, LN), 0) < s.r1 // 2

    def halves(z, carry):
        a, b = r1[z, 0], r1[z, 1]
        x = jnp.where(low, pltpu.roll(a, s.r1 // 2, 0), b)
        y = jnp.where(low, a, pltpu.roll(b, s.r1 // 2, 0))
        fore[z] = jnp.where(ahead, x, y)
        aft[z] = jnp.where(ahead, y, x)
        return carry

    lax.fori_loop(0, s.nz, halves, 0)


def middle_first_kernel(s, r1a, r1, r1b, up1, down1, e1, cu, cd, down2, *refs):
    far, (rx, w2, send, wa, buf) = refs[:-5], refs[-5:]
    level = Level(s, 1, up1, down1, e1, cu, cd)
    half, own, pad = s.r1, s.own1, s.pad1
    sub = iota((half, LN), 0)
    _, t = place()
    lower, ahead = even(1), even(2)
    from_p, from_n = (t >= 1).astype(F32), (t < s.nt - 1).astype(F32)
    from_pp, from_nn = (t >= 2).astype(F32), (t < s.nt - 2).astype(F32)
    zero_ends(s, wa, w2)

    def body(z, carry):
        for j in range(s.j1):
            mid = pltpu.roll(r1[z, j], half // 2, 0)
            up = from_p * jnp.where(lower, r1b[z, j], r1a[z, j]) + jnp.where(sub >= half // 2, mid, 0.0)
            down = from_n * jnp.where(lower, r1a[z, j], r1b[z, j]) + jnp.where(sub < half // 2, mid, 0.0)
            if far:
                a, b = far[0][z], far[1][z]
                fore, aft = jnp.where(ahead, b, a), jnp.where(ahead, a, b)
                fore = pltpu.roll(fore, half // 2, 0) if j == 1 else fore
                aft = pltpu.roll(aft, half // 2, 0) if j == 0 else aft
                up += from_pp * jnp.where(sub < half // 2, fore, 0.0)
                down += from_nn * jnp.where(sub >= half // 2, aft, 0.0)
            rx[z, j, :half, :] = up
            rx[z, j, half:, :] = down
            wa[z + 1, j, :half, :] = e1[z, j, :half, :] * up
            wa[z + 1, j, half:, :] = e1[z, j, half:, :] * down
        return carry

    lax.fori_loop(0, s.nz, body, 0)
    level.sweep(wa, w2, rx, pad - 4, pad + own + 4)

    def put(z, j, rows, x):
        buf[pl.ds(pl.multiple_of(z * 8, 8), 8), :] = x

    level.residual(w2, rx, pad - 2, pad + own + 2, put, 1)
    sub8, group = iota((8, LN), 0), iota((8, LN), 1) // s.c2
    tile = jnp.zeros((8, LN), F32)
    for h in range(s.nz // 8):
        part = [buf[pl.ds(64 * h + 2 + k, 8, stride=8), :] for k in range(own)]
        x = split_dot((part[0] + part[1]) + (part[2] + part[3]), down2[...])
        y = pltpu.roll(x, 4, 0)
        for g in (2 * h, 2 * h + 1):
            tile = jnp.where(group == g, jnp.where((sub8 < 4) == (g % 2 == 0), x, y), tile)
    for k in range(s.nd * s.nt * s.lz // 8):
        send[8 * k : 8 * k + 8, :] = tile


def coarse(s, got, u2, l2, e2, cs):
    lane = iota((s.nt, LN), 1)
    x, t = lane % s.c2, iota((s.nt, LN), 0)
    first_x, last_x = x == 0, x == s.c2 - 1
    slabs = s.nd * s.lz
    rhs, v = [], []
    for q in range(slabs):
        e, a = q // s.lz, q % s.lz
        r = got[pl.ds(e * s.nt * s.lz + a, s.nt, stride=s.lz), :]
        rhs.append(r)
        v.append(e2[q] * r)
    zero = jnp.zeros((s.nt, LN), F32)

    def body(_, v):
        new = []
        for q in range(slabs):
            e, a = q // s.lz, q % s.lz
            w = v[q]
            right = pltpu.roll(v[q + s.lz], s.c2 - 1, 1) if e < s.nd - 1 else zero
            left = pltpu.roll(v[q - s.lz], LN - (s.c2 - 1), 1) if e > 0 else zero
            side = jnp.where(last_x, right, pltpu.roll(w, LN - 1, 1))
            side += jnp.where(first_x, left, pltpu.roll(w, 1, 1))
            side += jnp.where(t == s.nt - 1, 0.0, pltpu.roll(w, s.nt - 1, 0))
            side += jnp.where(t == 0, 0.0, pltpu.roll(w, 1, 0))
            if a < s.lz - 1:
                up = v[q + 1]
            else:
                up = jnp.where(lane >= LN - s.c2, 0.0, pltpu.roll(v[q - a], LN - s.c2, 1))
            if a > 0:
                down = v[q - 1]
            else:
                down = jnp.where(lane < s.c2, 0.0, pltpu.roll(v[q + s.lz - 1], s.c2, 1))
            g = (rhs[q] + side) + (u2[q] * up + l2[q] * down)
            new.append((1.0 - OMEGA) * w + e2[q] * g)
        return tuple(new)

    v = lax.fori_loop(0, NC - 1, body, tuple(v))
    for q in range(slabs):
        cs[q, :HY, :] = jnp.zeros((HY, LN), F32)
        cs[q, HY + s.nt :, :] = jnp.zeros((HY, LN), F32)
        cs[q, HY : HY + s.nt, :] = v[q]


def middle_last(s, level, cs, spread2, w2, rx, comp, wide, wa, wb):
    d, t = place()
    lane, upper = iota((8, LN), 1), iota((8, LN), 0) < 4
    after = lax.rem(d + 1, s.nd) * s.lz
    before = lax.rem(d + s.nd - 1, s.nd) * s.lz
    zero_ends(s, wa, wb)
    for a in range(s.lz):
        rows = [cs[base + a, pl.ds(HY - 1 + t, 8), :] for base in (d * s.lz, after, before)]
        for g in range(s.nd):
            turn = []
            for r, by in zip(rows, (0, s.c2, LN - s.c2)):
                by = (by - g * s.c2) % LN
                turn.append(pltpu.roll(r, by, 1) if by else r)
            z = g * s.lz + a
            comp[8 * z : 8 * z + 8, :] = jnp.where(
                lane < s.c2, turn[0], jnp.where(lane < LN // 2, turn[1], turn[2])
            )
    wide[...] = split_dot(comp[...], spread2[...]).reshape(wide.shape)

    def body(z, carry):
        x = [[wide[z, k : k + 1, tiles(j)] for k in range(3)] for j in range(s.j1)]
        for k in range(2):
            rows = slice(s.pad1 - 4 + 4 * k, s.pad1 + 4 + 4 * k)
            for j in range(s.j1):
                y = w2[z + 1, j, rows, :] + jnp.where(upper, x[j][k], x[j][k + 1])
                wa[z + 1, j, rows, :] = jnp.where(level.scale[z, j, rows, :] > 0.0, y, 0.0)
        return carry

    lax.fori_loop(0, s.nz, body, 0)
    level.sweep(wa, wb, rx, s.pad1 - 3, s.pad1 + s.own1 + 3)
    level.sweep(wb, wa, rx, s.pad1 - 2, s.pad1 + s.own1 + 2)


def correct_fine(s, w, v, spread1, wide, dst):
    rows = slice(s.pad1 - 2, s.pad1 + s.own1 + 2)
    lhs = jnp.concatenate([w[1 : s.nz + 1, j, rows, :].reshape(s.nz * s.r1, LN) for j in range(s.j1)], axis=1)
    wide[...] = split_dot(lhs, spread1[...]).reshape(wide.shape)
    upper = iota((8, LN), 0) < 4

    def body(z, carry):
        for k in range(s.r1 // 2):
            rows = slice(8 * k, 8 * k + 8)
            for j in range(s.j0):
                x = [wide[z, 2 * k + i : 2 * k + i + 1, tiles(j)] for i in range(2)]
                dst[z + 1, j, rows, :] = v[z + 1, j, rows, :] + jnp.where(upper, x[0], x[1])
        return carry

    lax.fori_loop(0, s.nz, body, 0)


def back_kernel(
    s, got, own, w2, rx, u2, l2, e2, up1, down1, e1, up0, down0, e0, ic, cu, cd, spread2, spread1, down, *refs
):
    parts, refs = refs[: s.nd], refs[s.nd :]
    f, v, r1, cs, comp, wide2, wa, wb, va, vb, wide, rbuf = refs
    fine = Level(s, 0, up0, down0, e0, cu, cd)
    middle = Level(s, 1, up1, down1, e1, cu, cd)
    zero_ends(s, va, vb, v)
    d, _ = place()

    def put(z, j, rows, x):
        x = x * ic[z, 0:1, :]
        f[z, j, rows, :] = x
        va[z + 1, j, rows, :] = e0[z, j, rows, :] * x

    def body(z, carry):
        for j in range(s.j0):
            put(z, j, slice(HY, HY + s.rows), own[z * s.j0 + j])
        return carry

    lax.fori_loop(0, s.nz, body, 0)
    for step, part in enumerate(parts):
        e = lax.rem(d + s.nd - step, s.nd)
        for a in range(s.lz):
            for j in range(s.j0):
                at = (a * s.j0 + j) * s.rows
                put(e * s.lz + a, j, slice(0, HY), part[at : at + HY, :])
                put(e * s.lz + a, j, slice(s.re - HY, s.re), part[at + HY : at + 2 * HY, :])
    fine.sweep(va, vb, f, 1, s.re - 1)
    coarse(s, got, u2, l2, e2, cs)
    middle_last(s, middle, cs, spread2, w2, rx, comp, wide2, wa, wb)
    correct_fine(s, wa, vb, spread1, wide, va)
    fine.sweep(va, vb, f, 2, s.re - 2)
    fine.sweep(vb, va, f, 3, s.re - 3)
    fine.sweep(va, vb, f, 4, s.re - 4)
    fine.sweep(vb, v, f, 5, s.re - 5)
    restrict(s, fine, v, f, HY, HY + s.rows, down, rbuf, wide, r1)


def last_kernel(
    s, got, w2, rx, v2, f, u2, l2, e2, up1, down1, e1, up0, down0, e0, c, cu, cd, spread2, spread1, *refs,
):
    outs, (cs, comp, wide2, wa, wb, va, vb, wide, rbuf) = refs[: s.nd], refs[s.nd :]
    fine = Level(s, 0, up0, down0, e0, cu, cd)
    middle = Level(s, 1, up1, down1, e1, cu, cd)
    d, _ = place()
    zero_ends(s, va, vb)
    coarse(s, got, u2, l2, e2, cs)
    middle_last(s, middle, cs, spread2, w2, rx, comp, wide2, wa, wb)
    correct_fine(s, wa, v2, spread1, wide, va)
    fine.sweep(va, vb, f, HY - 2, HY + s.rows + 2)
    fine.sweep(vb, va, f, HY - 1, HY + s.rows + 1)

    def put(z, j, rows, x):
        at = (z * (s.j0 - 1) + j) * s.rows + rows.start - HY
        rbuf[pl.ds(pl.multiple_of(at, 8), 8), :] = x * c[z]

    fine.residual(va, f, HY, HY + s.rows, put, s.j0 - 1)
    for step, out in enumerate(outs):
        e = lax.rem(d + step, s.nd)
        for a in range(s.lz):
            z = e * s.lz + a
            for j in range(s.j0 - 1):
                out[0, a, :, tiles(j)] = va[z + 1, j, HY : HY + s.rows, :]
                at = pl.multiple_of((z * (s.j0 - 1) + j) * s.rows, 8)
                out[1, a, :, tiles(j)] = rbuf[pl.ds(at, s.rows), :]


def unpack_kernel(s, *refs):
    parts, outs, sem = refs[: s.nd], refs[s.nd : -1], refs[-1]
    d, _ = place()
    copies = []
    for step, part in enumerate(parts):
        e = lax.rem(d + s.nd - step, s.nd)
        cols = pl.ds(pl.multiple_of(e * s.wc, LN), s.wc)
        for k, out in enumerate(outs):
            copies.append(pltpu.make_async_copy(part.at[k], out.at[:, :, cols], sem.at[len(outs) * step + k]))
    for c in copies:
        c.start()
    for c in copies:
        c.wait()


def call(kernel, s, outs, scratch=(), to_hbm=False, from_hbm=False, in_vmem=False, limit=32 << 20):
    shapes = [pltpu.VMEM(o, F32) if in_vmem else jax.ShapeDtypeStruct(o, F32) for o in outs]
    spaces = [pl.BlockSpec(memory_space=m) for m in (pltpu.VMEM, pltpu.HBM)]

    def run(*args):
        total = sum(int(np.prod(a.shape)) * 4 for a in args) + sum(int(np.prod(o)) * 4 for o in outs)
        return pl.pallas_call(
            functools.partial(kernel, s),
            out_shape=shapes,
            in_specs=[spaces[from_hbm]] * len(args),
            out_specs=[spaces[to_hbm]] * len(outs),
            scratch_shapes=[pltpu.VMEM(x, F32) if isinstance(x, tuple) else x for x in scratch],
            compiler_params=pltpu.CompilerParams(vmem_limit_bytes=limit),
            cost_estimate=pl.CostEstimate(flops=4 * total, bytes_accessed=total, transcendentals=0),
        )(*args)

    return run


def shift(x, axis, by):
    n = lax.axis_size(axis)
    return lax.ppermute(x, axis, [(i, (i + by) % n) for i in range(n)])


def swap(x, odd, stride=1):
    n = lax.axis_size("tile") // stride
    to = [((q - odd) ^ 1) + odd for q in range(n)]
    to = [q if 0 <= q < n else k for k, q in enumerate(to)]
    return lax.ppermute(x, "tile", [(q * stride + i, to[q] * stride + i) for q in range(n) for i in range(stride)])


def tables(s):
    p = np.arange(s.we)
    at = p // 4 + np.where(p >= s.wc + HX, s.w1 - s.we // 4, 0)
    down = at[:, None] == np.arange(s.w1)[None, :]
    q = np.arange(s.w1)
    k = q // 4 + np.where(q >= s.w1 - HX // 4, LN - s.w1 // 4, 0)
    used = (q < s.c1 + HX // 4) | (q >= s.w1 - HX // 4)
    spread2 = (np.arange(LN)[:, None] == k[None, :]) & used[None, :]
    r = np.arange(LN)
    down2 = (r // 4)[:, None] == (r % s.c2)[None, :]
    return [jnp.asarray(m, BF16) for m in (down.T, spread2, down2 * 0.25)]


def local(s, source_heating, material_thermal_values, layer_material, via_conductance, via_blocks):
    spread1, spread2, down2 = tables(s)
    down = pl.pallas_call(
        functools.partial(down_kernel, s),
        name="down",
        out_shape=jax.ShapeDtypeStruct((s.we, s.w1), BF16),
        compiler_params=pltpu.CompilerParams(vmem_limit_bytes=4 << 20),
        cost_estimate=pl.CostEstimate(flops=1 << 20, bytes_accessed=1 << 20, transcendentals=0),
    )()
    smem, packed, edge = pltpu.SMEM, (s.part + 8, LN), (s.lz, HY, s.width)
    *sends, one, two = call(
        pack_kernel, s, [packed] * s.nd + [edge] * 2,
        [
            smem(material_thermal_values.shape, F32), smem(layer_material.shape, jnp.int32),
            smem((1, 1), F32), pltpu.VMEM((4, s.nb), jnp.int32),
            pltpu.VMEM(source_heating.shape, F32), pltpu.SemaphoreType.DMA((5,)),
        ],
        from_hbm=True, in_vmem=True, limit=VMEM - 4 * (s.nd * packed[0] * packed[1] + 2 * s.lz * HY * s.width),
    )(material_thermal_values, layer_material, via_conductance[None], via_blocks[0].T, source_heating)
    parts = [sends[0]] + [shift(sends[k], "die", k) for k in range(1, s.nd)]
    from_one, from_two = swap(one, 0), swap(two, 1)
    piece = (s.part, LN)
    *sends, own, prm = call(
        assemble_kernel, s, [piece] * s.nd + [(s.nz * s.j0, s.rows, LN), (s.nd, 8, LN)]
    )(from_one, from_two, *parts)
    parts = [sends[0]] + [shift(sends[k], "die", k) for k in range(1, s.nd)]
    f0, f1, small = (s.j0, s.re, LN), (s.j1, s.e1, LN), (s.nz, s.j1, s.r1, LN)
    fine, fine_v = (s.nz, *f0), (s.nz + 2, *f0)
    mid, mid_v = (s.nz, *f1), (s.nz + 2, *f1)
    slab, table = (s.nd * s.lz, s.nt, LN), (s.nz, 8, LN)
    up0, down0, e0, c, ic, cu, cd = call(
        coeff_fine_kernel, s, [(s.nd, *f0), (s.nd, *f0), fine, table, table, table, table]
    )(prm)
    flat, rbuf = (s.nz, s.r1, s.we), (s.nz * s.j0 * s.re, LN)
    r1, fore, aft = call(fine_own_kernel, s, [small, table, table], [fine, fine_v, fine_v, rbuf, flat])(
        own, up0, down0, e0, ic, cu, cd, down
    )
    up1, down1, e1, u2, l2, e2 = call(coeff_coarse_kernel, s, [(s.nd, *f1), (s.nd, *f1), mid, slab, slab, slab])(prm)

    def middle_first(r1, *far):
        return call(
            middle_first_kernel, s,
            [mid, mid_v, (s.nd * s.nt * s.lz, LN)], [mid_v, (s.nz * 8, LN)],
        )(swap(r1, 0), r1, swap(r1, 1), up1, down1, e1, cu, cd, down2, *far)

    def everywhere(send):
        return lax.all_to_all(send, ("die", "tile"), 0, 0, tiled=True)

    spaces = [(s.nd * s.lz, s.nt + 2 * HY, LN), (s.nz * 8, LN), (s.nz, 8, s.w1), mid_v, mid_v]
    spaces += [fine_v, fine_v, flat]
    rx, w2, send = middle_first(r1, swap(fore, 0, 2), swap(aft, 1, 2))
    *parts, send = lax.optimization_barrier((*parts, send))
    levels = (u2, l2, e2, up1, down1, e1, up0, down0, e0)
    f, v, r1 = call(back_kernel, s, [fine, fine_v, small], spaces + [rbuf])(
        everywhere(send), own, w2, rx, *levels, ic, cu, cd, spread2, spread1, down, *parts
    )
    rx, w2, send = middle_first(r1)
    piece = (2, s.lz, s.rows, s.wc)
    sends = call(
        last_kernel, s, [piece] * s.nd, spaces + [(s.nz * (s.j0 - 1) * s.rows, LN)]
    )(everywhere(send), w2, rx, v, f, *levels, c, cu, cd, spread2, spread1)
    parts = [sends[0]] + [shift(sends[k], "die", k) for k in range(1, s.nd)]
    whole = (s.lz, s.rows, s.width)
    return tuple(call(unpack_kernel, s, [whole] * 2, [pltpu.SemaphoreType.DMA((2 * s.nd,))], True)(*parts))


def solution(mesh):
    in_specs = (P("die", "tile", None), P(), P("die"), P("die"), P("die", None, None))
    out_specs = (P("die", "tile", None), P("die", "tile", None))

    def body(f, mat, material, conductance, blocks):
        s = Sizes(mesh.shape, f.shape, blocks.shape[1])
        return local(s, f, mat, material, conductance, blocks)

    return jax.shard_map(body, mesh=mesh, in_specs=in_specs, out_specs=out_specs, check_vma=False)
```

```python
import functools

import jax
import jax.numpy as jnp
import numpy as np
from jax import lax
from jax.experimental import pallas as pl
from jax.experimental.pallas import tpu as pltpu
from jax.sharding import PartitionSpec as P

OMEGA = 0.8
NC = 6
LN = 128
HX = 64
VMEM = 67_043_328
HY = 8
F32 = jnp.float32
BF16 = jnp.bfloat16


def iota(shape, axis):
    return lax.broadcasted_iota(jnp.int32, shape, axis)


def split_dot(x, m):
    hi = x.astype(BF16)
    lo = (x - hi.astype(F32)).astype(BF16)
    return jnp.dot(hi, m, preferred_element_type=F32) + jnp.dot(lo, m, preferred_element_type=F32)


def pair_dot(a, b):
    return lax.dot_general(a, b, (((0,), (0,)), ((), ())), preferred_element_type=F32)


class Sizes:
    def __init__(self, mesh_shape, f_shape, n_blocks):
        self.nd, self.nt = mesh_shape["die"], mesh_shape["tile"]
        self.lz, self.rows, self.width = f_shape
        self.nb = n_blocks
        self.wc = self.width // self.nd
        self.we = self.wc + LN
        self.j0 = self.we // LN
        self.nz = self.nd * self.lz
        self.re = self.rows + 2 * HY
        self.own1 = self.rows // 4
        self.r1 = self.re // 4
        self.c1 = self.wc // 4
        self.e1 = 2 * self.r1
        self.pad1 = (self.e1 - self.own1) // 2
        self.j1 = 2
        self.w1 = self.j1 * LN
        self.c2 = self.wc // 16
        self.part = self.lz * self.j0 * self.rows
        assert self.rows == 16 and self.lz == 4 and self.c1 == LN
        assert self.nd * self.c2 == LN and self.nb <= LN and self.nt <= LN and self.nt % 8 == 0


def place():
    return lax.axis_index("die"), lax.axis_index("tile")


def even():
    _, t = place()
    return lax.rem(t, 2) == 0


def tiles(j):
    return slice(j * LN, (j + 1) * LN)


def windows(lo, hi):
    return [min(r, hi - 8) for r in range(lo, hi, 8)]


def pack_kernel(s, mat_h, material_h, conductance_h, blocks_h, f_h, *refs):
    outs, (mat, material, conductance, blocks, f, sem) = refs[: s.nd], refs[s.nd :]
    pairs = [(f_h, f), (mat_h, mat), (material_h, material), (conductance_h, conductance), (blocks_h, blocks)]
    copies = [pltpu.make_async_copy(a, b, sem.at[k]) for k, (a, b) in enumerate(pairs)]
    for c in copies:
        c.start()
    for c in copies[1:]:
        c.wait()
    d, _ = place()
    lane, sub = iota((8, LN), 1), iota((8, LN), 0)
    info = jnp.where((sub == 5) & (lane == 0), conductance[0, 0], 0.0)
    for z in range(s.lz):
        info = jnp.where((sub == 4) & (lane == z), mat[material[z]], info)
    for out in outs:
        out[s.part :, :] = info
        out[s.part : s.part + 4, : s.nb] = blocks[...].astype(F32)
    copies[0].wait()
    low = iota((s.rows, LN), 1) < HX
    for step, out in enumerate(outs):
        e = lax.rem(d + step, s.nd)
        right = lax.rem(e + 1, s.nd) * s.wc
        left = lax.rem(e + s.nd - 1, s.nd) * s.wc + (s.wc - LN)

        def column(z, at):
            return f[z, :, pl.ds(pl.multiple_of(at, LN), LN)]

        for z in range(s.lz):
            for j in range(s.j0):
                at = (z * s.j0 + j) * s.rows
                if j < s.j0 - 1:
                    x = column(z, e * s.wc + j * LN)
                else:
                    x = jnp.where(low, column(z, right), column(z, left))
                out[at : at + s.rows, :] = x


def assemble_kernel(s, *refs):
    parts, (one, two, prm) = refs[: s.nd], refs[s.nd :]
    d, _ = place()
    n = s.lz * s.j0
    lower = even()
    for step, part in enumerate(parts):
        e = lax.rem(d + s.nd - step, s.nd)
        for q in range(n):
            top = part[q * s.rows : q * s.rows + HY, :]
            bot = part[q * s.rows + HY : (q + 1) * s.rows, :]
            one[n * e + q] = jnp.where(lower, bot, top)
            two[n * e + q] = jnp.where(lower, top, bot)
        prm[e] = part[s.part :, :]


def overlap(lo, size, first, past):
    return jnp.maximum(jnp.minimum(lo + size, past) - jnp.maximum(lo, first), 0.0)


def die_values(s, prm):
    lane8, sub8 = iota((8, LN), 1), iota((8, LN), 0)

    def pick(tile, row, col):
        return jnp.sum(jnp.where((lane8 == col) & (sub8 == row), tile, 0.0), keepdims=True)

    info = [prm[g] for g in range(s.nd)]
    cond = [pick(info[z // s.lz], 4, z % s.lz) for z in range(s.nz)]
    via = [pick(info[g], 5, 0) for g in range(s.nd)]
    vert = [2.0 * p * q / (p + q) for p, q in zip(cond, cond[1:] + cond[-1:])]
    blocks = []
    for g in range(s.nd):
        b = jnp.transpose(info[g])
        lane = iota((LN, 8), 1)
        col = [jnp.sum(jnp.where(lane == k, b, 0.0), axis=1, keepdims=True) for k in range(4)]
        col = [x[: s.nb] for x in col]
        blocks.append((col[0], col[0] + col[2], col[1], col[1] + col[3]))
    return cond, vert, via, blocks


def level_coeffs(s, level, values, via_up, via_down, scale):
    cond, vert, via, blocks = values
    d, t = place()
    size = 4**level
    n, own = (s.we, s.wc) if level == 0 else (s.w1, s.c1)
    height, nj = (s.re, s.j0) if level == 0 else (s.e1, s.j1)
    pad = HY if level == 0 else s.pad1
    halo = HX // size

    def columns(shape, axis):
        p = iota(shape, axis)
        return p, d * own + jnp.where(p >= n - halo, p - n, p)

    first = t * (s.rows // size) - pad
    row = ((first + iota((1, LN), 1)) * size).astype(F32)
    col = (columns((1, n), 1)[1] * size).astype(F32)
    rr = first + iota((height, n), 0)
    pp, cc = columns((height, n), 1)
    inside = (rr >= 0) & (rr < s.rows * s.nt // size) & (cc >= 0) & (cc < s.width // size)
    inside = jnp.where(inside & ((pp < own + halo) | (pp >= n - halo)), OMEGA, 0.0)
    via_down[0] = jnp.zeros(via_down.shape[1:], F32)
    for g in range(s.nd):
        r0, r1, c0, c1 = blocks[g]
        m = pair_dot(
            overlap(row, float(size), r0, r1).astype(BF16), overlap(col, float(size), c0, c1).astype(BF16)
        )[:height]
        top = (g + 1) * s.lz - 1
        m = m * (via[g] * (0.25**level))
        for j in range(nj):
            via_up[g, j] = m[:, tiles(j)] / cond[top]
            if g + 1 < s.nd:
                via_down[g + 1, j] = m[:, tiles(j)] / cond[top + 1]
    for z in range(s.nz):
        g, a = z // s.lz, z % s.lz
        const = 4.0
        if a < s.lz - 1:
            const = const + vert[z] * (4.0**level) / cond[z]
        if a > 0:
            const = const + vert[z - 1] * (4.0**level) / cond[z]
        for j in range(nj):
            diag = const
            if a == s.lz - 1:
                diag = diag + via_up[g, j]
            if a == 0:
                diag = diag + via_down[g, j]
            scale[z, j] = inside[:, tiles(j)] / diag


def coeff_fine_kernel(s, prm, up0, down0, e0, c, ic, cu, cd):
    values = die_values(s, prm)
    cond, vert = values[:2]
    for z in range(s.nz):
        c[z] = jnp.zeros((8, LN), F32) + cond[z]
        ic[z] = jnp.zeros((8, LN), F32) + 1.0 / cond[z]
        cu[z] = jnp.zeros((8, LN), F32) + vert[z] / cond[z]
        cd[z] = jnp.zeros((8, LN), F32) + vert[max(z - 1, 0)] / cond[z]
    level_coeffs(s, 0, values, up0, down0, e0)


def coeff_coarse_kernel(s, prm, up1, down1, e1, u2, l2, e2):
    values = die_values(s, prm)
    cond, vert, via, blocks = values
    level_coeffs(s, 1, values, up1, down1, e1)
    group = iota((1, LN), 1) // s.c2
    xin = iota((1, LN), 1) % s.c2

    def by_group(values):
        out = jnp.zeros((1, LN), F32)
        for g in range(s.nd):
            out = jnp.where(group == g, values[g], out)
        return out

    cl = [by_group([cond[s.lz * g + a] for g in range(s.nd)]) * 16.0 for a in range(s.lz)]
    vl = [by_group([vert[s.lz * g + a] for g in range(s.nd)]) * 256.0 for a in range(s.lz)]
    vial = by_group(via)
    row2 = (iota((1, LN), 1) * 16).astype(F32)
    ra = jnp.concatenate([overlap(row2, 16.0, b[0], b[1]) for b in blocks], axis=0).astype(BF16)
    zero2 = jnp.zeros((s.nt, LN), F32)
    for e in range(s.nd):
        col2 = ((e * s.c2 + xin) * 16).astype(F32)
        cb = jnp.concatenate(
            [jnp.where(group == g, overlap(col2, 16.0, b[2], b[3]), 0.0) for g, b in enumerate(blocks)],
            axis=0,
        ).astype(BF16)
        v2 = pair_dot(ra, cb)[: s.nt] * vial
        ups = [zero2 + vl[a] for a in range(s.lz - 1)] + [v2]
        first = jnp.where(iota((s.nt, LN), 1) >= s.c2, pltpu.roll(v2, s.c2, 1), 0.0)
        lows = [first] + ups[:-1]
        for a in range(s.lz):
            q = e * s.lz + a
            u2[q] = ups[a] / cl[a]
            l2[q] = lows[a] / cl[a]
            e2[q] = OMEGA * cl[a] / (4.0 * cl[a] + ups[a] + lows[a])


class Level:
    def __init__(self, s, level, up, down, scale, cu, cd):
        self.s, self.up, self.down, self.scale, self.cu, self.cd = s, up, down, scale, cu, cd
        self.nj = (s.j0, s.j1)[level]
        self.us = 4.0**level

    def walk(self, src, f, lo, hi, emit, count=None):
        s, n = self.s, self.nj
        lane = iota((8, LN), 1)
        first, last = lane == 0, lane == LN - 1

        def group(g, carry):
            for a in range(s.lz):
                z = g * s.lz + a
                for r in windows(lo, hi):
                    rows = pl.ds(r, 8)
                    v = [src[z + 1, j, rows, :] for j in range(n)]
                    ahead = [pltpu.roll(x, LN - 1, 1) for x in v]
                    behind = [pltpu.roll(x, 1, 1) for x in v]
                    for j in range(count or n):
                        k_up = self.cu[z] * self.us if a < s.lz - 1 else self.up[g, j, rows, :]
                        k_down = self.cd[z] * self.us if a > 0 else self.down[g, j, rows, :]
                        x = jnp.where(last, ahead[(j + 1) % n], ahead[j]) + jnp.where(first, behind[j - 1], behind[j])
                        y = src[z + 1, j, pl.ds(r - 1, 8), :] + src[z + 1, j, pl.ds(r + 1, 8), :]
                        x = (f[z, j, rows, :] + x) + y
                        x = x + (k_up * src[z + 2, j, rows, :] + k_down * src[z, j, rows, :])
                        emit(z, j, rows, v[j], x, k_up, k_down)
            return carry

        lax.fori_loop(0, s.nd, group, 0)

    def sweep(self, src, dst, f, lo, hi):
        def emit(z, j, rows, v, g, *_):
            dst[z + 1, j, rows, :] = (1.0 - OMEGA) * v + self.scale[z, j, rows, :] * g

        self.walk(src, f, lo, hi, emit)

    def residual(self, src, f, lo, hi, put, count=None):
        def emit(z, j, rows, v, g, k_up, k_down):
            put(z, j, rows, g - (4.0 + k_up + k_down) * v)

        self.walk(src, f, lo, hi, emit, count)


def zero_ends(s, *bufs):
    for b in bufs:
        b[0] = jnp.zeros(b.shape[1:], F32)
        b[s.nz + 1] = jnp.zeros(b.shape[1:], F32)


def restrict(s, level, src, f, lo, hi, down, rbuf, sums, r1):
    for k in range(s.nz * s.j0):
        rbuf[k * s.re : k * s.re + 8, :] = jnp.zeros((8, LN), F32)
        rbuf[(k + 1) * s.re - 8 : (k + 1) * s.re, :] = jnp.zeros((8, LN), F32)

    def put(z, j, rows, x):
        rbuf[pl.ds((z * s.j0 + j) * s.re + rows.start, 8), :] = x

    level.residual(src, f, lo, hi, put)

    def body(z, carry):
        for j in range(s.j0):
            part = [rbuf[pl.ds((z * s.j0 + j) * s.re + k, s.r1, stride=4), :] for k in range(4)]
            sums[z, :, tiles(j)] = (part[0] + part[1]) + (part[2] + part[3])
        return carry

    lax.fori_loop(0, s.nz, body, 0)
    out = split_dot(sums[...].reshape(s.nz * s.r1, s.we), down[...])
    for z in range(s.nz):
        for j in range(s.j1):
            r1[z, j] = out[z * s.r1 : (z + 1) * s.r1, tiles(j)]


def down_kernel(s, out):
    p, q = iota((s.we, s.w1), 0), iota((s.we, s.w1), 1)
    at = p // 4 + jnp.where(p >= s.wc + HX, s.w1 - s.we // 4, 0)
    out[...] = jnp.where(at == q, 0.25, 0.0).astype(BF16)


def fine_first_kernel(s, from_one, from_two, one, two, up0, down0, e0, ic, cu, cd, down, f, v2, r1, va, rbuf, sums):
    level = Level(s, 0, up0, down0, e0, cu, cd)
    lower = even()
    zero_ends(s, va, v2)

    def body(z, carry):
        for k, (a, b) in enumerate(((from_two, from_one), (two, one), (one, two), (from_one, from_two))):
            rows = slice(k * HY, (k + 1) * HY)
            for j in range(s.j0):
                q = z * s.j0 + j
                x = jnp.where(lower, a[q], b[q]) * ic[z]
                f[z, j, rows, :] = x
                va[z + 1, j, rows, :] = e0[z, j, rows, :] * x
        return carry

    lax.fori_loop(0, s.nz, body, 0)
    level.sweep(va, v2, f, 1, s.re - 1)
    restrict(s, level, v2, f, HY - 4, s.re - HY + 4, down, rbuf, sums, r1)


def middle_first_kernel(s, r1a, r1, r1b, up1, down1, e1, cu, cd, down2, rx, w2, send, wa, buf):
    level = Level(s, 1, up1, down1, e1, cu, cd)
    half, own, pad = s.r1, s.own1, s.pad1
    sub = iota((half, LN), 0)
    lower = even()
    zero_ends(s, wa, w2)

    def body(z, carry):
        for j in range(s.j1):
            mid = pltpu.roll(r1[z, j], half // 2, 0)
            up = jnp.where(sub >= pad, mid, jnp.where(lower, r1b[z, j], r1a[z, j]))
            down = jnp.where(sub < own - (half - pad), mid, jnp.where(lower, r1a[z, j], r1b[z, j]))
            rx[z, j, :half, :] = up
            rx[z, j, half:, :] = down
            wa[z + 1, j, :half, :] = e1[z, j, :half, :] * up
            wa[z + 1, j, half:, :] = e1[z, j, half:, :] * down
        return carry

    lax.fori_loop(0, s.nz, body, 0)
    level.sweep(wa, w2, rx, pad - 4, pad + own + 4)

    def put(z, j, rows, x):
        buf[pl.ds(pl.multiple_of(z * 8, 8), 8), :] = x

    level.residual(w2, rx, pad - 2, pad + own + 2, put, 1)
    sub8, group = iota((8, LN), 0), iota((8, LN), 1) // s.c2
    tile = jnp.zeros((8, LN), F32)
    for h in range(s.nz // 8):
        part = [buf[pl.ds(64 * h + 2 + k, 8, stride=8), :] for k in range(own)]
        x = split_dot((part[0] + part[1]) + (part[2] + part[3]), down2[...])
        y = pltpu.roll(x, 4, 0)
        for g in (2 * h, 2 * h + 1):
            tile = jnp.where(group == g, jnp.where((sub8 < 4) == (g % 2 == 0), x, y), tile)
    for k in range(s.nd * s.nt * s.lz // 8):
        send[8 * k : 8 * k + 8, :] = tile


def coarse(s, got, u2, l2, e2, cs):
    lane = iota((s.nt, LN), 1)
    x, t = lane % s.c2, iota((s.nt, LN), 0)
    first_x, last_x = x == 0, x == s.c2 - 1
    slabs = s.nd * s.lz
    rhs, v = [], []
    for q in range(slabs):
        e, a = q // s.lz, q % s.lz
        r = got[pl.ds(e * s.nt * s.lz + a, s.nt, stride=s.lz), :]
        rhs.append(r)
        v.append(e2[q] * r)
    zero = jnp.zeros((s.nt, LN), F32)

    def body(_, v):
        new = []
        for q in range(slabs):
            e, a = q // s.lz, q % s.lz
            w = v[q]
            right = pltpu.roll(v[q + s.lz], s.c2 - 1, 1) if e < s.nd - 1 else zero
            left = pltpu.roll(v[q - s.lz], LN - (s.c2 - 1), 1) if e > 0 else zero
            side = jnp.where(last_x, right, pltpu.roll(w, LN - 1, 1))
            side += jnp.where(first_x, left, pltpu.roll(w, 1, 1))
            side += jnp.where(t == s.nt - 1, 0.0, pltpu.roll(w, s.nt - 1, 0))
            side += jnp.where(t == 0, 0.0, pltpu.roll(w, 1, 0))
            if a < s.lz - 1:
                up = v[q + 1]
            else:
                up = jnp.where(lane >= LN - s.c2, 0.0, pltpu.roll(v[q - a], LN - s.c2, 1))
            if a > 0:
                down = v[q - 1]
            else:
                down = jnp.where(lane < s.c2, 0.0, pltpu.roll(v[q + s.lz - 1], s.c2, 1))
            g = (rhs[q] + side) + (u2[q] * up + l2[q] * down)
            new.append((1.0 - OMEGA) * w + e2[q] * g)
        return tuple(new)

    v = lax.fori_loop(0, NC - 1, body, tuple(v))
    for q in range(slabs):
        cs[q, :HY, :] = jnp.zeros((HY, LN), F32)
        cs[q, HY + s.nt :, :] = jnp.zeros((HY, LN), F32)
        cs[q, HY : HY + s.nt, :] = v[q]


def middle_last(s, level, cs, spread2, w2, rx, comp, wide, wa, wb):
    d, t = place()
    lane, upper = iota((8, LN), 1), iota((8, LN), 0) < 4
    after = lax.rem(d + 1, s.nd) * s.lz
    before = lax.rem(d + s.nd - 1, s.nd) * s.lz
    zero_ends(s, wa, wb)
    for a in range(s.lz):
        rows = [cs[base + a, pl.ds(HY - 1 + t, 8), :] for base in (d * s.lz, after, before)]
        for g in range(s.nd):
            turn = []
            for r, by in zip(rows, (0, s.c2, LN - s.c2)):
                by = (by - g * s.c2) % LN
                turn.append(pltpu.roll(r, by, 1) if by else r)
            z = g * s.lz + a
            comp[8 * z : 8 * z + 8, :] = jnp.where(
                lane < s.c2, turn[0], jnp.where(lane < LN // 2, turn[1], turn[2])
            )
    wide[...] = split_dot(comp[...], spread2[...]).reshape(wide.shape)

    def body(z, carry):
        x = [[wide[z, k : k + 1, tiles(j)] for k in range(3)] for j in range(s.j1)]
        for k in range(2):
            rows = slice(s.pad1 - 4 + 4 * k, s.pad1 + 4 + 4 * k)
            for j in range(s.j1):
                y = w2[z + 1, j, rows, :] + jnp.where(upper, x[j][k], x[j][k + 1])
                wa[z + 1, j, rows, :] = jnp.where(level.scale[z, j, rows, :] > 0.0, y, 0.0)
        return carry

    lax.fori_loop(0, s.nz, body, 0)
    level.sweep(wa, wb, rx, s.pad1 - 3, s.pad1 + s.own1 + 3)
    level.sweep(wb, wa, rx, s.pad1 - 2, s.pad1 + s.own1 + 2)


def correct_fine(s, w, v, spread1, wide, dst):
    rows = slice(s.pad1 - 2, s.pad1 + s.own1 + 2)
    lhs = jnp.concatenate([w[1 : s.nz + 1, j, rows, :].reshape(s.nz * s.r1, LN) for j in range(s.j1)], axis=1)
    wide[...] = split_dot(lhs, spread1[...]).reshape(wide.shape)
    upper = iota((8, LN), 0) < 4

    def body(z, carry):
        for k in range(s.r1 // 2):
            rows = slice(8 * k, 8 * k + 8)
            for j in range(s.j0):
                x = [wide[z, 2 * k + i : 2 * k + i + 1, tiles(j)] for i in range(2)]
                dst[z + 1, j, rows, :] = v[z + 1, j, rows, :] + jnp.where(upper, x[0], x[1])
        return carry

    lax.fori_loop(0, s.nz, body, 0)


def back_kernel(
    s, got, v2, f, w2, rx,
    u2, l2, e2, up1, down1, e1, up0, down0, e0, cu, cd, spread2, spread1, down,
    v, r1, cs, comp, wide2, wa, wb, va, vb, wide, rbuf,
):
    fine = Level(s, 0, up0, down0, e0, cu, cd)
    middle = Level(s, 1, up1, down1, e1, cu, cd)
    zero_ends(s, va, vb, v)
    coarse(s, got, u2, l2, e2, cs)
    middle_last(s, middle, cs, spread2, w2, rx, comp, wide2, wa, wb)
    correct_fine(s, wa, v2, spread1, wide, va)
    fine.sweep(va, vb, f, 2, s.re - 2)
    fine.sweep(vb, va, f, 3, s.re - 3)
    fine.sweep(va, vb, f, 4, s.re - 4)
    fine.sweep(vb, v, f, 5, s.re - 5)
    restrict(s, fine, v, f, HY, HY + s.rows, down, rbuf, wide, r1)


def last_kernel(
    s, got, w2, rx, v2, f, u2, l2, e2, up1, down1, e1, up0, down0, e0, c, cu, cd, spread2, spread1, *refs,
):
    outs, (cs, comp, wide2, wa, wb, va, vb, wide, rbuf) = refs[: s.nd], refs[s.nd :]
    fine = Level(s, 0, up0, down0, e0, cu, cd)
    middle = Level(s, 1, up1, down1, e1, cu, cd)
    d, _ = place()
    zero_ends(s, va, vb)
    coarse(s, got, u2, l2, e2, cs)
    middle_last(s, middle, cs, spread2, w2, rx, comp, wide2, wa, wb)
    correct_fine(s, wa, v2, spread1, wide, va)
    fine.sweep(va, vb, f, HY - 2, HY + s.rows + 2)
    fine.sweep(vb, va, f, HY - 1, HY + s.rows + 1)

    def put(z, j, rows, x):
        at = (z * (s.j0 - 1) + j) * s.rows + rows.start - HY
        rbuf[pl.ds(pl.multiple_of(at, 8), 8), :] = x * c[z]

    fine.residual(va, f, HY, HY + s.rows, put, s.j0 - 1)
    for step, out in enumerate(outs):
        e = lax.rem(d + step, s.nd)
        for a in range(s.lz):
            z = e * s.lz + a
            for j in range(s.j0 - 1):
                out[0, a, :, tiles(j)] = va[z + 1, j, HY : HY + s.rows, :]
                at = pl.multiple_of((z * (s.j0 - 1) + j) * s.rows, 8)
                out[1, a, :, tiles(j)] = rbuf[pl.ds(at, s.rows), :]


def unpack_kernel(s, *refs):
    parts, outs, sem = refs[: s.nd], refs[s.nd : -1], refs[-1]
    d, _ = place()
    copies = []
    for step, part in enumerate(parts):
        e = lax.rem(d + s.nd - step, s.nd)
        cols = pl.ds(pl.multiple_of(e * s.wc, LN), s.wc)
        for k, out in enumerate(outs):
            copies.append(pltpu.make_async_copy(part.at[k], out.at[:, :, cols], sem.at[len(outs) * step + k]))
    for c in copies:
        c.start()
    for c in copies:
        c.wait()


def call(name, kernel, s, outs, scratch=(), to_hbm=False, from_hbm=False, in_vmem=False, limit=32 << 20):
    shapes = [pltpu.VMEM(o, F32) if in_vmem else jax.ShapeDtypeStruct(o, F32) for o in outs]
    spaces = [pl.BlockSpec(memory_space=m) for m in (pltpu.VMEM, pltpu.HBM)]

    def run(*args):
        total = sum(int(np.prod(a.shape)) * 4 for a in args) + sum(int(np.prod(o)) * 4 for o in outs)
        return pl.pallas_call(
            functools.partial(kernel, s),
            name=name,
            out_shape=shapes,
            in_specs=[spaces[from_hbm]] * len(args),
            out_specs=[spaces[to_hbm]] * len(outs),
            scratch_shapes=[pltpu.VMEM(x, F32) if isinstance(x, tuple) else x for x in scratch],
            compiler_params=pltpu.CompilerParams(vmem_limit_bytes=limit),
            cost_estimate=pl.CostEstimate(flops=4 * total, bytes_accessed=total, transcendentals=0),
        )(*args)

    return run


def shift(x, axis, by):
    n = lax.axis_size(axis)
    return lax.ppermute(x, axis, [(i, (i + by) % n) for i in range(n)])


def swap(x, odd):
    n = lax.axis_size("tile")
    to = [((k - odd) ^ 1) + odd for k in range(n)]
    return lax.ppermute(x, "tile", [(k, q if 0 <= q < n else k) for k, q in enumerate(to)])


def tables(s):
    p = np.arange(s.we)
    at = p // 4 + np.where(p >= s.wc + HX, s.w1 - s.we // 4, 0)
    down = at[:, None] == np.arange(s.w1)[None, :]
    q = np.arange(s.w1)
    k = q // 4 + np.where(q >= s.w1 - HX // 4, LN - s.w1 // 4, 0)
    used = (q < s.c1 + HX // 4) | (q >= s.w1 - HX // 4)
    spread2 = (np.arange(LN)[:, None] == k[None, :]) & used[None, :]
    r = np.arange(LN)
    down2 = (r // 4)[:, None] == (r % s.c2)[None, :]
    return [jnp.asarray(m, BF16) for m in (down.T, spread2, down2 * 0.25)]


def local(s, source_heating, material_thermal_values, layer_material, via_conductance, via_blocks):
    spread1, spread2, down2 = tables(s)
    down = pl.pallas_call(
        functools.partial(down_kernel, s),
        name="down",
        out_shape=jax.ShapeDtypeStruct((s.we, s.w1), BF16),
        compiler_params=pltpu.CompilerParams(vmem_limit_bytes=4 << 20),
        cost_estimate=pl.CostEstimate(flops=1 << 20, bytes_accessed=1 << 20, transcendentals=0),
    )()
    smem, packed = pltpu.SMEM, (s.part + 8, LN)
    sends = call(
        "pack", pack_kernel, s, [packed] * s.nd,
        [
            smem(material_thermal_values.shape, F32), smem(layer_material.shape, jnp.int32),
            smem((1, 1), F32), pltpu.VMEM((4, s.nb), jnp.int32),
            pltpu.VMEM(source_heating.shape, F32), pltpu.SemaphoreType.DMA((5,)),
        ],
        from_hbm=True, in_vmem=True, limit=VMEM - 4 * s.nd * packed[0] * packed[1],
    )(material_thermal_values, layer_material, via_conductance[None], via_blocks[0].T, source_heating)
    parts = [sends[0]] + [shift(sends[k], "die", k) for k in range(1, s.nd)]
    half = (s.nz * s.j0, HY, LN)
    one, two, prm = call("assemble", assemble_kernel, s, [half, half, (s.nd, 8, LN)])(*parts)
    f0, f1, small = (s.j0, s.re, LN), (s.j1, s.e1, LN), (s.nz, s.j1, s.r1, LN)
    fine, fine_v = (s.nz, *f0), (s.nz + 2, *f0)
    mid, mid_v = (s.nz, *f1), (s.nz + 2, *f1)
    slab, table = (s.nd * s.lz, s.nt, LN), (s.nz, 8, LN)
    up0, down0, e0, c, ic, cu, cd = call(
        "coeff_fine", coeff_fine_kernel, s, [(s.nd, *f0), (s.nd, *f0), fine, table, table, table, table]
    )(prm)
    flat, rbuf = (s.nz, s.r1, s.we), (s.nz * s.j0 * s.re, LN)
    f, v2, r1 = call("fine_first", fine_first_kernel, s, [fine, fine_v, small], [fine_v, rbuf, flat])(
        swap(one, 0), swap(two, 1), one, two, up0, down0, e0, ic, cu, cd, down
    )
    up1, down1, e1, u2, l2, e2 = call(
        "coeff_coarse", coeff_coarse_kernel, s, [(s.nd, *f1), (s.nd, *f1), mid, slab, slab, slab]
    )(prm)

    def middle_first(r1):
        return call(
            "middle_first", middle_first_kernel, s,
            [mid, mid_v, (s.nd * s.nt * s.lz, LN)], [mid_v, (s.nz * 8, LN)],
        )(swap(r1, 0), r1, swap(r1, 1), up1, down1, e1, cu, cd, down2)

    def everywhere(send):
        return lax.all_to_all(send, ("die", "tile"), 0, 0, tiled=True)

    spaces = [(s.nd * s.lz, s.nt + 2 * HY, LN), (s.nz * 8, LN), (s.nz, 8, s.w1), mid_v, mid_v]
    spaces += [fine_v, fine_v, flat]
    rx, w2, send = middle_first(r1)
    levels = (u2, l2, e2, up1, down1, e1, up0, down0, e0)
    v, r1 = call("back", back_kernel, s, [fine_v, small], spaces + [rbuf])(
        everywhere(send), v2, f, w2, rx, *levels, cu, cd, spread2, spread1, down
    )
    rx, w2, send = middle_first(r1)
    piece = (2, s.lz, s.rows, s.wc)
    sends = call(
        "last", last_kernel, s, [piece] * s.nd, spaces + [(s.nz * (s.j0 - 1) * s.rows, LN)]
    )(everywhere(send), w2, rx, v, f, *levels, c, cu, cd, spread2, spread1)
    parts = [sends[0]] + [shift(sends[k], "die", k) for k in range(1, s.nd)]
    whole = (s.lz, s.rows, s.width)
    return tuple(call("unpack", unpack_kernel, s, [whole] * 2, [pltpu.SemaphoreType.DMA((2 * s.nd,))], True)(*parts))


def solution(mesh):
    in_specs = (P("die", "tile", None), P(), P("die"), P("die"), P("die", None, None))
    out_specs = (P("die", "tile", None), P("die", "tile", None))

    def body(f, mat, material, conductance, blocks):
        s = Sizes(mesh.shape, f.shape, blocks.shape[1])
        return local(s, f, mat, material, conductance, blocks)

    return jax.shard_map(body, mesh=mesh, in_specs=in_specs, out_specs=out_specs, check_vma=False)
```

```python
import functools

import jax
import jax.numpy as jnp
import numpy as np
from jax import lax
from jax.experimental import pallas as pl
from jax.experimental.pallas import tpu as pltpu
from jax.sharding import PartitionSpec as P


OMEGA = 0.8
NC = 6
LN = 128
HX = 64
VMEM = 67_043_328
HY = 8
F32 = jnp.float32
BF16 = jnp.bfloat16


def iota(shape, axis):
    return lax.broadcasted_iota(jnp.int32, shape, axis)


def split_dot(x, m):
    hi = x.astype(BF16)
    lo = (x - hi.astype(F32)).astype(BF16)
    return jnp.dot(hi, m, preferred_element_type=F32) + jnp.dot(lo, m, preferred_element_type=F32)


def pair_dot(a, b):
    return lax.dot_general(a, b, (((0,), (0,)), ((), ())), preferred_element_type=F32)


class Sizes:
    def __init__(self, mesh_shape, f_shape, n_blocks):
        self.nd, self.nt = mesh_shape["die"], mesh_shape["tile"]
        self.lz, self.rows, self.width = f_shape
        self.nb = n_blocks
        self.wc = self.width // self.nd
        self.we = self.wc + LN
        self.j0 = self.we // LN
        self.nz = self.nd * self.lz
        self.re = self.rows + 2 * HY
        self.own1 = self.rows // 4
        self.r1 = self.re // 4
        self.c1 = self.wc // 4
        self.e1 = 2 * self.r1
        self.pad1 = (self.e1 - self.own1) // 2
        self.j1 = 2
        self.w1 = self.j1 * LN
        self.c2 = self.wc // 16
        self.part = self.lz * self.j0 * self.rows
        assert self.rows == 16 and self.lz == 4 and self.c1 == LN
        assert self.nd * self.c2 == LN and self.nb <= LN and self.nt <= LN and self.nt % 8 == 0


def place():
    return lax.axis_index("die"), lax.axis_index("tile")


def even():
    _, t = place()
    return lax.rem(t, 2) == 0


def tiles(j):
    return slice(j * LN, (j + 1) * LN)


def windows(lo, hi):
    return [min(r, hi - 8) for r in range(lo, hi, 8)]


def pack_kernel(s, mat_h, material_h, conductance_h, blocks_h, f_h, *refs):
    outs, (mat, material, conductance, blocks, f, sem) = refs[: s.nd], refs[s.nd :]
    pairs = [(f_h, f), (mat_h, mat), (material_h, material), (conductance_h, conductance), (blocks_h, blocks)]
    copies = [pltpu.make_async_copy(a, b, sem.at[k]) for k, (a, b) in enumerate(pairs)]
    for c in copies:
        c.start()
    for c in copies[1:]:
        c.wait()
    d, _ = place()
    lane, sub = iota((8, LN), 1), iota((8, LN), 0)
    info = jnp.where((sub == 5) & (lane == 0), conductance[0, 0], 0.0)
    for z in range(s.lz):
        info = jnp.where((sub == 4) & (lane == z), mat[material[z]], info)
    for out in outs:
        out[s.part :, :] = info
        out[s.part : s.part + 4, : s.nb] = blocks[...].astype(F32)
    copies[0].wait()
    low = iota((s.rows, LN), 1) < HX
    for step, out in enumerate(outs):
        e = lax.rem(d + step, s.nd)
        right = lax.rem(e + 1, s.nd) * s.wc
        left = lax.rem(e + s.nd - 1, s.nd) * s.wc + (s.wc - LN)

        def column(z, at):
            return f[z, :, pl.ds(pl.multiple_of(at, LN), LN)]

        for z in range(s.lz):
            for j in range(s.j0):
                at = (z * s.j0 + j) * s.rows
                if j < s.j0 - 1:
                    x = column(z, e * s.wc + j * LN)
                else:
                    x = jnp.where(low, column(z, right), column(z, left))
                out[at : at + s.rows, :] = x


def assemble_kernel(s, *refs):
    parts, (one, two, prm) = refs[: s.nd], refs[s.nd :]
    d, _ = place()
    n = s.lz * s.j0
    lower = even()
    for step, part in enumerate(parts):
        e = lax.rem(d + s.nd - step, s.nd)
        for q in range(n):
            top = part[q * s.rows : q * s.rows + HY, :]
            bot = part[q * s.rows + HY : (q + 1) * s.rows, :]
            one[n * e + q] = jnp.where(lower, bot, top)
            two[n * e + q] = jnp.where(lower, top, bot)
        prm[e] = part[s.part :, :]


def overlap(lo, size, first, past):
    return jnp.maximum(jnp.minimum(lo + size, past) - jnp.maximum(lo, first), 0.0)


def block_bounds(s, info):
    b = jnp.transpose(info)
    lane = iota((LN, 8), 1)
    col = [jnp.sum(jnp.where(lane == k, b, 0.0), axis=1, keepdims=True) for k in range(4)]
    col = [x[: s.nb] for x in col]
    return col[0], col[0] + col[2], col[1], col[1] + col[3]


def die_values(s, prm):
    lane8, sub8 = iota((8, LN), 1), iota((8, LN), 0)

    def pick(tile, row, col):
        return jnp.sum(jnp.where((lane8 == col) & (sub8 == row), tile, 0.0), keepdims=True)

    info = [prm[g] for g in range(s.nd)]
    cond = [pick(info[z // s.lz], 4, z % s.lz) for z in range(s.nz)]
    via = [pick(info[g], 5, 0) for g in range(s.nd)]
    vert = [2.0 * p * q / (p + q) for p, q in zip(cond, cond[1:] + cond[-1:])]
    return cond, vert, via, [block_bounds(s, x) for x in info]


def level_coeffs(s, level, values, via_up, via_down, scale):
    cond, vert, via, blocks = values
    d, t = place()
    size = 4**level
    n, own = (s.we, s.wc) if level == 0 else (s.w1, s.c1)
    height, nj = (s.re, s.j0) if level == 0 else (s.e1, s.j1)
    pad = HY if level == 0 else s.pad1
    halo = HX // size

    def columns(shape, axis):
        p = iota(shape, axis)
        return p, d * own + jnp.where(p >= n - halo, p - n, p)

    first = t * (s.rows // size) - pad
    row = ((first + iota((1, LN), 1)) * size).astype(F32)
    col = (columns((1, n), 1)[1] * size).astype(F32)
    rr = first + iota((height, n), 0)
    pp, cc = columns((height, n), 1)
    inside = (rr >= 0) & (rr < s.rows * s.nt // size) & (cc >= 0) & (cc < s.width // size)
    inside = jnp.where(inside & ((pp < own + halo) | (pp >= n - halo)), OMEGA, 0.0)
    via_down[0] = jnp.zeros(via_down.shape[1:], F32)
    for g in range(s.nd):
        r0, r1, c0, c1 = blocks[g]
        m = pair_dot(
            overlap(row, float(size), r0, r1).astype(BF16), overlap(col, float(size), c0, c1).astype(BF16)
        )[:height]
        top = (g + 1) * s.lz - 1
        m = m * (via[g] * (0.25**level))
        for j in range(nj):
            via_up[g, j] = m[:, tiles(j)] / cond[top]
            if g + 1 < s.nd:
                via_down[g + 1, j] = m[:, tiles(j)] / cond[top + 1]
    for z in range(s.nz):
        g, a = z // s.lz, z % s.lz
        const = 4.0
        if a < s.lz - 1:
            const = const + vert[z] * (4.0**level) / cond[z]
        if a > 0:
            const = const + vert[z - 1] * (4.0**level) / cond[z]
        for j in range(nj):
            diag = const
            if a == s.lz - 1:
                diag = diag + via_up[g, j]
            if a == 0:
                diag = diag + via_down[g, j]
            scale[z, j] = inside[:, tiles(j)] / diag


def coeff_fine_kernel(s, prm, up0, down0, e0, c, ic, cu, cd):
    values = die_values(s, prm)
    cond, vert = values[:2]
    for z in range(s.nz):
        c[z] = jnp.zeros((8, LN), F32) + cond[z]
        ic[z] = jnp.zeros((8, LN), F32) + 1.0 / cond[z]
        cu[z] = jnp.zeros((8, LN), F32) + vert[z] / cond[z]
        cd[z] = jnp.zeros((8, LN), F32) + vert[max(z - 1, 0)] / cond[z]
    level_coeffs(s, 0, values, up0, down0, e0)


def coeff_coarse_kernel(s, prm, up1, down1, e1, u2, l2, e2):
    values = die_values(s, prm)
    cond, vert, via, blocks = values
    level_coeffs(s, 1, values, up1, down1, e1)
    group = iota((1, LN), 1) // s.c2
    xin = iota((1, LN), 1) % s.c2

    def by_group(values):
        out = jnp.zeros((1, LN), F32)
        for g in range(s.nd):
            out = jnp.where(group == g, values[g], out)
        return out

    cl = [by_group([cond[s.lz * g + a] for g in range(s.nd)]) * 16.0 for a in range(s.lz)]
    vl = [by_group([vert[s.lz * g + a] for g in range(s.nd)]) * 256.0 for a in range(s.lz)]
    vial = by_group(via)
    row2 = (iota((1, LN), 1) * 16).astype(F32)
    ra = jnp.concatenate([overlap(row2, 16.0, b[0], b[1]) for b in blocks], axis=0).astype(BF16)
    zero2 = jnp.zeros((s.nt, LN), F32)
    for e in range(s.nd):
        col2 = ((e * s.c2 + xin) * 16).astype(F32)
        cb = jnp.concatenate(
            [jnp.where(group == g, overlap(col2, 16.0, b[2], b[3]), 0.0) for g, b in enumerate(blocks)],
            axis=0,
        ).astype(BF16)
        v2 = pair_dot(ra, cb)[: s.nt] * vial
        ups = [zero2 + vl[a] for a in range(s.lz - 1)] + [v2]
        first = jnp.where(iota((s.nt, LN), 1) >= s.c2, pltpu.roll(v2, s.c2, 1), 0.0)
        lows = [first] + ups[:-1]
        for a in range(s.lz):
            q = e * s.lz + a
            u2[q] = ups[a] / cl[a]
            l2[q] = lows[a] / cl[a]
            e2[q] = OMEGA * cl[a] / (4.0 * cl[a] + ups[a] + lows[a])


class Level:
    def __init__(self, s, level, up, down, scale, cu, cd):
        self.s, self.up, self.down, self.scale, self.cu, self.cd = s, up, down, scale, cu, cd
        self.nj = (s.j0, s.j1)[level]
        self.us = 4.0**level

    def walk(self, src, f, lo, hi, emit, count=None):
        s, n = self.s, self.nj
        lane = iota((8, LN), 1)
        first, last = lane == 0, lane == LN - 1

        def group(g, carry):
            for a in range(s.lz):
                z = g * s.lz + a
                for r in windows(lo, hi):
                    rows = pl.ds(r, 8)
                    v = [src[z + 1, j, rows, :] for j in range(n)]
                    ahead = [pltpu.roll(x, LN - 1, 1) for x in v]
                    behind = [pltpu.roll(x, 1, 1) for x in v]
                    for j in range(count or n):
                        k_up = self.cu[z] * self.us if a < s.lz - 1 else self.up[g, j, rows, :]
                        k_down = self.cd[z] * self.us if a > 0 else self.down[g, j, rows, :]
                        x = jnp.where(last, ahead[(j + 1) % n], ahead[j]) + jnp.where(first, behind[j - 1], behind[j])
                        y = src[z + 1, j, pl.ds(r - 1, 8), :] + src[z + 1, j, pl.ds(r + 1, 8), :]
                        x = (f[z, j, rows, :] + x) + y
                        x = x + (k_up * src[z + 2, j, rows, :] + k_down * src[z, j, rows, :])
                        emit(z, j, rows, v[j], x, k_up, k_down)
            return carry

        lax.fori_loop(0, s.nd, group, 0)

    def sweep(self, src, dst, f, lo, hi):
        def emit(z, j, rows, v, g, *_):
            dst[z + 1, j, rows, :] = (1.0 - OMEGA) * v + self.scale[z, j, rows, :] * g

        self.walk(src, f, lo, hi, emit)

    def residual(self, src, f, lo, hi, put, count=None):
        def emit(z, j, rows, v, g, k_up, k_down):
            put(z, j, rows, g - (4.0 + k_up + k_down) * v)

        self.walk(src, f, lo, hi, emit, count)


def zero_ends(s, *bufs):
    for b in bufs:
        b[0] = jnp.zeros(b.shape[1:], F32)
        b[s.nz + 1] = jnp.zeros(b.shape[1:], F32)


def restrict(s, level, src, f, lo, hi, down, rbuf, sums, r1):
    for k in range(s.nz * s.j0):
        rbuf[k * s.re : k * s.re + 8, :] = jnp.zeros((8, LN), F32)
        rbuf[(k + 1) * s.re - 8 : (k + 1) * s.re, :] = jnp.zeros((8, LN), F32)

    def put(z, j, rows, x):
        rbuf[pl.ds((z * s.j0 + j) * s.re + rows.start, 8), :] = x

    level.residual(src, f, lo, hi, put)

    def body(z, carry):
        for j in range(s.j0):
            part = [rbuf[pl.ds((z * s.j0 + j) * s.re + k, s.r1, stride=4), :] for k in range(4)]
            sums[z, :, tiles(j)] = (part[0] + part[1]) + (part[2] + part[3])
        return carry

    lax.fori_loop(0, s.nz, body, 0)
    out = split_dot(sums[...].reshape(s.nz * s.r1, s.we), down[...])
    for z in range(s.nz):
        for j in range(s.j1):
            r1[z, j] = out[z * s.r1 : (z + 1) * s.r1, tiles(j)]


def down_kernel(s, out):
    p, q = iota((s.we, s.w1), 0), iota((s.we, s.w1), 1)
    at = p // 4 + jnp.where(p >= s.wc + HX, s.w1 - s.we // 4, 0)
    out[...] = jnp.where(at == q, 0.25, 0.0).astype(BF16)


def fine_first_kernel(s, from_one, from_two, one, two, up0, down0, e0, ic, cu, cd, down, f, v2, r1, va, rbuf, sums):
    level = Level(s, 0, up0, down0, e0, cu, cd)
    lower = even()
    zero_ends(s, va, v2)

    def body(z, carry):
        for k, (a, b) in enumerate(((from_two, from_one), (two, one), (one, two), (from_one, from_two))):
            rows = slice(k * HY, (k + 1) * HY)
            for j in range(s.j0):
                q = z * s.j0 + j
                x = jnp.where(lower, a[q], b[q]) * ic[z]
                f[z, j, rows, :] = x
                va[z + 1, j, rows, :] = e0[z, j, rows, :] * x
        return carry

    lax.fori_loop(0, s.nz, body, 0)
    level.sweep(va, v2, f, 1, s.re - 1)
    restrict(s, level, v2, f, HY - 4, s.re - HY + 4, down, rbuf, sums, r1)


def middle_first_kernel(s, r1a, r1, r1b, up1, down1, e1, cu, cd, down2, rx, w2, send, wa, buf):
    level = Level(s, 1, up1, down1, e1, cu, cd)
    half, own, pad = s.r1, s.own1, s.pad1
    sub = iota((half, LN), 0)
    lower = even()
    zero_ends(s, wa, w2)

    def body(z, carry):
        for j in range(s.j1):
            mid = pltpu.roll(r1[z, j], half // 2, 0)
            up = jnp.where(sub >= pad, mid, jnp.where(lower, r1b[z, j], r1a[z, j]))
            down = jnp.where(sub < own - (half - pad), mid, jnp.where(lower, r1a[z, j], r1b[z, j]))
            rx[z, j, :half, :] = up
            rx[z, j, half:, :] = down
            wa[z + 1, j, :half, :] = e1[z, j, :half, :] * up
            wa[z + 1, j, half:, :] = e1[z, j, half:, :] * down
        return carry

    lax.fori_loop(0, s.nz, body, 0)
    level.sweep(wa, w2, rx, pad - 4, pad + own + 4)

    def put(z, j, rows, x):
        buf[pl.ds(pl.multiple_of(z * 8, 8), 8), :] = x

    level.residual(w2, rx, pad - 2, pad + own + 2, put, 1)
    sub8, group = iota((8, LN), 0), iota((8, LN), 1) // s.c2
    tile = jnp.zeros((8, LN), F32)
    for h in range(s.nz // 8):
        part = [buf[pl.ds(64 * h + 2 + k, 8, stride=8), :] for k in range(own)]
        x = split_dot((part[0] + part[1]) + (part[2] + part[3]), down2[...])
        y = pltpu.roll(x, 4, 0)
        for g in (2 * h, 2 * h + 1):
            tile = jnp.where(group == g, jnp.where((sub8 < 4) == (g % 2 == 0), x, y), tile)
    for k in range(s.nd * s.nt * s.lz // 8):
        send[8 * k : 8 * k + 8, :] = tile


def coarse(s, got, u2, l2, e2, cs):
    lane = iota((s.nt, LN), 1)
    x, t = lane % s.c2, iota((s.nt, LN), 0)
    first_x, last_x = x == 0, x == s.c2 - 1
    slabs = s.nd * s.lz
    rhs, v = [], []
    for q in range(slabs):
        e, a = q // s.lz, q % s.lz
        r = got[pl.ds(e * s.nt * s.lz + a, s.nt, stride=s.lz), :]
        rhs.append(r)
        v.append(e2[q] * r)
    zero = jnp.zeros((s.nt, LN), F32)

    def body(_, v):
        new = []
        for q in range(slabs):
            e, a = q // s.lz, q % s.lz
            w = v[q]
            right = pltpu.roll(v[q + s.lz], s.c2 - 1, 1) if e < s.nd - 1 else zero
            left = pltpu.roll(v[q - s.lz], LN - (s.c2 - 1), 1) if e > 0 else zero
            side = jnp.where(last_x, right, pltpu.roll(w, LN - 1, 1))
            side += jnp.where(first_x, left, pltpu.roll(w, 1, 1))
            side += jnp.where(t == s.nt - 1, 0.0, pltpu.roll(w, s.nt - 1, 0))
            side += jnp.where(t == 0, 0.0, pltpu.roll(w, 1, 0))
            if a < s.lz - 1:
                up = v[q + 1]
            else:
                up = jnp.where(lane >= LN - s.c2, 0.0, pltpu.roll(v[q - a], LN - s.c2, 1))
            if a > 0:
                down = v[q - 1]
            else:
                down = jnp.where(lane < s.c2, 0.0, pltpu.roll(v[q + s.lz - 1], s.c2, 1))
            g = (rhs[q] + side) + (u2[q] * up + l2[q] * down)
            new.append((1.0 - OMEGA) * w + e2[q] * g)
        return tuple(new)

    v = lax.fori_loop(0, NC - 1, body, tuple(v))
    for q in range(slabs):
        cs[q, :HY, :] = jnp.zeros((HY, LN), F32)
        cs[q, HY + s.nt :, :] = jnp.zeros((HY, LN), F32)
        cs[q, HY : HY + s.nt, :] = v[q]


def middle_last(s, level, cs, spread2, w2, rx, comp, wide, wa, wb):
    d, t = place()
    lane, upper = iota((8, LN), 1), iota((8, LN), 0) < 4
    after = lax.rem(d + 1, s.nd) * s.lz
    before = lax.rem(d + s.nd - 1, s.nd) * s.lz
    zero_ends(s, wa, wb)
    for a in range(s.lz):
        rows = [cs[base + a, pl.ds(HY - 1 + t, 8), :] for base in (d * s.lz, after, before)]
        for g in range(s.nd):
            turn = []
            for r, by in zip(rows, (0, s.c2, LN - s.c2)):
                by = (by - g * s.c2) % LN
                turn.append(pltpu.roll(r, by, 1) if by else r)
            z = g * s.lz + a
            comp[8 * z : 8 * z + 8, :] = jnp.where(
                lane < s.c2, turn[0], jnp.where(lane < LN // 2, turn[1], turn[2])
            )
    wide[...] = split_dot(comp[...], spread2[...]).reshape(wide.shape)

    def body(z, carry):
        x = [[wide[z, k : k + 1, tiles(j)] for k in range(3)] for j in range(s.j1)]
        for k in range(2):
            rows = slice(s.pad1 - 4 + 4 * k, s.pad1 + 4 + 4 * k)
            for j in range(s.j1):
                y = w2[z + 1, j, rows, :] + jnp.where(upper, x[j][k], x[j][k + 1])
                wa[z + 1, j, rows, :] = jnp.where(level.scale[z, j, rows, :] > 0.0, y, 0.0)
        return carry

    lax.fori_loop(0, s.nz, body, 0)
    level.sweep(wa, wb, rx, s.pad1 - 3, s.pad1 + s.own1 + 3)
    level.sweep(wb, wa, rx, s.pad1 - 2, s.pad1 + s.own1 + 2)


def correct_fine(s, w, v, spread1, wide, dst):
    rows = slice(s.pad1 - 2, s.pad1 + s.own1 + 2)
    lhs = jnp.concatenate([w[1 : s.nz + 1, j, rows, :].reshape(s.nz * s.r1, LN) for j in range(s.j1)], axis=1)
    wide[...] = split_dot(lhs, spread1[...]).reshape(wide.shape)
    upper = iota((8, LN), 0) < 4

    def body(z, carry):
        for k in range(s.r1 // 2):
            rows = slice(8 * k, 8 * k + 8)
            for j in range(s.j0):
                x = [wide[z, 2 * k + i : 2 * k + i + 1, tiles(j)] for i in range(2)]
                dst[z + 1, j, rows, :] = v[z + 1, j, rows, :] + jnp.where(upper, x[0], x[1])
        return carry

    lax.fori_loop(0, s.nz, body, 0)


def back_kernel(
    s, got, v2, f, w2, rx,
    u2, l2, e2, up1, down1, e1, up0, down0, e0, cu, cd, spread2, spread1, down,
    v, r1, cs, comp, wide2, wa, wb, va, vb, wide, rbuf,
):
    fine = Level(s, 0, up0, down0, e0, cu, cd)
    middle = Level(s, 1, up1, down1, e1, cu, cd)
    zero_ends(s, va, vb, v)
    coarse(s, got, u2, l2, e2, cs)
    middle_last(s, middle, cs, spread2, w2, rx, comp, wide2, wa, wb)
    correct_fine(s, wa, v2, spread1, wide, va)
    fine.sweep(va, vb, f, 2, s.re - 2)
    fine.sweep(vb, va, f, 3, s.re - 3)
    fine.sweep(va, vb, f, 4, s.re - 4)
    fine.sweep(vb, v, f, 5, s.re - 5)
    restrict(s, fine, v, f, HY, HY + s.rows, down, rbuf, wide, r1)


def last_kernel(
    s, got, w2, rx, v2, f, u2, l2, e2, up1, down1, e1, up0, down0, e0, cu, cd, spread2, spread1, *refs,
):
    outs, (cs, comp, wide2, wa, wb, va, vb, wide) = refs[: s.nd], refs[s.nd :]
    fine = Level(s, 0, up0, down0, e0, cu, cd)
    middle = Level(s, 1, up1, down1, e1, cu, cd)
    d, _ = place()
    zero_ends(s, va, vb)
    coarse(s, got, u2, l2, e2, cs)
    middle_last(s, middle, cs, spread2, w2, rx, comp, wide2, wa, wb)
    correct_fine(s, wa, v2, spread1, wide, va)
    fine.sweep(va, vb, f, HY - 2, HY + s.rows + 2)
    fine.sweep(vb, va, f, HY - 1, HY + s.rows + 1)

    nj = s.j0 - 1
    for step, out in enumerate(outs):
        e = lax.rem(d + step, s.nd)
        for k in range(s.lz + 2):
            for j in range(nj):
                at = (k * nj + j) * s.rows
                out[at : at + s.rows, :] = va[s.lz * e + k, j, HY : HY + s.rows, :]
        for a in range(s.lz):
            for j in range(nj):
                at = (s.lz + 2) * nj * s.rows + (a * nj + j) * 2
                out[at : at + 1, :] = va[s.lz * e + a + 1, j, HY - 1 : HY, :]
                out[at + 1 : at + 2, :] = va[s.lz * e + a + 1, j, HY + s.rows : HY + s.rows + 1, :]


def coeff_own_kernel(s, prm, up, down):
    d, t = place()
    lane8, sub8 = iota((8, LN), 1), iota((8, LN), 0)
    row = (t * s.rows + iota((1, LN), 1)).astype(F32)
    col = iota((1, s.width), 1).astype(F32)
    for k, out in enumerate((up, down)):
        info = prm[lax.rem(d + s.nd - k, s.nd)]
        via = jnp.sum(jnp.where((lane8 == 0) & (sub8 == 5), info, 0.0), keepdims=True)
        if k == 1:
            via = via * (d > 0).astype(F32)
        r0, r1, c0, c1 = block_bounds(s, info)
        m = pair_dot(overlap(row, 1.0, r0, r1).astype(BF16), overlap(col, 1.0, c0, c1).astype(BF16))
        for j in range(s.width // LN):
            out[j] = m[: s.rows, tiles(j)] * via


def finish_kernel(s, f, c, cu, up, down, *refs):
    parts, (u_out, defect_out, v, u, defect, sem) = refs[: s.nd], refs[s.nd :]
    d, _ = place()
    nj, n = s.j0 - 1, s.width // LN
    for step, part in enumerate(parts):
        e = lax.rem(d + s.nd - step, s.nd)
        for j in range(nj):
            for k in range(s.lz + 2):
                at = (k * nj + j) * s.rows
                v[k, e * nj + j, HY : HY + s.rows, :] = part[at : at + s.rows, :]
            for a in range(s.lz):
                at = (s.lz + 2) * nj * s.rows + (a * nj + j) * 2
                v[a + 1, e * nj + j, HY - 1 : HY, :] = part[at : at + 1, :]
                v[a + 1, e * nj + j, HY + s.rows : HY + s.rows + 1, :] = part[at + 1 : at + 2, :]
    lane = iota((8, LN), 1)
    first, last = lane == 0, lane == LN - 1
    zero = jnp.zeros((8, LN), F32)
    copies = []
    for a in range(s.lz):
        z = d * s.lz + a
        cz, above = c[z], cu[z] * c[z]
        if a > 0:
            below = cu[z - 1] * c[z - 1]
        for r in range(0, s.rows, 8):
            rows, own = slice(HY + r, HY + r + 8), slice(r, r + 8)
            x = [v[a + 1, j, rows, :] for j in range(n)]
            ahead = [pltpu.roll(w, LN - 1, 1) for w in x] + [zero]
            behind = [pltpu.roll(w, 1, 1) for w in x] + [zero]
            for j in range(n):
                k_up = above if a < s.lz - 1 else up[j, own, :]
                k_down = below if a > 0 else down[j, own, :]
                side = jnp.where(last, ahead[j + 1], ahead[j]) + jnp.where(first, behind[j - 1], behind[j])
                side += v[a + 1, j, HY + r - 1 : HY + r + 7, :] + v[a + 1, j, HY + r + 1 : HY + r + 9, :]
                g = cz * side + (k_up * v[a + 2, j, rows, :] + k_down * v[a, j, rows, :])
                u[a, own, tiles(j)] = x[j]
                defect[a, own, tiles(j)] = (f[a, own, tiles(j)] + g) - (4.0 * cz + k_up + k_down) * x[j]
        for k, (src, dst) in enumerate(((u, u_out), (defect, defect_out))):
            copies.append(pltpu.make_async_copy(src.at[a], dst.at[a], sem.at[2 * a + k]))
            copies[-1].start()
    for x in copies:
        x.wait()


def call(kernel, s, outs, scratch=(), to_hbm=False, from_hbm=False, in_vmem=False, limit=32 << 20):
    shapes = [pltpu.VMEM(o, F32) if in_vmem else jax.ShapeDtypeStruct(o, F32) for o in outs]
    spaces = [pl.BlockSpec(memory_space=m) for m in (pltpu.VMEM, pltpu.HBM)]

    def run(*args):
        total = sum(int(np.prod(a.shape)) * 4 for a in args) + sum(int(np.prod(o)) * 4 for o in outs)
        return pl.pallas_call(
            functools.partial(kernel, s),
            out_shape=shapes,
            in_specs=[spaces[from_hbm]] * len(args),
            out_specs=[spaces[to_hbm]] * len(outs),
            scratch_shapes=[pltpu.VMEM(x, F32) if isinstance(x, tuple) else x for x in scratch],
            compiler_params=pltpu.CompilerParams(vmem_limit_bytes=limit),
            cost_estimate=pl.CostEstimate(flops=4 * total, bytes_accessed=total, transcendentals=0),
        )(*args)

    return run


def shift(x, axis, by):
    n = lax.axis_size(axis)
    return lax.ppermute(x, axis, [(i, (i + by) % n) for i in range(n)])


def swap(x, odd):
    n = lax.axis_size("tile")
    to = [((k - odd) ^ 1) + odd for k in range(n)]
    return lax.ppermute(x, "tile", [(k, q if 0 <= q < n else k) for k, q in enumerate(to)])


def tables(s):
    p = np.arange(s.we)
    at = p // 4 + np.where(p >= s.wc + HX, s.w1 - s.we // 4, 0)
    down = at[:, None] == np.arange(s.w1)[None, :]
    q = np.arange(s.w1)
    k = q // 4 + np.where(q >= s.w1 - HX // 4, LN - s.w1 // 4, 0)
    used = (q < s.c1 + HX // 4) | (q >= s.w1 - HX // 4)
    spread2 = (np.arange(LN)[:, None] == k[None, :]) & used[None, :]
    r = np.arange(LN)
    down2 = (r // 4)[:, None] == (r % s.c2)[None, :]
    return [jnp.asarray(m, BF16) for m in (down.T, spread2, down2 * 0.25)]


def local(s, source_heating, material_thermal_values, layer_material, via_conductance, via_blocks):
    spread1, spread2, down2 = tables(s)
    down = pl.pallas_call(
        functools.partial(down_kernel, s),
        name="down",
        out_shape=jax.ShapeDtypeStruct((s.we, s.w1), BF16),
        compiler_params=pltpu.CompilerParams(vmem_limit_bytes=4 << 20),
        cost_estimate=pl.CostEstimate(flops=1 << 20, bytes_accessed=1 << 20, transcendentals=0),
    )()
    smem, packed = pltpu.SMEM, (s.part + 8, LN)
    sends = call(
        pack_kernel, s, [packed] * s.nd,
        [
            smem(material_thermal_values.shape, F32), smem(layer_material.shape, jnp.int32),
            smem((1, 1), F32), pltpu.VMEM((4, s.nb), jnp.int32),
            pltpu.VMEM(source_heating.shape, F32), pltpu.SemaphoreType.DMA((5,)),
        ],
        from_hbm=True, in_vmem=True, limit=VMEM - 4 * s.nd * packed[0] * packed[1],
    )(material_thermal_values, layer_material, via_conductance[None], via_blocks[0].T, source_heating)
    parts = [sends[0]] + [shift(sends[k], "die", k) for k in range(1, s.nd)]
    half = (s.nz * s.j0, HY, LN)
    one, two, prm = call(assemble_kernel, s, [half, half, (s.nd, 8, LN)])(*parts)
    f0, f1, small = (s.j0, s.re, LN), (s.j1, s.e1, LN), (s.nz, s.j1, s.r1, LN)
    fine, fine_v = (s.nz, *f0), (s.nz + 2, *f0)
    mid, mid_v = (s.nz, *f1), (s.nz + 2, *f1)
    slab, table = (s.nd * s.lz, s.nt, LN), (s.nz, 8, LN)
    up0, down0, e0, c, ic, cu, cd = call(
        coeff_fine_kernel, s, [(s.nd, *f0), (s.nd, *f0), fine, table, table, table, table]
    )(prm)
    flat, rbuf = (s.nz, s.r1, s.we), (s.nz * s.j0 * s.re, LN)
    from_two = swap(two, 1)
    from_one = swap(one, 0)
    f, v2, r1 = call(fine_first_kernel, s, [fine, fine_v, small], [fine_v, rbuf, flat])(
        from_one, from_two, one, two, up0, down0, e0, ic, cu, cd, down
    )
    up1, down1, e1, u2, l2, e2 = call(coeff_coarse_kernel, s, [(s.nd, *f1), (s.nd, *f1), mid, slab, slab, slab])(prm)

    def middle_first(r1):
        return call(
            middle_first_kernel, s,
            [mid, mid_v, (s.nd * s.nt * s.lz, LN)], [mid_v, (s.nz * 8, LN)],
        )(swap(r1, 0), r1, swap(r1, 1), up1, down1, e1, cu, cd, down2)

    def everywhere(send):
        return lax.all_to_all(send, ("die", "tile"), 0, 0, tiled=True)

    spaces = [(s.nd * s.lz, s.nt + 2 * HY, LN), (s.nz * 8, LN), (s.nz, 8, s.w1), mid_v, mid_v]
    spaces += [fine_v, fine_v, flat]
    rx, w2, send = middle_first(r1)
    levels = (u2, l2, e2, up1, down1, e1, up0, down0, e0)
    v, r1 = call(back_kernel, s, [fine_v, small], spaces + [rbuf])(
        everywhere(send), v2, f, w2, rx, *levels, cu, cd, spread2, spread1, down
    )
    rx, w2, send = middle_first(r1)
    piece = ((s.lz + 2) * (s.j0 - 1) * s.rows + 2 * s.lz * (s.j0 - 1), LN)
    sends = call(last_kernel, s, [piece] * s.nd, spaces)(
        everywhere(send), w2, rx, v, f, *levels, cu, cd, spread2, spread1
    )
    parts = [sends[0]] + [shift(sends[k], "die", k) for k in range(1, s.nd)]
    whole, columns = (s.lz, s.rows, s.width), (s.width // LN, s.rows, LN)
    own_up, own_down = call(coeff_own_kernel, s, [columns] * 2)(prm)
    scratch = [(s.lz + 2, s.width // LN, s.re, LN), whole, whole, pltpu.SemaphoreType.DMA((2 * s.lz,))]
    return tuple(call(finish_kernel, s, [whole] * 2, scratch, True)(source_heating, c, cu, own_up, own_down, *parts))


def solution(mesh):
    in_specs = (P("die", "tile", None), P(), P("die"), P("die"), P("die", None, None))
    out_specs = (P("die", "tile", None), P("die", "tile", None))

    def body(f, mat, material, conductance, blocks):
        s = Sizes(mesh.shape, f.shape, blocks.shape[1])
        return local(s, f, mat, material, conductance, blocks)

    return jax.shard_map(body, mesh=mesh, in_specs=in_specs, out_specs=out_specs, check_vma=False)
```

```python
import functools

import jax
import jax.numpy as jnp
import numpy as np
from jax import lax
from jax.experimental import pallas as pl
from jax.experimental.pallas import tpu as pltpu
from jax.sharding import PartitionSpec as P


OMEGA = 0.8
NC = 6
LN = 128
HX = 64
VMEM = 67_043_328
HY = 8
F32 = jnp.float32
BF16 = jnp.bfloat16


def iota(shape, axis):
    return lax.broadcasted_iota(jnp.int32, shape, axis)


def split_dot(x, m):
    hi = x.astype(BF16)
    lo = (x - hi.astype(F32)).astype(BF16)
    return jnp.dot(hi, m, preferred_element_type=F32) + jnp.dot(lo, m, preferred_element_type=F32)


def pair_dot(a, b):
    return lax.dot_general(a, b, (((0,), (0,)), ((), ())), preferred_element_type=F32)


class Sizes:
    def __init__(self, mesh_shape, f_shape, n_blocks):
        self.nd, self.nt = mesh_shape["die"], mesh_shape["tile"]
        self.lz, self.rows, self.width = f_shape
        self.nb = n_blocks
        self.wc = self.width // self.nd
        self.we = self.wc + LN
        self.j0 = self.we // LN
        self.nz = self.nd * self.lz
        self.re = self.rows + 2 * HY
        self.own1 = self.rows // 4
        self.r1 = self.re // 4
        self.c1 = self.wc // 4
        self.e1 = 2 * self.r1
        self.pad1 = (self.e1 - self.own1) // 2
        self.j1 = 2
        self.w1 = self.j1 * LN
        self.c2 = self.wc // 16
        self.part = self.lz * self.j0 * self.rows
        assert self.rows == 16 and self.lz == 4 and self.c1 == LN
        assert self.nd * self.c2 == LN and self.nb <= LN and self.nt <= LN and self.nt % 8 == 0


def place():
    return lax.axis_index("die"), lax.axis_index("tile")


def even():
    _, t = place()
    return lax.rem(t, 2) == 0


def tiles(j):
    return slice(j * LN, (j + 1) * LN)


def windows(lo, hi):
    return [min(r, hi - 8) for r in range(lo, hi, 8)]


def pack_kernel(s, mat_h, material_h, conductance_h, blocks_h, f_h, *refs):
    outs, (mat, material, conductance, blocks, f, sem) = refs[: s.nd], refs[s.nd :]
    pairs = [(f_h, f), (mat_h, mat), (material_h, material), (conductance_h, conductance), (blocks_h, blocks)]
    copies = [pltpu.make_async_copy(a, b, sem.at[k]) for k, (a, b) in enumerate(pairs)]
    for c in copies:
        c.start()
    for c in copies[1:]:
        c.wait()
    d, _ = place()
    lane, sub = iota((8, LN), 1), iota((8, LN), 0)
    info = jnp.where((sub == 5) & (lane == 0), conductance[0, 0], 0.0)
    for z in range(s.lz):
        info = jnp.where((sub == 4) & (lane == z), mat[material[z]], info)
    for out in outs:
        out[s.part :, :] = info
        out[s.part : s.part + 4, : s.nb] = blocks[...].astype(F32)
    copies[0].wait()
    low = iota((s.rows, LN), 1) < HX
    for step, out in enumerate(outs):
        e = lax.rem(d + step, s.nd)
        right = lax.rem(e + 1, s.nd) * s.wc
        left = lax.rem(e + s.nd - 1, s.nd) * s.wc + (s.wc - LN)

        def column(z, at):
            return f[z, :, pl.ds(pl.multiple_of(at, LN), LN)]

        for z in range(s.lz):
            for j in range(s.j0):
                at = (z * s.j0 + j) * s.rows
                if j < s.j0 - 1:
                    x = column(z, e * s.wc + j * LN)
                else:
                    x = jnp.where(low, column(z, right), column(z, left))
                out[at : at + s.rows, :] = x


def assemble_kernel(s, *refs):
    parts, (one, two, prm) = refs[: s.nd], refs[s.nd :]
    d, _ = place()
    n = s.lz * s.j0
    lower = even()
    for step, part in enumerate(parts):
        e = lax.rem(d + s.nd - step, s.nd)
        for q in range(n):
            top = part[q * s.rows : q * s.rows + HY, :]
            bot = part[q * s.rows + HY : (q + 1) * s.rows, :]
            one[n * e + q] = jnp.where(lower, bot, top)
            two[n * e + q] = jnp.where(lower, top, bot)
        prm[e] = part[s.part :, :]


def overlap(lo, size, first, past):
    return jnp.maximum(jnp.minimum(lo + size, past) - jnp.maximum(lo, first), 0.0)


def block_bounds(s, info):
    b = jnp.transpose(info)
    lane = iota((LN, 8), 1)
    col = [jnp.sum(jnp.where(lane == k, b, 0.0), axis=1, keepdims=True) for k in range(4)]
    col = [x[: s.nb] for x in col]
    return col[0], col[0] + col[2], col[1], col[1] + col[3]


def die_values(s, prm):
    lane8, sub8 = iota((8, LN), 1), iota((8, LN), 0)

    def pick(tile, row, col):
        return jnp.sum(jnp.where((lane8 == col) & (sub8 == row), tile, 0.0), keepdims=True)

    info = [prm[g] for g in range(s.nd)]
    cond = [pick(info[z // s.lz], 4, z % s.lz) for z in range(s.nz)]
    via = [pick(info[g], 5, 0) for g in range(s.nd)]
    vert = [2.0 * p * q / (p + q) for p, q in zip(cond, cond[1:] + cond[-1:])]
    return cond, vert, via, [block_bounds(s, x) for x in info]


def level_coeffs(s, level, values, via_up, via_down, scale):
    cond, vert, via, blocks = values
    d, t = place()
    size = 4**level
    n, own = (s.we, s.wc) if level == 0 else (s.w1, s.c1)
    height, nj = (s.re, s.j0) if level == 0 else (s.e1, s.j1)
    pad = HY if level == 0 else s.pad1
    halo = HX // size

    def columns(shape, axis):
        p = iota(shape, axis)
        return p, d * own + jnp.where(p >= n - halo, p - n, p)

    first = t * (s.rows // size) - pad
    row = ((first + iota((1, LN), 1)) * size).astype(F32)
    col = (columns((1, n), 1)[1] * size).astype(F32)
    rr = first + iota((height, n), 0)
    pp, cc = columns((height, n), 1)
    inside = (rr >= 0) & (rr < s.rows * s.nt // size) & (cc >= 0) & (cc < s.width // size)
    inside = jnp.where(inside & ((pp < own + halo) | (pp >= n - halo)), OMEGA, 0.0)
    via_down[0] = jnp.zeros(via_down.shape[1:], F32)
    for g in range(s.nd):
        r0, r1, c0, c1 = blocks[g]
        m = pair_dot(
            overlap(row, float(size), r0, r1).astype(BF16), overlap(col, float(size), c0, c1).astype(BF16)
        )[:height]
        top = (g + 1) * s.lz - 1
        m = m * (via[g] * (0.25**level))
        for j in range(nj):
            via_up[g, j] = m[:, tiles(j)] / cond[top]
            if g + 1 < s.nd:
                via_down[g + 1, j] = m[:, tiles(j)] / cond[top + 1]
    for z in range(s.nz):
        g, a = z // s.lz, z % s.lz
        const = 4.0
        if a < s.lz - 1:
            const = const + vert[z] * (4.0**level) / cond[z]
        if a > 0:
            const = const + vert[z - 1] * (4.0**level) / cond[z]
        for j in range(nj):
            diag = const
            if a == s.lz - 1:
                diag = diag + via_up[g, j]
            if a == 0:
                diag = diag + via_down[g, j]
            scale[z, j] = inside[:, tiles(j)] / diag


def coeff_fine_kernel(s, prm, up0, down0, e0, c, ic, cu, cd):
    values = die_values(s, prm)
    cond, vert = values[:2]
    for z in range(s.nz):
        c[z] = jnp.zeros((8, LN), F32) + cond[z]
        ic[z] = jnp.zeros((8, LN), F32) + 1.0 / cond[z]
        cu[z] = jnp.zeros((8, LN), F32) + vert[z] / cond[z]
        cd[z] = jnp.zeros((8, LN), F32) + vert[max(z - 1, 0)] / cond[z]
    level_coeffs(s, 0, values, up0, down0, e0)


def coeff_coarse_kernel(s, prm, up1, down1, e1, u2, l2, e2):
    values = die_values(s, prm)
    cond, vert, via, blocks = values
    level_coeffs(s, 1, values, up1, down1, e1)
    at = (iota((1, LN), 1) * 16).astype(F32)
    ups = []
    for z in range(s.nz):
        g = z // s.lz
        if z % s.lz < s.lz - 1:
            up = jnp.zeros((s.nt, LN), F32) + vert[z] * 256.0
        else:
            r0, r1, c0, c1 = blocks[g]
            up = pair_dot(overlap(at, 16.0, r0, r1).astype(BF16), overlap(at, 16.0, c0, c1).astype(BF16))
            up = up[: s.nt] * via[g]
        down = ups[-1] if ups else jnp.zeros((s.nt, LN), F32)
        ups.append(up)
        u2[z] = up / (cond[z] * 16.0)
        l2[z] = down / (cond[z] * 16.0)
        e2[z] = OMEGA * 16.0 * cond[z] / (64.0 * cond[z] + up + down)


class Level:
    def __init__(self, s, level, up, down, scale, cu, cd):
        self.s, self.up, self.down, self.scale, self.cu, self.cd = s, up, down, scale, cu, cd
        self.nj = (s.j0, s.j1)[level]
        self.us = 4.0**level

    def walk(self, src, f, lo, hi, emit, count=None):
        s, n = self.s, self.nj
        lane = iota((8, LN), 1)
        first, last = lane == 0, lane == LN - 1

        def group(g, carry):
            for a in range(s.lz):
                z = g * s.lz + a
                for r in windows(lo, hi):
                    rows = pl.ds(r, 8)
                    v = [src[z + 1, j, rows, :] for j in range(n)]
                    ahead = [pltpu.roll(x, LN - 1, 1) for x in v]
                    behind = [pltpu.roll(x, 1, 1) for x in v]
                    for j in range(count or n):
                        k_up = self.cu[z] * self.us if a < s.lz - 1 else self.up[g, j, rows, :]
                        k_down = self.cd[z] * self.us if a > 0 else self.down[g, j, rows, :]
                        x = jnp.where(last, ahead[(j + 1) % n], ahead[j]) + jnp.where(first, behind[j - 1], behind[j])
                        y = src[z + 1, j, pl.ds(r - 1, 8), :] + src[z + 1, j, pl.ds(r + 1, 8), :]
                        x = (f[z, j, rows, :] + x) + y
                        x = x + (k_up * src[z + 2, j, rows, :] + k_down * src[z, j, rows, :])
                        emit(z, j, rows, v[j], x, k_up, k_down)
            return carry

        lax.fori_loop(0, s.nd, group, 0)

    def sweep(self, src, dst, f, lo, hi):
        def emit(z, j, rows, v, g, *_):
            dst[z + 1, j, rows, :] = (1.0 - OMEGA) * v + self.scale[z, j, rows, :] * g

        self.walk(src, f, lo, hi, emit)

    def residual(self, src, f, lo, hi, put, count=None):
        def emit(z, j, rows, v, g, k_up, k_down):
            put(z, j, rows, g - (4.0 + k_up + k_down) * v)

        self.walk(src, f, lo, hi, emit, count)


def zero_ends(s, *bufs):
    for b in bufs:
        b[0] = jnp.zeros(b.shape[1:], F32)
        b[s.nz + 1] = jnp.zeros(b.shape[1:], F32)


def turn(a):
    return a * 2 * (HX // 4) + HX // 4


def restrict(s, level, src, f, lo, hi, down, rbuf, sums, r1, ship):
    for k in range(s.nz * s.j0):
        rbuf[k * s.re : k * s.re + 8, :] = jnp.zeros((8, LN), F32)
        rbuf[(k + 1) * s.re - 8 : (k + 1) * s.re, :] = jnp.zeros((8, LN), F32)

    def put(z, j, rows, x):
        rbuf[pl.ds((z * s.j0 + j) * s.re + rows.start, 8), :] = x

    level.residual(src, f, lo, hi, put)

    def body(z, carry):
        for j in range(s.j0):
            part = [rbuf[pl.ds((z * s.j0 + j) * s.re + k, s.r1, stride=4), :] for k in range(4)]
            sums[z, :, tiles(j)] = (part[0] + part[1]) + (part[2] + part[3])
        return carry

    lax.fori_loop(0, s.nz, body, 0)
    out = split_dot(sums[...].reshape(s.nz * s.r1, s.we), down[...])
    part = iota((s.r1, LN), 1) // (HX // 2)
    for g in range(s.nd):
        shared = jnp.zeros((s.r1, LN), F32)
        for a in range(s.lz):
            z = g * s.lz + a
            x, halo = (out[z * s.r1 : (z + 1) * s.r1, tiles(j)] for j in range(s.j1))
            r1[z, 0] = x
            r1[z, 1] = halo
            ship[z] = x
            shared = jnp.where(part == a, pltpu.roll(halo, turn(a), 1), shared)
        ship[s.nz + g] = shared


def down_kernel(s, out):
    p, q = iota((s.we, s.w1), 0), iota((s.we, s.w1), 1)
    at = p // 4 + jnp.where(p >= s.wc + HX, s.w1 - s.we // 4, 0)
    out[...] = jnp.where(at == q, 0.25, 0.0).astype(BF16)


def fine_first_kernel(s, from_one, from_two, one, two, up0, down0, e0, ic, cu, cd, down, f, v2, r1, ship, va, rbuf, sums):
    level = Level(s, 0, up0, down0, e0, cu, cd)
    lower = even()
    zero_ends(s, va, v2)

    def body(z, carry):
        for k, (a, b) in enumerate(((from_two, from_one), (two, one), (one, two), (from_one, from_two))):
            rows = slice(k * HY, (k + 1) * HY)
            for j in range(s.j0):
                q = z * s.j0 + j
                x = jnp.where(lower, a[q], b[q]) * ic[z]
                f[z, j, rows, :] = x
                va[z + 1, j, rows, :] = e0[z, j, rows, :] * x
        return carry

    lax.fori_loop(0, s.nz, body, 0)
    level.sweep(va, v2, f, 1, s.re - 1)
    restrict(s, level, v2, f, HY - 4, s.re - HY + 4, down, rbuf, sums, r1, ship)


def middle_first_kernel(s, r1a, r1, r1b, up1, down1, e1, cu, cd, down2, rx, w2, send, wa, buf):
    level = Level(s, 1, up1, down1, e1, cu, cd)
    half, own, pad = s.r1, s.own1, s.pad1
    sub = iota((half, LN), 0)
    lower = even()
    zero_ends(s, wa, w2)

    def body(g, carry):
        for a in range(s.lz):
            z = g * s.lz + a
            for j in range(s.j1):
                mid = pltpu.roll(r1[z, j], half // 2, 0)
                if j == 0:
                    p, q = r1a[z], r1b[z]
                else:
                    p, q = (pltpu.roll(x[s.nz + g], LN - turn(a), 1) for x in (r1a, r1b))
                up = jnp.where(sub >= pad, mid, jnp.where(lower, q, p))
                down = jnp.where(sub < own - (half - pad), mid, jnp.where(lower, p, q))
                rx[z, j, :half, :] = up
                rx[z, j, half:, :] = down
                wa[z + 1, j, :half, :] = e1[z, j, :half, :] * up
                wa[z + 1, j, half:, :] = e1[z, j, half:, :] * down
        return carry

    lax.fori_loop(0, s.nd, body, 0)
    level.sweep(wa, w2, rx, pad - 4, pad + own + 4)

    def put(z, j, rows, x):
        buf[pl.ds(pl.multiple_of(z * 8, 8), 8), :] = x

    level.residual(w2, rx, pad - 2, pad + own + 2, put, 1)
    sub8, group = iota((8, LN), 0), iota((8, LN), 1) // s.c2
    tile = jnp.zeros((8, LN), F32)
    for h in range(s.nz // 8):
        part = [buf[pl.ds(64 * h + 2 + k, 8, stride=8), :] for k in range(own)]
        x = split_dot((part[0] + part[1]) + (part[2] + part[3]), down2[...])
        y = pltpu.roll(x, 4, 0)
        for g in (2 * h, 2 * h + 1):
            tile = jnp.where(group == g, jnp.where((sub8 < 4) == (g % 2 == 0), x, y), tile)
    for k in range(s.nd * s.nt * s.lz // 8):
        send[8 * k : 8 * k + 8, :] = tile


def coarse(s, got, u2, l2, e2, cs):
    lane, t = iota((s.nt, LN), 1), iota((s.nt, LN), 0)
    rhs, v = [], []
    for z in range(s.nz):
        g, a = z // s.lz, z % s.lz
        r = jnp.zeros((s.nt, LN), F32)
        for e in range(s.nd):
            x = got[pl.ds(e * s.nt * s.lz + a, s.nt, stride=s.lz), :]
            x = pltpu.roll(x, (e - g) * s.c2 % LN, 1) if e != g else x
            r = jnp.where(lane // s.c2 == e, x, r)
        rhs.append(r)
        v.append(e2[z] * r)

    def body(_, v):
        new = []
        for z in range(s.nz):
            w = v[z]
            side = jnp.where(lane == LN - 1, 0.0, pltpu.roll(w, LN - 1, 1))
            side += jnp.where(lane == 0, 0.0, pltpu.roll(w, 1, 1))
            side += jnp.where(t == s.nt - 1, 0.0, pltpu.roll(w, s.nt - 1, 0))
            side += jnp.where(t == 0, 0.0, pltpu.roll(w, 1, 0))
            g = rhs[z] + side
            if z < s.nz - 1:
                g += u2[z] * v[z + 1]
            if z > 0:
                g += l2[z] * v[z - 1]
            new.append((1.0 - OMEGA) * w + e2[z] * g)
        return tuple(new)

    v = lax.fori_loop(0, NC - 1, body, tuple(v))
    for z in range(s.nz):
        cs[z, :HY, :] = jnp.zeros((HY, LN), F32)
        cs[z, HY + s.nt :, :] = jnp.zeros((HY, LN), F32)
        cs[z, HY : HY + s.nt, :] = v[z]


def middle_last(s, level, cs, spread2, w2, rx, comp, wide, wa, wb):
    d, t = place()
    upper = iota((8, LN), 0) < 4
    zero_ends(s, wa, wb)
    for z in range(s.nz):
        comp[8 * z : 8 * z + 8, :] = pltpu.roll(cs[z, pl.ds(HY - 1 + t, 8), :], lax.rem(LN - d * s.c2, LN), 1)
    wide[...] = split_dot(comp[...], spread2[...]).reshape(wide.shape)

    def body(z, carry):
        x = [[wide[z, k : k + 1, tiles(j)] for k in range(3)] for j in range(s.j1)]
        for k in range(2):
            rows = slice(s.pad1 - 4 + 4 * k, s.pad1 + 4 + 4 * k)
            for j in range(s.j1):
                y = w2[z + 1, j, rows, :] + jnp.where(upper, x[j][k], x[j][k + 1])
                wa[z + 1, j, rows, :] = jnp.where(level.scale[z, j, rows, :] > 0.0, y, 0.0)
        return carry

    lax.fori_loop(0, s.nz, body, 0)
    level.sweep(wa, wb, rx, s.pad1 - 3, s.pad1 + s.own1 + 3)
    level.sweep(wb, wa, rx, s.pad1 - 2, s.pad1 + s.own1 + 2)


def correct_fine(s, w, v, spread1, wide, dst):
    rows = slice(s.pad1 - 2, s.pad1 + s.own1 + 2)
    lhs = jnp.concatenate([w[1 : s.nz + 1, j, rows, :].reshape(s.nz * s.r1, LN) for j in range(s.j1)], axis=1)
    wide[...] = split_dot(lhs, spread1[...]).reshape(wide.shape)
    upper = iota((8, LN), 0) < 4

    def body(z, carry):
        for k in range(s.r1 // 2):
            rows = slice(8 * k, 8 * k + 8)
            for j in range(s.j0):
                x = [wide[z, 2 * k + i : 2 * k + i + 1, tiles(j)] for i in range(2)]
                dst[z + 1, j, rows, :] = v[z + 1, j, rows, :] + jnp.where(upper, x[0], x[1])
        return carry

    lax.fori_loop(0, s.nz, body, 0)


def back_kernel(
    s, got, v2, f, w2, rx,
    u2, l2, e2, up1, down1, e1, up0, down0, e0, cu, cd, spread2, spread1, down,
    v, r1, ship, cs, comp, wide2, wa, wb, va, vb, wide, rbuf,
):
    fine = Level(s, 0, up0, down0, e0, cu, cd)
    middle = Level(s, 1, up1, down1, e1, cu, cd)
    zero_ends(s, va, vb, v)
    coarse(s, got, u2, l2, e2, cs)
    middle_last(s, middle, cs, spread2, w2, rx, comp, wide2, wa, wb)
    correct_fine(s, wa, v2, spread1, wide, va)
    fine.sweep(va, vb, f, 2, s.re - 2)
    fine.sweep(vb, va, f, 3, s.re - 3)
    fine.sweep(va, vb, f, 4, s.re - 4)
    fine.sweep(vb, v, f, 5, s.re - 5)
    restrict(s, fine, v, f, HY, HY + s.rows, down, rbuf, wide, r1, ship)


def last_kernel(
    s, got, w2, rx, v2, f, u2, l2, e2, up1, down1, e1, up0, down0, e0, cu, cd, spread2, spread1, *refs,
):
    outs, (cs, comp, wide2, wa, wb, va, vb, wide) = refs[: s.nd], refs[s.nd :]
    fine = Level(s, 0, up0, down0, e0, cu, cd)
    middle = Level(s, 1, up1, down1, e1, cu, cd)
    d, _ = place()
    zero_ends(s, va, vb)
    coarse(s, got, u2, l2, e2, cs)
    middle_last(s, middle, cs, spread2, w2, rx, comp, wide2, wa, wb)
    correct_fine(s, wa, v2, spread1, wide, va)
    fine.sweep(va, vb, f, HY - 2, HY + s.rows + 2)
    fine.sweep(vb, va, f, HY - 1, HY + s.rows + 1)

    nj = s.j0 - 1
    for step, out in enumerate(outs):
        e = lax.rem(d + step, s.nd)
        for k in range(s.lz + 2):
            for j in range(nj):
                at = (k * nj + j) * s.rows
                out[at : at + s.rows, :] = va[s.lz * e + k, j, HY : HY + s.rows, :]
        for a in range(s.lz):
            for j in range(nj):
                at = (s.lz + 2) * nj * s.rows + (a * nj + j) * 2
                out[at : at + 1, :] = va[s.lz * e + a + 1, j, HY - 1 : HY, :]
                out[at + 1 : at + 2, :] = va[s.lz * e + a + 1, j, HY + s.rows : HY + s.rows + 1, :]


def coeff_own_kernel(s, prm, up, down):
    d, t = place()
    lane8, sub8 = iota((8, LN), 1), iota((8, LN), 0)
    row = (t * s.rows + iota((1, LN), 1)).astype(F32)
    col = iota((1, s.width), 1).astype(F32)
    for k, out in enumerate((up, down)):
        info = prm[lax.rem(d + s.nd - k, s.nd)]
        via = jnp.sum(jnp.where((lane8 == 0) & (sub8 == 5), info, 0.0), keepdims=True)
        if k == 1:
            via = via * (d > 0).astype(F32)
        r0, r1, c0, c1 = block_bounds(s, info)
        m = pair_dot(overlap(row, 1.0, r0, r1).astype(BF16), overlap(col, 1.0, c0, c1).astype(BF16))
        for j in range(s.width // LN):
            out[j] = m[: s.rows, tiles(j)] * via


def finish_kernel(s, f, c, cu, up, down, *refs):
    parts, (u_out, defect_out, v, u, defect, sem) = refs[: s.nd], refs[s.nd :]
    d, _ = place()
    nj, n = s.j0 - 1, s.width // LN
    for step, part in enumerate(parts):
        e = lax.rem(d + s.nd - step, s.nd)
        for j in range(nj):
            for k in range(s.lz + 2):
                at = (k * nj + j) * s.rows
                v[k, e * nj + j, HY : HY + s.rows, :] = part[at : at + s.rows, :]
            for a in range(s.lz):
                at = (s.lz + 2) * nj * s.rows + (a * nj + j) * 2
                v[a + 1, e * nj + j, HY - 1 : HY, :] = part[at : at + 1, :]
                v[a + 1, e * nj + j, HY + s.rows : HY + s.rows + 1, :] = part[at + 1 : at + 2, :]
    lane = iota((8, LN), 1)
    first, last = lane == 0, lane == LN - 1
    zero = jnp.zeros((8, LN), F32)
    copies = []
    for a in range(s.lz):
        z = d * s.lz + a
        cz, above = c[z], cu[z] * c[z]
        if a > 0:
            below = cu[z - 1] * c[z - 1]
        for r in range(0, s.rows, 8):
            rows, own = slice(HY + r, HY + r + 8), slice(r, r + 8)
            x = [v[a + 1, j, rows, :] for j in range(n)]
            ahead = [pltpu.roll(w, LN - 1, 1) for w in x] + [zero]
            behind = [pltpu.roll(w, 1, 1) for w in x] + [zero]
            for j in range(n):
                k_up = above if a < s.lz - 1 else up[j, own, :]
                k_down = below if a > 0 else down[j, own, :]
                side = jnp.where(last, ahead[j + 1], ahead[j]) + jnp.where(first, behind[j - 1], behind[j])
                side += v[a + 1, j, HY + r - 1 : HY + r + 7, :] + v[a + 1, j, HY + r + 1 : HY + r + 9, :]
                g = cz * side + (k_up * v[a + 2, j, rows, :] + k_down * v[a, j, rows, :])
                u[a, own, tiles(j)] = x[j]
                defect[a, own, tiles(j)] = (f[a, own, tiles(j)] + g) - (4.0 * cz + k_up + k_down) * x[j]
        for k, (src, dst) in enumerate(((u, u_out), (defect, defect_out))):
            copies.append(pltpu.make_async_copy(src.at[a], dst.at[a], sem.at[2 * a + k]))
            copies[-1].start()
    for x in copies:
        x.wait()


def call(kernel, s, outs, scratch=(), to_hbm=False, from_hbm=False, in_vmem=False, limit=32 << 20):
    shapes = [pltpu.VMEM(o, F32) if in_vmem else jax.ShapeDtypeStruct(o, F32) for o in outs]
    spaces = [pl.BlockSpec(memory_space=m) for m in (pltpu.VMEM, pltpu.HBM)]

    def run(*args):
        total = sum(int(np.prod(a.shape)) * 4 for a in args) + sum(int(np.prod(o)) * 4 for o in outs)
        return pl.pallas_call(
            functools.partial(kernel, s),
            out_shape=shapes,
            in_specs=[spaces[from_hbm]] * len(args),
            out_specs=[spaces[to_hbm]] * len(outs),
            scratch_shapes=[pltpu.VMEM(x, F32) if isinstance(x, tuple) else x for x in scratch],
            compiler_params=pltpu.CompilerParams(vmem_limit_bytes=limit),
            cost_estimate=pl.CostEstimate(flops=4 * total, bytes_accessed=total, transcendentals=0),
        )(*args)

    return run


def shift(x, axis, by):
    n = lax.axis_size(axis)
    return lax.ppermute(x, axis, [(i, (i + by) % n) for i in range(n)])


def swap(x, odd):
    n = lax.axis_size("tile")
    to = [((k - odd) ^ 1) + odd for k in range(n)]
    return lax.ppermute(x, "tile", [(k, q if 0 <= q < n else k) for k, q in enumerate(to)])


def tables(s):
    p = np.arange(s.we)
    at = p // 4 + np.where(p >= s.wc + HX, s.w1 - s.we // 4, 0)
    down = at[:, None] == np.arange(s.w1)[None, :]
    q = np.arange(s.w1)
    k = q // 4 + np.where(q >= s.w1 - HX // 4, LN - s.w1 // 4, 0)
    used = (q < s.c1 + HX // 4) | (q >= s.w1 - HX // 4)
    spread2 = (np.arange(LN)[:, None] == k[None, :]) & used[None, :]
    r = np.arange(LN)
    down2 = (r // 4)[:, None] == (r % s.c2)[None, :]
    return [jnp.asarray(m, BF16) for m in (down.T, spread2, down2 * 0.25)]


def local(s, source_heating, material_thermal_values, layer_material, via_conductance, via_blocks):
    spread1, spread2, down2 = tables(s)
    down = pl.pallas_call(
        functools.partial(down_kernel, s),
        name="down",
        out_shape=jax.ShapeDtypeStruct((s.we, s.w1), BF16),
        compiler_params=pltpu.CompilerParams(vmem_limit_bytes=4 << 20),
        cost_estimate=pl.CostEstimate(flops=1 << 20, bytes_accessed=1 << 20, transcendentals=0),
    )()
    smem, packed = pltpu.SMEM, (s.part + 8, LN)
    sends = call(
        pack_kernel, s, [packed] * s.nd,
        [
            smem(material_thermal_values.shape, F32), smem(layer_material.shape, jnp.int32),
            smem((1, 1), F32), pltpu.VMEM((4, s.nb), jnp.int32),
            pltpu.VMEM(source_heating.shape, F32), pltpu.SemaphoreType.DMA((5,)),
        ],
        from_hbm=True, in_vmem=True, limit=VMEM - 4 * s.nd * packed[0] * packed[1],
    )(material_thermal_values, layer_material, via_conductance[None], via_blocks[0].T, source_heating)
    parts = [sends[0]] + [shift(sends[k], "die", k) for k in range(1, s.nd)]
    half = (s.nz * s.j0, HY, LN)
    one, two, prm = call(assemble_kernel, s, [half, half, (s.nd, 8, LN)])(*parts)
    f0, f1, small = (s.j0, s.re, LN), (s.j1, s.e1, LN), (s.nz, s.j1, s.r1, LN)
    fine, fine_v = (s.nz, *f0), (s.nz + 2, *f0)
    mid, mid_v = (s.nz, *f1), (s.nz + 2, *f1)
    slab, table = (s.nd * s.lz, s.nt, LN), (s.nz, 8, LN)
    up0, down0, e0, c, ic, cu, cd = call(
        coeff_fine_kernel, s, [(s.nd, *f0), (s.nd, *f0), fine, table, table, table, table]
    )(prm)
    shared = (s.nz + s.nd, s.r1, LN)
    flat, rbuf = (s.nz, s.r1, s.we), (s.nz * s.j0 * s.re, LN)
    from_two = swap(two, 1)
    from_one = swap(one, 0)
    f, v2, r1, ship = call(fine_first_kernel, s, [fine, fine_v, small, shared], [fine_v, rbuf, flat])(
        from_one, from_two, one, two, up0, down0, e0, ic, cu, cd, down
    )
    up1, down1, e1, u2, l2, e2 = call(coeff_coarse_kernel, s, [(s.nd, *f1), (s.nd, *f1), mid, slab, slab, slab])(prm)

    def middle_first(r1, ship):
        return call(
            middle_first_kernel, s,
            [mid, mid_v, (s.nd * s.nt * s.lz, LN)], [mid_v, (s.nz * 8, LN)],
        )(swap(ship, 0), r1, swap(ship, 1), up1, down1, e1, cu, cd, down2)

    def everywhere(send):
        return lax.all_to_all(send, ("die", "tile"), 0, 0, tiled=True)

    spaces = [(s.nd * s.lz, s.nt + 2 * HY, LN), (s.nz * 8, LN), (s.nz, 8, s.w1), mid_v, mid_v]
    spaces += [fine_v, fine_v, flat]
    rx, w2, send = middle_first(r1, ship)
    levels = (u2, l2, e2, up1, down1, e1, up0, down0, e0)
    v, r1, ship = call(back_kernel, s, [fine_v, small, shared], spaces + [rbuf])(
        everywhere(send), v2, f, w2, rx, *levels, cu, cd, spread2, spread1, down
    )
    rx, w2, send = middle_first(r1, ship)
    piece = ((s.lz + 2) * (s.j0 - 1) * s.rows + 2 * s.lz * (s.j0 - 1), LN)
    sends = call(last_kernel, s, [piece] * s.nd, spaces)(
        everywhere(send), w2, rx, v, f, *levels, cu, cd, spread2, spread1
    )
    parts = [sends[0]] + [shift(sends[k], "die", k) for k in range(1, s.nd)]
    whole, columns = (s.lz, s.rows, s.width), (s.width // LN, s.rows, LN)
    own_up, own_down = call(coeff_own_kernel, s, [columns] * 2)(prm)
    scratch = [(s.lz + 2, s.width // LN, s.re, LN), whole, whole, pltpu.SemaphoreType.DMA((2 * s.lz,))]
    return tuple(call(finish_kernel, s, [whole] * 2, scratch, True)(source_heating, c, cu, own_up, own_down, *parts))


def solution(mesh):
    in_specs = (P("die", "tile", None), P(), P("die"), P("die"), P("die", None, None))
    out_specs = (P("die", "tile", None), P("die", "tile", None))

    def body(f, mat, material, conductance, blocks):
        s = Sizes(mesh.shape, f.shape, blocks.shape[1])
        return local(s, f, mat, material, conductance, blocks)

    return jax.shard_map(body, mesh=mesh, in_specs=in_specs, out_specs=out_specs, check_vma=False)
```

```python
import functools

import jax
import jax.numpy as jnp
import numpy as np
from jax import lax
from jax.experimental import pallas as pl
from jax.experimental.pallas import tpu as pltpu
from jax.sharding import PartitionSpec as P


OMEGA = 0.8
NC = 6
LN = 128
HX = 64
VMEM = 67_043_328
HY = 8
F32 = jnp.float32
BF16 = jnp.bfloat16


def iota(shape, axis):
    return lax.broadcasted_iota(jnp.int32, shape, axis)


def split_dot(x, m):
    hi = x.astype(BF16)
    lo = (x - hi.astype(F32)).astype(BF16)
    return jnp.dot(hi, m, preferred_element_type=F32) + jnp.dot(lo, m, preferred_element_type=F32)


def pair_dot(a, b):
    return lax.dot_general(a, b, (((0,), (0,)), ((), ())), preferred_element_type=F32)


class Sizes:
    def __init__(self, mesh_shape, f_shape, n_blocks):
        self.nd, self.nt = mesh_shape["die"], mesh_shape["tile"]
        self.lz, self.rows, self.width = f_shape
        self.nb = n_blocks
        self.wc = self.width // self.nd
        self.we = self.wc + LN
        self.j0 = self.we // LN
        self.nz = self.nd * self.lz
        self.re = self.rows + 2 * HY
        self.own1 = self.rows // 4
        self.r1 = self.re // 4
        self.c1 = self.wc // 4
        self.e1 = 2 * self.r1
        self.pad1 = (self.e1 - self.own1) // 2
        self.j1 = 2
        self.w1 = self.j1 * LN
        self.c2 = self.wc // 16
        self.part = self.lz * self.j0 * self.rows
        assert self.rows == 16 and self.lz == 4 and self.c1 == LN
        assert self.nd * self.c2 == LN and self.nb <= LN and self.nt <= LN and self.nt % 8 == 0


def place():
    return lax.axis_index("die"), lax.axis_index("tile")


def even():
    _, t = place()
    return lax.rem(t, 2) == 0


def tiles(j):
    return slice(j * LN, (j + 1) * LN)


def windows(lo, hi):
    return [min(r, hi - 8) for r in range(lo, hi, 8)]


def pack_kernel(s, mat_h, material_h, conductance_h, blocks_h, f_h, *refs):
    outs, (mat, material, conductance, blocks, f, sem) = refs[: s.nd], refs[s.nd :]
    pairs = [(f_h.at[z], f.at[z]) for z in range(s.lz)]
    pairs += [(mat_h, mat), (material_h, material), (conductance_h, conductance), (blocks_h, blocks)]
    copies = [pltpu.make_async_copy(a, b, sem.at[k]) for k, (a, b) in enumerate(pairs)]
    for c in copies:
        c.start()
    for c in copies[s.lz :]:
        c.wait()
    d, _ = place()
    lane, sub = iota((8, LN), 1), iota((8, LN), 0)
    info = jnp.where((sub == 5) & (lane == 0), conductance[0, 0], 0.0)
    for z in range(s.lz):
        info = jnp.where((sub == 4) & (lane == z), mat[material[z]], info)
    for out in outs:
        out[s.part :, :] = info
        out[s.part : s.part + 4, : s.nb] = blocks[...].astype(F32)
    low = iota((s.rows, LN), 1) < HX
    for z in range(s.lz):
        copies[z].wait()
        for step, out in enumerate(outs):
            e = lax.rem(d + step, s.nd)
            right = lax.rem(e + 1, s.nd) * s.wc
            left = lax.rem(e + s.nd - 1, s.nd) * s.wc + (s.wc - LN)
            column = lambda at: f[z, :, pl.ds(pl.multiple_of(at, LN), LN)]
            for j in range(s.j0):
                at = (z * s.j0 + j) * s.rows
                if j < s.j0 - 1:
                    x = column(e * s.wc + j * LN)
                else:
                    x = jnp.where(low, column(right), column(left))
                out[at : at + s.rows, :] = x


def assemble_kernel(s, *refs):
    parts, (one, two, prm) = refs[: s.nd], refs[s.nd :]
    d, _ = place()
    n = s.lz * s.j0
    lower = even()
    for step, part in enumerate(parts):
        e = lax.rem(d + s.nd - step, s.nd)
        for q in range(n):
            top = part[q * s.rows : q * s.rows + HY, :]
            bot = part[q * s.rows + HY : (q + 1) * s.rows, :]
            one[n * e + q] = jnp.where(lower, bot, top)
            two[n * e + q] = jnp.where(lower, top, bot)
        prm[e] = part[s.part :, :]


def overlap(lo, size, first, past):
    return jnp.maximum(jnp.minimum(lo + size, past) - jnp.maximum(lo, first), 0.0)


def block_bounds(s, info):
    b = jnp.transpose(info)
    lane = iota((LN, 8), 1)
    col = [jnp.sum(jnp.where(lane == k, b, 0.0), axis=1, keepdims=True) for k in range(4)]
    col = [x[: s.nb] for x in col]
    return col[0], col[0] + col[2], col[1], col[1] + col[3]


def die_values(s, prm):
    lane8, sub8 = iota((8, LN), 1), iota((8, LN), 0)

    def pick(tile, row, col):
        return jnp.sum(jnp.where((lane8 == col) & (sub8 == row), tile, 0.0), keepdims=True)

    info = [prm[g] for g in range(s.nd)]
    cond = [pick(info[z // s.lz], 4, z % s.lz) for z in range(s.nz)]
    via = [pick(info[g], 5, 0) for g in range(s.nd)]
    vert = [2.0 * p * q / (p + q) for p, q in zip(cond, cond[1:] + cond[-1:])]
    return cond, vert, via, [block_bounds(s, x) for x in info]


def level_coeffs(s, level, values, via_up, via_down, scale):
    cond, vert, via, blocks = values
    d, t = place()
    size = 4**level
    n, own = (s.we, s.wc) if level == 0 else (s.w1, s.c1)
    height, nj = (s.re, s.j0) if level == 0 else (s.e1, s.j1)
    pad = HY if level == 0 else s.pad1
    halo = HX // size

    def columns(shape, axis):
        p = iota(shape, axis)
        return p, d * own + jnp.where(p >= n - halo, p - n, p)

    first = t * (s.rows // size) - pad
    row = ((first + iota((1, LN), 1)) * size).astype(F32)
    col = (columns((1, n), 1)[1] * size).astype(F32)
    rr = first + iota((height, n), 0)
    pp, cc = columns((height, n), 1)
    inside = (rr >= 0) & (rr < s.rows * s.nt // size) & (cc >= 0) & (cc < s.width // size)
    inside = jnp.where(inside & ((pp < own + halo) | (pp >= n - halo)), OMEGA, 0.0)
    via_down[0] = jnp.zeros(via_down.shape[1:], F32)
    for g in range(s.nd):
        r0, r1, c0, c1 = blocks[g]
        m = pair_dot(
            overlap(row, float(size), r0, r1).astype(BF16), overlap(col, float(size), c0, c1).astype(BF16)
        )[:height]
        top = (g + 1) * s.lz - 1
        m = m * (via[g] * (0.25**level))
        for j in range(nj):
            via_up[g, j] = m[:, tiles(j)] / cond[top]
            if g + 1 < s.nd:
                via_down[g + 1, j] = m[:, tiles(j)] / cond[top + 1]
    for z in range(s.nz):
        g, a = z // s.lz, z % s.lz
        const = 4.0
        if a < s.lz - 1:
            const = const + vert[z] * (4.0**level) / cond[z]
        if a > 0:
            const = const + vert[z - 1] * (4.0**level) / cond[z]
        for j in range(nj):
            diag = const
            if a == s.lz - 1:
                diag = diag + via_up[g, j]
            if a == 0:
                diag = diag + via_down[g, j]
            scale[z, j] = inside[:, tiles(j)] / diag


def coeff_fine_kernel(s, prm, up0, down0, e0, c, ic, cu, cd):
    values = die_values(s, prm)
    cond, vert = values[:2]
    for z in range(s.nz):
        c[z] = jnp.zeros((8, LN), F32) + cond[z]
        ic[z] = jnp.zeros((8, LN), F32) + 1.0 / cond[z]
        cu[z] = jnp.zeros((8, LN), F32) + vert[z] / cond[z]
        cd[z] = jnp.zeros((8, LN), F32) + vert[max(z - 1, 0)] / cond[z]
    level_coeffs(s, 0, values, up0, down0, e0)


def coeff_coarse_kernel(s, prm, up1, down1, e1, u2, l2, e2):
    values = die_values(s, prm)
    cond, vert, via, blocks = values
    level_coeffs(s, 1, values, up1, down1, e1)
    at = (iota((1, LN), 1) * 16).astype(F32)
    ups = []
    for z in range(s.nz):
        g = z // s.lz
        if z % s.lz < s.lz - 1:
            up = jnp.zeros((s.nt, LN), F32) + vert[z] * 256.0
        else:
            r0, r1, c0, c1 = blocks[g]
            up = pair_dot(overlap(at, 16.0, r0, r1).astype(BF16), overlap(at, 16.0, c0, c1).astype(BF16))
            up = up[: s.nt] * via[g]
        down = ups[-1] if ups else jnp.zeros((s.nt, LN), F32)
        ups.append(up)
        u2[z] = up / (cond[z] * 16.0)
        l2[z] = down / (cond[z] * 16.0)
        e2[z] = OMEGA * 16.0 * cond[z] / (64.0 * cond[z] + up + down)


class Level:
    def __init__(self, s, level, up, down, scale, cu, cd):
        self.s, self.up, self.down, self.scale, self.cu, self.cd = s, up, down, scale, cu, cd
        self.nj = (s.j0, s.j1)[level]
        self.us = 4.0**level

    def walk(self, src, f, lo, hi, emit, count=None):
        s, n = self.s, self.nj
        lane = iota((8, LN), 1)
        first, last = lane == 0, lane == LN - 1

        def group(g, carry):
            for a in range(s.lz):
                z = g * s.lz + a
                for r in windows(lo, hi):
                    rows = pl.ds(r, 8)
                    v = [src[z + 1, j, rows, :] for j in range(n)]
                    ahead = [pltpu.roll(x, LN - 1, 1) for x in v]
                    behind = [pltpu.roll(x, 1, 1) for x in v]
                    for j in range(count or n):
                        k_up = self.cu[z] * self.us if a < s.lz - 1 else self.up[g, j, rows, :]
                        k_down = self.cd[z] * self.us if a > 0 else self.down[g, j, rows, :]
                        x = jnp.where(last, ahead[(j + 1) % n], ahead[j]) + jnp.where(first, behind[j - 1], behind[j])
                        y = src[z + 1, j, pl.ds(r - 1, 8), :] + src[z + 1, j, pl.ds(r + 1, 8), :]
                        x = (f[z, j, rows, :] + x) + y
                        x = x + (k_up * src[z + 2, j, rows, :] + k_down * src[z, j, rows, :])
                        emit(z, j, rows, v[j], x, k_up, k_down)
            return carry

        lax.fori_loop(0, s.nd, group, 0, unroll=2)

    def sweep(self, src, dst, f, lo, hi):
        def emit(z, j, rows, v, g, *_):
            dst[z + 1, j, rows, :] = (1.0 - OMEGA) * v + self.scale[z, j, rows, :] * g

        self.walk(src, f, lo, hi, emit)

    def residual(self, src, f, lo, hi, put, count=None):
        def emit(z, j, rows, v, g, k_up, k_down):
            put(z, j, rows, g - (4.0 + k_up + k_down) * v)

        self.walk(src, f, lo, hi, emit, count)


def zero_ends(s, *bufs):
    for b in bufs:
        b[0] = jnp.zeros(b.shape[1:], F32)
        b[s.nz + 1] = jnp.zeros(b.shape[1:], F32)


def turn(a):
    return a * 2 * (HX // 4) + HX // 4


def restrict(s, level, src, f, lo, hi, down, rbuf, sums, r1, ship):
    for k in range(s.nz * s.j0):
        rbuf[k * s.re : k * s.re + 8, :] = jnp.zeros((8, LN), F32)
        rbuf[(k + 1) * s.re - 8 : (k + 1) * s.re, :] = jnp.zeros((8, LN), F32)

    def put(z, j, rows, x):
        rbuf[pl.ds((z * s.j0 + j) * s.re + rows.start, 8), :] = x

    level.residual(src, f, lo, hi, put)

    def body(z, carry):
        for j in range(s.j0):
            part = [rbuf[pl.ds((z * s.j0 + j) * s.re + k, s.r1, stride=4), :] for k in range(4)]
            sums[z, :, tiles(j)] = (part[0] + part[1]) + (part[2] + part[3])
        return carry

    lax.fori_loop(0, s.nz, body, 0)
    out = split_dot(sums[...].reshape(s.nz * s.r1, s.we), down[...])
    part = iota((s.r1, LN), 1) // (HX // 2)
    for g in range(s.nd):
        shared = jnp.zeros((s.r1, LN), F32)
        for a in range(s.lz):
            z = g * s.lz + a
            x, halo = (out[z * s.r1 : (z + 1) * s.r1, tiles(j)] for j in range(s.j1))
            r1[z, 0] = x
            r1[z, 1] = halo
            ship[z] = x
            shared = jnp.where(part == a, pltpu.roll(halo, turn(a), 1), shared)
        ship[s.nz + g] = shared


def down_kernel(s, out):
    p, q = iota((s.we, s.w1), 0), iota((s.we, s.w1), 1)
    at = p // 4 + jnp.where(p >= s.wc + HX, s.w1 - s.we // 4, 0)
    out[...] = jnp.where(at == q, 0.25, 0.0).astype(BF16)


def fine_first_kernel(s, from_one, from_two, one, two, up0, down0, e0, ic, cu, cd, down, f, v2, r1, ship, va, rbuf, sums):
    level = Level(s, 0, up0, down0, e0, cu, cd)
    lower = even()
    zero_ends(s, va, v2)

    def body(z, carry):
        for k, (a, b) in enumerate(((from_two, from_one), (two, one), (one, two), (from_one, from_two))):
            rows = slice(k * HY, (k + 1) * HY)
            for j in range(s.j0):
                q = z * s.j0 + j
                x = jnp.where(lower, a[q], b[q]) * ic[z]
                f[z, j, rows, :] = x
                va[z + 1, j, rows, :] = e0[z, j, rows, :] * x
        return carry

    lax.fori_loop(0, s.nz, body, 0)
    level.sweep(va, v2, f, 1, s.re - 1)
    restrict(s, level, v2, f, HY - 4, s.re - HY + 4, down, rbuf, sums, r1, ship)


def middle_first_kernel(s, r1a, r1, r1b, up1, down1, e1, cu, cd, down2, rx, w2, send, wa, buf):
    level = Level(s, 1, up1, down1, e1, cu, cd)
    half, own, pad = s.r1, s.own1, s.pad1
    sub = iota((half, LN), 0)
    lower = even()
    zero_ends(s, wa, w2)

    def body(g, carry):
        for a in range(s.lz):
            z = g * s.lz + a
            for j in range(s.j1):
                mid = pltpu.roll(r1[z, j], half // 2, 0)
                if j == 0:
                    p, q = r1a[z], r1b[z]
                else:
                    p, q = (pltpu.roll(x[s.nz + g], LN - turn(a), 1) for x in (r1a, r1b))
                up = jnp.where(sub >= pad, mid, jnp.where(lower, q, p))
                down = jnp.where(sub < own - (half - pad), mid, jnp.where(lower, p, q))
                rx[z, j, :half, :] = up
                rx[z, j, half:, :] = down
                wa[z + 1, j, :half, :] = e1[z, j, :half, :] * up
                wa[z + 1, j, half:, :] = e1[z, j, half:, :] * down
        return carry

    lax.fori_loop(0, s.nd, body, 0)
    level.sweep(wa, w2, rx, pad - 4, pad + own + 4)

    def put(z, j, rows, x):
        buf[pl.ds(pl.multiple_of(z * 8, 8), 8), :] = x

    level.residual(w2, rx, pad - 2, pad + own + 2, put, 1)
    sub8, group = iota((8, LN), 0), iota((8, LN), 1) // s.c2
    tile = jnp.zeros((8, LN), F32)
    for h in range(s.nz // 8):
        part = [buf[pl.ds(64 * h + 2 + k, 8, stride=8), :] for k in range(own)]
        x = split_dot((part[0] + part[1]) + (part[2] + part[3]), down2[...])
        y = pltpu.roll(x, 4, 0)
        for g in (2 * h, 2 * h + 1):
            tile = jnp.where(group == g, jnp.where((sub8 < 4) == (g % 2 == 0), x, y), tile)
    for k in range(s.nd * s.nt * s.lz // 8):
        send[8 * k : 8 * k + 8, :] = tile


def coarse(s, got, u2, l2, e2, cs):
    lane, t = iota((s.nt, LN), 1), iota((s.nt, LN), 0)
    rhs, v = [], []
    for z in range(s.nz):
        g, a = z // s.lz, z % s.lz
        r = jnp.zeros((s.nt, LN), F32)
        for e in range(s.nd):
            x = got[pl.ds(e * s.nt * s.lz + a, s.nt, stride=s.lz), :]
            x = pltpu.roll(x, (e - g) * s.c2 % LN, 1) if e != g else x
            r = jnp.where(lane // s.c2 == e, x, r)
        rhs.append(r)
        v.append(e2[z] * r)

    def body(_, v):
        new = []
        for z in range(s.nz):
            w = v[z]
            side = jnp.where(lane == LN - 1, 0.0, pltpu.roll(w, LN - 1, 1))
            side += jnp.where(lane == 0, 0.0, pltpu.roll(w, 1, 1))
            side += jnp.where(t == s.nt - 1, 0.0, pltpu.roll(w, s.nt - 1, 0))
            side += jnp.where(t == 0, 0.0, pltpu.roll(w, 1, 0))
            g = rhs[z] + side
            if z < s.nz - 1:
                g += u2[z] * v[z + 1]
            if z > 0:
                g += l2[z] * v[z - 1]
            new.append((1.0 - OMEGA) * w + e2[z] * g)
        return tuple(new)

    v = lax.fori_loop(0, NC - 1, body, tuple(v))
    for z in range(s.nz):
        cs[z, :HY, :] = jnp.zeros((HY, LN), F32)
        cs[z, HY + s.nt :, :] = jnp.zeros((HY, LN), F32)
        cs[z, HY : HY + s.nt, :] = v[z]


def middle_last(s, level, cs, spread2, w2, rx, comp, wide, wa, wb):
    d, t = place()
    upper = iota((8, LN), 0) < 4
    zero_ends(s, wa, wb)
    for z in range(s.nz):
        comp[8 * z : 8 * z + 8, :] = pltpu.roll(cs[z, pl.ds(HY - 1 + t, 8), :], lax.rem(LN - d * s.c2, LN), 1)
    wide[...] = split_dot(comp[...], spread2[...]).reshape(wide.shape)

    def body(z, carry):
        x = [[wide[z, k : k + 1, tiles(j)] for k in range(3)] for j in range(s.j1)]
        for k in range(2):
            rows = slice(s.pad1 - 4 + 4 * k, s.pad1 + 4 + 4 * k)
            for j in range(s.j1):
                y = w2[z + 1, j, rows, :] + jnp.where(upper, x[j][k], x[j][k + 1])
                wa[z + 1, j, rows, :] = jnp.where(level.scale[z, j, rows, :] > 0.0, y, 0.0)
        return carry

    lax.fori_loop(0, s.nz, body, 0)
    level.sweep(wa, wb, rx, s.pad1 - 3, s.pad1 + s.own1 + 3)
    level.sweep(wb, wa, rx, s.pad1 - 2, s.pad1 + s.own1 + 2)


def correct_fine(s, w, v, spread1, wide, dst):
    rows = slice(s.pad1 - 2, s.pad1 + s.own1 + 2)
    lhs = jnp.concatenate([w[1 : s.nz + 1, j, rows, :].reshape(s.nz * s.r1, LN) for j in range(s.j1)], axis=1)
    wide[...] = split_dot(lhs, spread1[...]).reshape(wide.shape)
    upper = iota((8, LN), 0) < 4

    def body(z, carry):
        for k in range(s.r1 // 2):
            rows = slice(8 * k, 8 * k + 8)
            for j in range(s.j0):
                x = [wide[z, 2 * k + i : 2 * k + i + 1, tiles(j)] for i in range(2)]
                dst[z + 1, j, rows, :] = v[z + 1, j, rows, :] + jnp.where(upper, x[0], x[1])
        return carry

    lax.fori_loop(0, s.nz, body, 0)


def back_kernel(
    s, got, v2, f, w2, rx,
    u2, l2, e2, up1, down1, e1, up0, down0, e0, cu, cd, spread2, spread1, down,
    v, r1, ship, cs, comp, wide2, wa, wb, va, vb, wide, rbuf,
):
    fine = Level(s, 0, up0, down0, e0, cu, cd)
    middle = Level(s, 1, up1, down1, e1, cu, cd)
    zero_ends(s, va, vb, v)
    coarse(s, got, u2, l2, e2, cs)
    middle_last(s, middle, cs, spread2, w2, rx, comp, wide2, wa, wb)
    correct_fine(s, wa, v2, spread1, wide, va)
    fine.sweep(va, vb, f, 2, s.re - 2)
    fine.sweep(vb, va, f, 3, s.re - 3)
    fine.sweep(va, vb, f, 4, s.re - 4)
    fine.sweep(vb, v, f, 5, s.re - 5)
    restrict(s, fine, v, f, HY, HY + s.rows, down, rbuf, wide, r1, ship)


def last_kernel(
    s, got, w2, rx, v2, f, u2, l2, e2, up1, down1, e1, up0, down0, e0, cu, cd, spread2, spread1, *refs,
):
    outs, (cs, comp, wide2, wa, wb, va, vb, wide) = refs[: s.nd], refs[s.nd :]
    fine = Level(s, 0, up0, down0, e0, cu, cd)
    middle = Level(s, 1, up1, down1, e1, cu, cd)
    d, _ = place()
    zero_ends(s, va, vb)
    coarse(s, got, u2, l2, e2, cs)
    middle_last(s, middle, cs, spread2, w2, rx, comp, wide2, wa, wb)
    correct_fine(s, wa, v2, spread1, wide, va)
    fine.sweep(va, vb, f, HY - 2, HY + s.rows + 2)
    fine.sweep(vb, va, f, HY - 1, HY + s.rows + 1)

    nj = s.j0 - 1
    for step, out in enumerate(outs):
        e = lax.rem(d + step, s.nd)
        for k in range(s.lz + 2):
            for j in range(nj):
                at = (k * nj + j) * s.rows
                out[at : at + s.rows, :] = va[s.lz * e + k, j, HY : HY + s.rows, :]
        for a in range(s.lz):
            for j in range(nj):
                at = (s.lz + 2) * nj * s.rows + (a * nj + j) * 2
                out[at : at + 1, :] = va[s.lz * e + a + 1, j, HY - 1 : HY, :]
                out[at + 1 : at + 2, :] = va[s.lz * e + a + 1, j, HY + s.rows : HY + s.rows + 1, :]


def coeff_own_kernel(s, prm, up, down):
    d, t = place()
    lane8, sub8 = iota((8, LN), 1), iota((8, LN), 0)
    row = (t * s.rows + iota((1, LN), 1)).astype(F32)
    col = iota((1, s.width), 1).astype(F32)
    for k, out in enumerate((up, down)):
        info = prm[lax.rem(d + s.nd - k, s.nd)]
        via = jnp.sum(jnp.where((lane8 == 0) & (sub8 == 5), info, 0.0), keepdims=True)
        if k == 1:
            via = via * (d > 0).astype(F32)
        r0, r1, c0, c1 = block_bounds(s, info)
        m = pair_dot(overlap(row, 1.0, r0, r1).astype(BF16), overlap(col, 1.0, c0, c1).astype(BF16))
        for j in range(s.width // LN):
            out[j] = m[: s.rows, tiles(j)] * via


def finish_kernel(s, f, c, cu, up, down, *refs):
    parts, (u_out, defect_out, v, u, defect, sem) = refs[: s.nd], refs[s.nd :]
    d, _ = place()
    nj, n = s.j0 - 1, s.width // LN
    for step, part in enumerate(parts):
        e = lax.rem(d + s.nd - step, s.nd)
        for j in range(nj):
            for k in range(s.lz + 2):
                at = (k * nj + j) * s.rows
                v[k, e * nj + j, HY : HY + s.rows, :] = part[at : at + s.rows, :]
            for a in range(s.lz):
                at = (s.lz + 2) * nj * s.rows + (a * nj + j) * 2
                v[a + 1, e * nj + j, HY - 1 : HY, :] = part[at : at + 1, :]
                v[a + 1, e * nj + j, HY + s.rows : HY + s.rows + 1, :] = part[at + 1 : at + 2, :]
    lane = iota((8, LN), 1)
    first, last = lane == 0, lane == LN - 1
    zero = jnp.zeros((8, LN), F32)
    copies = []
    for a in range(s.lz):
        z = d * s.lz + a
        cz, above = c[z], cu[z] * c[z]
        if a > 0:
            below = cu[z - 1] * c[z - 1]
        for r in range(0, s.rows, 8):
            rows, own = slice(HY + r, HY + r + 8), slice(r, r + 8)
            x = [v[a + 1, j, rows, :] for j in range(n)]
            ahead = [pltpu.roll(w, LN - 1, 1) for w in x] + [zero]
            behind = [pltpu.roll(w, 1, 1) for w in x] + [zero]
            for j in range(n):
                k_up = above if a < s.lz - 1 else up[j, own, :]
                k_down = below if a > 0 else down[j, own, :]
                side = jnp.where(last, ahead[j + 1], ahead[j]) + jnp.where(first, behind[j - 1], behind[j])
                side += v[a + 1, j, HY + r - 1 : HY + r + 7, :] + v[a + 1, j, HY + r + 1 : HY + r + 9, :]
                g = cz * side + (k_up * v[a + 2, j, rows, :] + k_down * v[a, j, rows, :])
                u[a, own, tiles(j)] = x[j]
                defect[a, own, tiles(j)] = (f[a, own, tiles(j)] + g) - (4.0 * cz + k_up + k_down) * x[j]
        for k, (src, dst) in enumerate(((u, u_out), (defect, defect_out))):
            copies.append(pltpu.make_async_copy(src.at[a], dst.at[a], sem.at[2 * a + k]))
            copies[-1].start()
    for x in copies:
        x.wait()


def call(kernel, s, outs, scratch=(), to_hbm=False, from_hbm=False, in_vmem=False, limit=32 << 20):
    shapes = [pltpu.VMEM(o, F32) if in_vmem else jax.ShapeDtypeStruct(o, F32) for o in outs]
    spaces = [pl.BlockSpec(memory_space=m) for m in (pltpu.VMEM, pltpu.HBM)]

    def run(*args):
        total = sum(int(np.prod(a.shape)) * 4 for a in args) + sum(int(np.prod(o)) * 4 for o in outs)
        return pl.pallas_call(
            functools.partial(kernel, s),
            out_shape=shapes,
            in_specs=[spaces[from_hbm]] * len(args),
            out_specs=[spaces[to_hbm]] * len(outs),
            scratch_shapes=[pltpu.VMEM(x, F32) if isinstance(x, tuple) else x for x in scratch],
            compiler_params=pltpu.CompilerParams(vmem_limit_bytes=limit),
            cost_estimate=pl.CostEstimate(flops=4 * total, bytes_accessed=total, transcendentals=0),
        )(*args)

    return run


def shift(x, axis, by):
    n = lax.axis_size(axis)
    return lax.ppermute(x, axis, [(i, (i + by) % n) for i in range(n)])


def swap(x, odd):
    n = lax.axis_size("tile")
    to = [((k - odd) ^ 1) + odd for k in range(n)]
    return lax.ppermute(x, "tile", [(k, q if 0 <= q < n else k) for k, q in enumerate(to)])


def tables(s):
    p = np.arange(s.we)
    at = p // 4 + np.where(p >= s.wc + HX, s.w1 - s.we // 4, 0)
    down = at[:, None] == np.arange(s.w1)[None, :]
    q = np.arange(s.w1)
    k = q // 4 + np.where(q >= s.w1 - HX // 4, LN - s.w1 // 4, 0)
    used = (q < s.c1 + HX // 4) | (q >= s.w1 - HX // 4)
    spread2 = (np.arange(LN)[:, None] == k[None, :]) & used[None, :]
    r = np.arange(LN)
    down2 = (r // 4)[:, None] == (r % s.c2)[None, :]
    return [jnp.asarray(m, BF16) for m in (down.T, spread2, down2 * 0.25)]


def local(s, source_heating, material_thermal_values, layer_material, via_conductance, via_blocks):
    spread1, spread2, down2 = tables(s)
    down = pl.pallas_call(
        functools.partial(down_kernel, s),
        name="down",
        out_shape=jax.ShapeDtypeStruct((s.we, s.w1), BF16),
        compiler_params=pltpu.CompilerParams(vmem_limit_bytes=4 << 20),
        cost_estimate=pl.CostEstimate(flops=1 << 20, bytes_accessed=1 << 20, transcendentals=0),
    )()
    smem, packed = pltpu.SMEM, (s.part + 8, LN)
    sends = call(
        pack_kernel, s, [packed] * s.nd,
        [
            smem(material_thermal_values.shape, F32), smem(layer_material.shape, jnp.int32),
            smem((1, 1), F32), pltpu.VMEM((4, s.nb), jnp.int32),
            pltpu.VMEM(source_heating.shape, F32), pltpu.SemaphoreType.DMA((s.lz + 4,)),
        ],
        from_hbm=True, in_vmem=True, limit=VMEM - 4 * s.nd * packed[0] * packed[1],
    )(material_thermal_values, layer_material, via_conductance[None], via_blocks[0].T, source_heating)
    parts = [sends[0]] + [shift(sends[k], "die", k) for k in range(1, s.nd)]
    half = (s.nz * s.j0, HY, LN)
    one, two, prm = call(assemble_kernel, s, [half, half, (s.nd, 8, LN)])(*parts)
    f0, f1, small = (s.j0, s.re, LN), (s.j1, s.e1, LN), (s.nz, s.j1, s.r1, LN)
    fine, fine_v = (s.nz, *f0), (s.nz + 2, *f0)
    mid, mid_v = (s.nz, *f1), (s.nz + 2, *f1)
    slab, table = (s.nd * s.lz, s.nt, LN), (s.nz, 8, LN)
    up0, down0, e0, c, ic, cu, cd = call(
        coeff_fine_kernel, s, [(s.nd, *f0), (s.nd, *f0), fine, table, table, table, table]
    )(prm)
    shared = (s.nz + s.nd, s.r1, LN)
    flat, rbuf = (s.nz, s.r1, s.we), (s.nz * s.j0 * s.re, LN)
    from_two = swap(two, 1)
    from_one = swap(one, 0)
    f, v2, r1, ship = call(fine_first_kernel, s, [fine, fine_v, small, shared], [fine_v, rbuf, flat])(
        from_one, from_two, one, two, up0, down0, e0, ic, cu, cd, down
    )
    up1, down1, e1, u2, l2, e2 = call(coeff_coarse_kernel, s, [(s.nd, *f1), (s.nd, *f1), mid, slab, slab, slab])(prm)

    def middle_first(r1, ship):
        return call(
            middle_first_kernel, s,
            [mid, mid_v, (s.nd * s.nt * s.lz, LN)], [mid_v, (s.nz * 8, LN)],
        )(swap(ship, 0), r1, swap(ship, 1), up1, down1, e1, cu, cd, down2)

    def everywhere(send):
        return lax.all_to_all(send, ("die", "tile"), 0, 0, tiled=True)

    spaces = [(s.nd * s.lz, s.nt + 2 * HY, LN), (s.nz * 8, LN), (s.nz, 8, s.w1), mid_v, mid_v]
    spaces += [fine_v, fine_v, flat]
    rx, w2, send = middle_first(r1, ship)
    levels = (u2, l2, e2, up1, down1, e1, up0, down0, e0)
    v, r1, ship = call(back_kernel, s, [fine_v, small, shared], spaces + [rbuf])(
        everywhere(send), v2, f, w2, rx, *levels, cu, cd, spread2, spread1, down
    )
    rx, w2, send = middle_first(r1, ship)
    piece = ((s.lz + 2) * (s.j0 - 1) * s.rows + 2 * s.lz * (s.j0 - 1), LN)
    sends = call(last_kernel, s, [piece] * s.nd, spaces)(
        everywhere(send), w2, rx, v, f, *levels, cu, cd, spread2, spread1
    )
    parts = [sends[0]] + [shift(sends[k], "die", k) for k in range(1, s.nd)]
    whole, columns = (s.lz, s.rows, s.width), (s.width // LN, s.rows, LN)
    own_up, own_down = call(coeff_own_kernel, s, [columns] * 2)(prm)
    scratch = [(s.lz + 2, s.width // LN, s.re, LN), whole, whole, pltpu.SemaphoreType.DMA((2 * s.lz,))]
    return tuple(call(finish_kernel, s, [whole] * 2, scratch, True)(source_heating, c, cu, own_up, own_down, *parts))


def solution(mesh):
    in_specs = (P("die", "tile", None), P(), P("die"), P("die"), P("die", None, None))
    out_specs = (P("die", "tile", None), P("die", "tile", None))

    def body(f, mat, material, conductance, blocks):
        s = Sizes(mesh.shape, f.shape, blocks.shape[1])
        return local(s, f, mat, material, conductance, blocks)

    return jax.shard_map(body, mesh=mesh, in_specs=in_specs, out_specs=out_specs, check_vma=False)
```

```python
import functools

import jax
import jax.numpy as jnp
import numpy as np
from jax import lax
from jax.experimental import pallas as pl
from jax.experimental.pallas import tpu as pltpu
from jax.sharding import PartitionSpec as P


OMEGA = 0.8
NC = 6
LN = 128
HX = 64
VMEM = 67_043_328
HY = 8
F32 = jnp.float32
BF16 = jnp.bfloat16


def iota(shape, axis):
    return lax.broadcasted_iota(jnp.int32, shape, axis)


def split_dot(x, m):
    hi = x.astype(BF16)
    lo = (x - hi.astype(F32)).astype(BF16)
    return jnp.dot(hi, m, preferred_element_type=F32) + jnp.dot(lo, m, preferred_element_type=F32)


def pair_dot(a, b):
    return lax.dot_general(a, b, (((0,), (0,)), ((), ())), preferred_element_type=F32)


class Sizes:
    def __init__(self, mesh_shape, f_shape, n_blocks):
        self.nd, self.nt = mesh_shape["die"], mesh_shape["tile"]
        self.lz, self.rows, self.width = f_shape
        self.nb = n_blocks
        self.wc = self.width // self.nd
        self.we = self.wc + LN
        self.j0 = self.we // LN
        self.nz = self.nd * self.lz
        self.re = self.rows + 2 * HY
        self.own1 = self.rows // 4
        self.r1 = self.re // 4
        self.c1 = self.wc // 4
        self.e1 = 2 * self.r1
        self.pad1 = (self.e1 - self.own1) // 2
        self.j1 = 2
        self.w1 = self.j1 * LN
        self.c2 = self.wc // 16
        self.part = self.lz * self.j0 * self.rows
        assert self.rows == 16 and self.lz == 4 and self.c1 == LN
        assert self.nd * self.c2 == LN and self.nb <= LN and self.nt <= LN and self.nt % 8 == 0


def place():
    return lax.axis_index("die"), lax.axis_index("tile")


def even():
    _, t = place()
    return lax.rem(t, 2) == 0


def tiles(j):
    return slice(j * LN, (j + 1) * LN)


def windows(lo, hi):
    return [min(r, hi - 8) for r in range(lo, hi, 8)]


def pack_kernel(s, mat_h, material_h, conductance_h, blocks_h, f_h, *refs):
    outs, (mat, material, conductance, blocks, f, sem) = refs[: s.nd], refs[s.nd :]
    pairs = [(f_h.at[z], f.at[z]) for z in range(s.lz)]
    pairs += [(mat_h, mat), (material_h, material), (conductance_h, conductance), (blocks_h, blocks)]
    copies = [pltpu.make_async_copy(a, b, sem.at[k]) for k, (a, b) in enumerate(pairs)]
    for c in copies:
        c.start()
    for c in copies[s.lz :]:
        c.wait()
    d, _ = place()
    lane, sub = iota((8, LN), 1), iota((8, LN), 0)
    info = jnp.where((sub == 5) & (lane == 0), conductance[0, 0], 0.0)
    for z in range(s.lz):
        info = jnp.where((sub == 4) & (lane == z), mat[material[z]], info)
    for out in outs:
        out[s.part :, :] = info
        out[s.part : s.part + 4, : s.nb] = blocks[...].astype(F32)
    low = iota((s.rows, LN), 1) < HX
    for z in range(s.lz):
        copies[z].wait()
        for step, out in enumerate(outs):
            e = lax.rem(d + step, s.nd)
            right = lax.rem(e + 1, s.nd) * s.wc
            left = lax.rem(e + s.nd - 1, s.nd) * s.wc + (s.wc - LN)
            column = lambda at: f[z, :, pl.ds(pl.multiple_of(at, LN), LN)]
            for j in range(s.j0):
                at = (z * s.j0 + j) * s.rows
                if j < s.j0 - 1:
                    x = column(e * s.wc + j * LN)
                else:
                    x = jnp.where(low, column(right), column(left))
                out[at : at + s.rows, :] = x


def assemble_kernel(s, *refs):
    parts, (one, two, prm) = refs[: s.nd], refs[s.nd :]
    d, _ = place()
    n = s.lz * s.j0
    lower = even()
    for step, part in enumerate(parts):
        e = lax.rem(d + s.nd - step, s.nd)
        for q in range(n):
            top = part[q * s.rows : q * s.rows + HY, :]
            bot = part[q * s.rows + HY : (q + 1) * s.rows, :]
            one[n * e + q] = jnp.where(lower, bot, top)
            two[n * e + q] = jnp.where(lower, top, bot)
        prm[e] = part[s.part :, :]


def overlap(lo, size, first, past):
    return jnp.maximum(jnp.minimum(lo + size, past) - jnp.maximum(lo, first), 0.0)


def block_bounds(s, info):
    b = jnp.transpose(info)
    lane = iota((LN, 8), 1)
    col = [jnp.sum(jnp.where(lane == k, b, 0.0), axis=1, keepdims=True) for k in range(4)]
    col = [x[: s.nb] for x in col]
    return col[0], col[0] + col[2], col[1], col[1] + col[3]


def die_values(s, prm):
    lane8, sub8 = iota((8, LN), 1), iota((8, LN), 0)

    def pick(tile, row, col):
        return jnp.sum(jnp.where((lane8 == col) & (sub8 == row), tile, 0.0), keepdims=True)

    info = [prm[g] for g in range(s.nd)]
    cond = [pick(info[z // s.lz], 4, z % s.lz) for z in range(s.nz)]
    via = [pick(info[g], 5, 0) for g in range(s.nd)]
    vert = [2.0 * p * q / (p + q) for p, q in zip(cond, cond[1:] + cond[-1:])]
    return cond, vert, via, [block_bounds(s, x) for x in info]


def level_coeffs(s, level, values, via_up, via_down, scale):
    cond, vert, via, blocks = values
    d, t = place()
    size = 4**level
    n, own = (s.we, s.wc) if level == 0 else (s.w1, s.c1)
    height, nj = (s.re, s.j0) if level == 0 else (s.e1, s.j1)
    pad = HY if level == 0 else s.pad1
    halo = HX // size

    def columns(shape, axis):
        p = iota(shape, axis)
        return p, d * own + jnp.where(p >= n - halo, p - n, p)

    first = t * (s.rows // size) - pad
    row = ((first + iota((1, LN), 1)) * size).astype(F32)
    col = (columns((1, n), 1)[1] * size).astype(F32)
    rr = first + iota((height, n), 0)
    pp, cc = columns((height, n), 1)
    inside = (rr >= 0) & (rr < s.rows * s.nt // size) & (cc >= 0) & (cc < s.width // size)
    inside = jnp.where(inside & ((pp < own + halo) | (pp >= n - halo)), OMEGA, 0.0)
    via_down[0] = jnp.zeros(via_down.shape[1:], F32)
    for g in range(s.nd):
        r0, r1, c0, c1 = blocks[g]
        m = pair_dot(
            overlap(row, float(size), r0, r1).astype(BF16), overlap(col, float(size), c0, c1).astype(BF16)
        )[:height]
        top = (g + 1) * s.lz - 1
        m = m * (via[g] * (0.25**level))
        for j in range(nj):
            via_up[g, j] = m[:, tiles(j)] / cond[top]
            if g + 1 < s.nd:
                via_down[g + 1, j] = m[:, tiles(j)] / cond[top + 1]
    for z in range(s.nz):
        g, a = z // s.lz, z % s.lz
        const = 4.0
        if a < s.lz - 1:
            const = const + vert[z] * (4.0**level) / cond[z]
        if a > 0:
            const = const + vert[z - 1] * (4.0**level) / cond[z]
        for j in range(nj):
            diag = const
            if a == s.lz - 1:
                diag = diag + via_up[g, j]
            if a == 0:
                diag = diag + via_down[g, j]
            scale[z, j] = inside[:, tiles(j)] / diag


def coeff_fine_kernel(s, prm, up0, down0, e0, c, ic, cu, cd):
    values = die_values(s, prm)
    cond, vert = values[:2]
    for z in range(s.nz):
        c[z] = jnp.zeros((8, LN), F32) + cond[z]
        ic[z] = jnp.zeros((8, LN), F32) + 1.0 / cond[z]
        cu[z] = jnp.zeros((8, LN), F32) + vert[z] / cond[z]
        cd[z] = jnp.zeros((8, LN), F32) + vert[max(z - 1, 0)] / cond[z]
    level_coeffs(s, 0, values, up0, down0, e0)


def coeff_coarse_kernel(s, prm, up1, down1, e1, u2, l2, e2):
    values = die_values(s, prm)
    cond, vert, via, blocks = values
    level_coeffs(s, 1, values, up1, down1, e1)
    at = (iota((1, LN), 1) * 16).astype(F32)
    ups = []
    for z in range(s.nz):
        g = z // s.lz
        if z % s.lz < s.lz - 1:
            up = jnp.zeros((s.nt, LN), F32) + vert[z] * 256.0
        else:
            r0, r1, c0, c1 = blocks[g]
            up = pair_dot(overlap(at, 16.0, r0, r1).astype(BF16), overlap(at, 16.0, c0, c1).astype(BF16))
            up = up[: s.nt] * via[g]
        down = ups[-1] if ups else jnp.zeros((s.nt, LN), F32)
        ups.append(up)
        u2[z] = up / (cond[z] * 16.0)
        l2[z] = down / (cond[z] * 16.0)
        e2[z] = OMEGA * 16.0 * cond[z] / (64.0 * cond[z] + up + down)


class Level:
    def __init__(self, s, level, up, down, scale, cu, cd):
        self.s, self.up, self.down, self.scale, self.cu, self.cd = s, up, down, scale, cu, cd
        self.nj = (s.j0, s.j1)[level]
        self.us = 4.0**level

    def walk(self, src, f, lo, hi, emit, count=None):
        s, n = self.s, self.nj
        lane = iota((8, LN), 1)
        first, last = lane == 0, lane == LN - 1

        def group(g, carry):
            for a in range(s.lz):
                z = g * s.lz + a
                for r in windows(lo, hi):
                    rows = pl.ds(r, 8)
                    v = [src[z + 1, j, rows, :] for j in range(n)]
                    ahead = [pltpu.roll(x, LN - 1, 1) for x in v]
                    behind = [pltpu.roll(x, 1, 1) for x in v]
                    for j in range(count or n):
                        k_up = self.cu[z] * self.us if a < s.lz - 1 else self.up[g, j, rows, :]
                        k_down = self.cd[z] * self.us if a > 0 else self.down[g, j, rows, :]
                        x = jnp.where(last, ahead[(j + 1) % n], ahead[j]) + jnp.where(first, behind[j - 1], behind[j])
                        y = src[z + 1, j, pl.ds(r - 1, 8), :] + src[z + 1, j, pl.ds(r + 1, 8), :]
                        x = (f[z, j, rows, :] + x) + y
                        x = x + (k_up * src[z + 2, j, rows, :] + k_down * src[z, j, rows, :])
                        emit(z, j, rows, v[j], x, k_up, k_down)
            return carry

        lax.fori_loop(0, s.nd, group, 0, unroll=2)

    def sweep(self, src, dst, f, lo, hi):
        def emit(z, j, rows, v, g, *_):
            dst[z + 1, j, rows, :] = (1.0 - OMEGA) * v + self.scale[z, j, rows, :] * g

        self.walk(src, f, lo, hi, emit)

    def residual(self, src, f, lo, hi, put, count=None):
        def emit(z, j, rows, v, g, k_up, k_down):
            put(z, j, rows, g - (4.0 + k_up + k_down) * v)

        self.walk(src, f, lo, hi, emit, count)


def zero_ends(s, *bufs):
    for b in bufs:
        b[0] = jnp.zeros(b.shape[1:], F32)
        b[s.nz + 1] = jnp.zeros(b.shape[1:], F32)


def turn(a):
    return a * 2 * (HX // 4) + HX // 4


def restrict(s, level, src, f, lo, hi, down, rbuf, sums, r1, ship):
    for k in range(s.nz * s.j0):
        rbuf[k * s.re : k * s.re + 8, :] = jnp.zeros((8, LN), F32)
        rbuf[(k + 1) * s.re - 8 : (k + 1) * s.re, :] = jnp.zeros((8, LN), F32)

    def put(z, j, rows, x):
        rbuf[pl.ds((z * s.j0 + j) * s.re + rows.start, 8), :] = x

    level.residual(src, f, lo, hi, put)

    def body(z, carry):
        for j in range(s.j0):
            part = [rbuf[pl.ds((z * s.j0 + j) * s.re + k, s.r1, stride=4), :] for k in range(4)]
            sums[z, :, tiles(j)] = (part[0] + part[1]) + (part[2] + part[3])
        return carry

    lax.fori_loop(0, s.nz, body, 0, unroll=4)
    out = split_dot(sums[...].reshape(s.nz * s.r1, s.we), down[...])
    part = iota((s.r1, LN), 1) // (HX // 2)
    for g in range(s.nd):
        shared = jnp.zeros((s.r1, LN), F32)
        for a in range(s.lz):
            z = g * s.lz + a
            x, halo = (out[z * s.r1 : (z + 1) * s.r1, tiles(j)] for j in range(s.j1))
            r1[z, 0] = x
            r1[z, 1] = halo
            ship[z] = x
            shared = jnp.where(part == a, pltpu.roll(halo, turn(a), 1), shared)
        ship[s.nz + g] = shared


def down_kernel(s, out):
    p, q = iota((s.we, s.w1), 0), iota((s.we, s.w1), 1)
    at = p // 4 + jnp.where(p >= s.wc + HX, s.w1 - s.we // 4, 0)
    out[...] = jnp.where(at == q, 0.25, 0.0).astype(BF16)


def fine_first_kernel(s, from_one, from_two, one, two, up0, down0, e0, ic, cu, cd, down, f, v2, r1, ship, va, rbuf, sums):
    level = Level(s, 0, up0, down0, e0, cu, cd)
    lower = even()
    zero_ends(s, va, v2)

    def body(z, carry):
        for k, (a, b) in enumerate(((from_two, from_one), (two, one), (one, two), (from_one, from_two))):
            rows = slice(k * HY, (k + 1) * HY)
            for j in range(s.j0):
                q = z * s.j0 + j
                x = jnp.where(lower, a[q], b[q]) * ic[z]
                f[z, j, rows, :] = x
                va[z + 1, j, rows, :] = e0[z, j, rows, :] * x
        return carry

    lax.fori_loop(0, s.nz, body, 0, unroll=4)
    level.sweep(va, v2, f, 1, s.re - 1)
    restrict(s, level, v2, f, HY - 4, s.re - HY + 4, down, rbuf, sums, r1, ship)


def middle_first_kernel(s, r1a, r1, r1b, up1, down1, e1, cu, cd, down2, rx, w2, send, wa, buf):
    level = Level(s, 1, up1, down1, e1, cu, cd)
    half, own, pad = s.r1, s.own1, s.pad1
    sub = iota((half, LN), 0)
    lower = even()
    zero_ends(s, wa, w2)

    def body(g, carry):
        for a in range(s.lz):
            z = g * s.lz + a
            for j in range(s.j1):
                mid = pltpu.roll(r1[z, j], half // 2, 0)
                if j == 0:
                    p, q = r1a[z], r1b[z]
                else:
                    p, q = (pltpu.roll(x[s.nz + g], LN - turn(a), 1) for x in (r1a, r1b))
                up = jnp.where(sub >= pad, mid, jnp.where(lower, q, p))
                down = jnp.where(sub < own - (half - pad), mid, jnp.where(lower, p, q))
                rx[z, j, :half, :] = up
                rx[z, j, half:, :] = down
                wa[z + 1, j, :half, :] = e1[z, j, :half, :] * up
                wa[z + 1, j, half:, :] = e1[z, j, half:, :] * down
        return carry

    lax.fori_loop(0, s.nd, body, 0, unroll=2)
    level.sweep(wa, w2, rx, pad - 4, pad + own + 4)

    def put(z, j, rows, x):
        buf[pl.ds(pl.multiple_of(z * 8, 8), 8), :] = x

    level.residual(w2, rx, pad - 2, pad + own + 2, put, 1)
    sub8, group = iota((8, LN), 0), iota((8, LN), 1) // s.c2
    tile = jnp.zeros((8, LN), F32)
    for h in range(s.nz // 8):
        part = [buf[pl.ds(64 * h + 2 + k, 8, stride=8), :] for k in range(own)]
        x = split_dot((part[0] + part[1]) + (part[2] + part[3]), down2[...])
        y = pltpu.roll(x, 4, 0)
        for g in (2 * h, 2 * h + 1):
            tile = jnp.where(group == g, jnp.where((sub8 < 4) == (g % 2 == 0), x, y), tile)
    for k in range(s.nd * s.nt * s.lz // 8):
        send[8 * k : 8 * k + 8, :] = tile


def coarse(s, got, u2, l2, e2, cs):
    lane, t = iota((s.nt, LN), 1), iota((s.nt, LN), 0)
    rhs, v = [], []
    for z in range(s.nz):
        g, a = z // s.lz, z % s.lz
        r = jnp.zeros((s.nt, LN), F32)
        for e in range(s.nd):
            x = got[pl.ds(e * s.nt * s.lz + a, s.nt, stride=s.lz), :]
            x = pltpu.roll(x, (e - g) * s.c2 % LN, 1) if e != g else x
            r = jnp.where(lane // s.c2 == e, x, r)
        rhs.append(r)
        v.append(e2[z] * r)

    def body(_, v):
        new = []
        for z in range(s.nz):
            w = v[z]
            side = jnp.where(lane == LN - 1, 0.0, pltpu.roll(w, LN - 1, 1))
            side += jnp.where(lane == 0, 0.0, pltpu.roll(w, 1, 1))
            side += jnp.where(t == s.nt - 1, 0.0, pltpu.roll(w, s.nt - 1, 0))
            side += jnp.where(t == 0, 0.0, pltpu.roll(w, 1, 0))
            g = rhs[z] + side
            if z < s.nz - 1:
                g += u2[z] * v[z + 1]
            if z > 0:
                g += l2[z] * v[z - 1]
            new.append((1.0 - OMEGA) * w + e2[z] * g)
        return tuple(new)

    v = lax.fori_loop(0, NC - 1, body, tuple(v), unroll=True)
    for z in range(s.nz):
        cs[z, :HY, :] = jnp.zeros((HY, LN), F32)
        cs[z, HY + s.nt :, :] = jnp.zeros((HY, LN), F32)
        cs[z, HY : HY + s.nt, :] = v[z]


def middle_last(s, level, cs, spread2, w2, rx, comp, wide, wa, wb):
    d, t = place()
    upper = iota((8, LN), 0) < 4
    zero_ends(s, wa, wb)
    for z in range(s.nz):
        comp[8 * z : 8 * z + 8, :] = pltpu.roll(cs[z, pl.ds(HY - 1 + t, 8), :], lax.rem(LN - d * s.c2, LN), 1)
    wide[...] = split_dot(comp[...], spread2[...]).reshape(wide.shape)

    def body(z, carry):
        x = [[wide[z, k : k + 1, tiles(j)] for k in range(3)] for j in range(s.j1)]
        for k in range(2):
            rows = slice(s.pad1 - 4 + 4 * k, s.pad1 + 4 + 4 * k)
            for j in range(s.j1):
                y = w2[z + 1, j, rows, :] + jnp.where(upper, x[j][k], x[j][k + 1])
                wa[z + 1, j, rows, :] = jnp.where(level.scale[z, j, rows, :] > 0.0, y, 0.0)
        return carry

    lax.fori_loop(0, s.nz, body, 0, unroll=4)
    level.sweep(wa, wb, rx, s.pad1 - 3, s.pad1 + s.own1 + 3)
    level.sweep(wb, wa, rx, s.pad1 - 2, s.pad1 + s.own1 + 2)


def correct_fine(s, w, v, spread1, wide, dst):
    rows = slice(s.pad1 - 2, s.pad1 + s.own1 + 2)
    lhs = jnp.concatenate([w[1 : s.nz + 1, j, rows, :].reshape(s.nz * s.r1, LN) for j in range(s.j1)], axis=1)
    wide[...] = split_dot(lhs, spread1[...]).reshape(wide.shape)
    upper = iota((8, LN), 0) < 4

    def body(z, carry):
        for k in range(s.r1 // 2):
            rows = slice(8 * k, 8 * k + 8)
            for j in range(s.j0):
                x = [wide[z, 2 * k + i : 2 * k + i + 1, tiles(j)] for i in range(2)]
                dst[z + 1, j, rows, :] = v[z + 1, j, rows, :] + jnp.where(upper, x[0], x[1])
        return carry

    lax.fori_loop(0, s.nz, body, 0, unroll=4)


def back_kernel(
    s, got, v2, f, w2, rx,
    u2, l2, e2, up1, down1, e1, up0, down0, e0, cu, cd, spread2, spread1, down,
    v, r1, ship, cs, comp, wide2, wa, wb, va, vb, wide, rbuf,
):
    fine = Level(s, 0, up0, down0, e0, cu, cd)
    middle = Level(s, 1, up1, down1, e1, cu, cd)
    zero_ends(s, va, vb, v)
    coarse(s, got, u2, l2, e2, cs)
    middle_last(s, middle, cs, spread2, w2, rx, comp, wide2, wa, wb)
    correct_fine(s, wa, v2, spread1, wide, va)
    fine.sweep(va, vb, f, 2, s.re - 2)
    fine.sweep(vb, va, f, 3, s.re - 3)
    fine.sweep(va, vb, f, 4, s.re - 4)
    fine.sweep(vb, v, f, 5, s.re - 5)
    restrict(s, fine, v, f, HY, HY + s.rows, down, rbuf, wide, r1, ship)


def last_kernel(
    s, got, w2, rx, v2, f, u2, l2, e2, up1, down1, e1, up0, down0, e0, cu, cd, spread2, spread1, *refs,
):
    outs, (cs, comp, wide2, wa, wb, va, vb, wide) = refs[: s.nd], refs[s.nd :]
    fine = Level(s, 0, up0, down0, e0, cu, cd)
    middle = Level(s, 1, up1, down1, e1, cu, cd)
    d, _ = place()
    zero_ends(s, va, vb)
    coarse(s, got, u2, l2, e2, cs)
    middle_last(s, middle, cs, spread2, w2, rx, comp, wide2, wa, wb)
    correct_fine(s, wa, v2, spread1, wide, va)
    fine.sweep(va, vb, f, HY - 2, HY + s.rows + 2)
    fine.sweep(vb, va, f, HY - 1, HY + s.rows + 1)

    nj = s.j0 - 1
    for step, out in enumerate(outs):
        e = lax.rem(d + step, s.nd)
        for k in range(s.lz + 2):
            for j in range(nj):
                at = (k * nj + j) * s.rows
                out[at : at + s.rows, :] = va[s.lz * e + k, j, HY : HY + s.rows, :]
        for a in range(s.lz):
            for j in range(nj):
                at = (s.lz + 2) * nj * s.rows + (a * nj + j) * 2
                out[at : at + 1, :] = va[s.lz * e + a + 1, j, HY - 1 : HY, :]
                out[at + 1 : at + 2, :] = va[s.lz * e + a + 1, j, HY + s.rows : HY + s.rows + 1, :]


def coeff_own_kernel(s, prm, up, down):
    d, t = place()
    lane8, sub8 = iota((8, LN), 1), iota((8, LN), 0)
    row = (t * s.rows + iota((1, LN), 1)).astype(F32)
    col = iota((1, s.width), 1).astype(F32)
    for k, out in enumerate((up, down)):
        info = prm[lax.rem(d + s.nd - k, s.nd)]
        via = jnp.sum(jnp.where((lane8 == 0) & (sub8 == 5), info, 0.0), keepdims=True)
        if k == 1:
            via = via * (d > 0).astype(F32)
        r0, r1, c0, c1 = block_bounds(s, info)
        m = pair_dot(overlap(row, 1.0, r0, r1).astype(BF16), overlap(col, 1.0, c0, c1).astype(BF16))
        for j in range(s.width // LN):
            out[j] = m[: s.rows, tiles(j)] * via


def finish_kernel(s, f, c, cu, up, down, *refs):
    parts, (u_out, defect_out, v, u, defect, sem) = refs[: s.nd], refs[s.nd :]
    d, _ = place()
    nj, n = s.j0 - 1, s.width // LN
    for step, part in enumerate(parts):
        e = lax.rem(d + s.nd - step, s.nd)
        for j in range(nj):
            for k in range(s.lz + 2):
                at = (k * nj + j) * s.rows
                v[k, e * nj + j, HY : HY + s.rows, :] = part[at : at + s.rows, :]
            for a in range(s.lz):
                at = (s.lz + 2) * nj * s.rows + (a * nj + j) * 2
                v[a + 1, e * nj + j, HY - 1 : HY, :] = part[at : at + 1, :]
                v[a + 1, e * nj + j, HY + s.rows : HY + s.rows + 1, :] = part[at + 1 : at + 2, :]
    lane = iota((8, LN), 1)
    first, last = lane == 0, lane == LN - 1
    zero = jnp.zeros((8, LN), F32)
    copies = []
    for a in range(s.lz):
        z = d * s.lz + a
        cz, above = c[z], cu[z] * c[z]
        if a > 0:
            below = cu[z - 1] * c[z - 1]
        for r in range(0, s.rows, 8):
            rows, own = slice(HY + r, HY + r + 8), slice(r, r + 8)
            x = [v[a + 1, j, rows, :] for j in range(n)]
            ahead = [pltpu.roll(w, LN - 1, 1) for w in x] + [zero]
            behind = [pltpu.roll(w, 1, 1) for w in x] + [zero]
            for j in range(n):
                k_up = above if a < s.lz - 1 else up[j, own, :]
                k_down = below if a > 0 else down[j, own, :]
                side = jnp.where(last, ahead[j + 1], ahead[j]) + jnp.where(first, behind[j - 1], behind[j])
                side += v[a + 1, j, HY + r - 1 : HY + r + 7, :] + v[a + 1, j, HY + r + 1 : HY + r + 9, :]
                g = cz * side + (k_up * v[a + 2, j, rows, :] + k_down * v[a, j, rows, :])
                u[a, own, tiles(j)] = x[j]
                defect[a, own, tiles(j)] = (f[a, own, tiles(j)] + g) - (4.0 * cz + k_up + k_down) * x[j]
        for k, (src, dst) in enumerate(((u, u_out), (defect, defect_out))):
            copies.append(pltpu.make_async_copy(src.at[a], dst.at[a], sem.at[2 * a + k]))
            copies[-1].start()
    for x in copies:
        x.wait()


def call(kernel, s, outs, scratch=(), to_hbm=False, from_hbm=False, in_vmem=False, limit=32 << 20):
    shapes = [pltpu.VMEM(o, F32) if in_vmem else jax.ShapeDtypeStruct(o, F32) for o in outs]
    spaces = [pl.BlockSpec(memory_space=m) for m in (pltpu.VMEM, pltpu.HBM)]

    def run(*args):
        total = sum(int(np.prod(a.shape)) * 4 for a in args) + sum(int(np.prod(o)) * 4 for o in outs)
        return pl.pallas_call(
            functools.partial(kernel, s),
            out_shape=shapes,
            in_specs=[spaces[from_hbm]] * len(args),
            out_specs=[spaces[to_hbm]] * len(outs),
            scratch_shapes=[pltpu.VMEM(x, F32) if isinstance(x, tuple) else x for x in scratch],
            compiler_params=pltpu.CompilerParams(vmem_limit_bytes=limit),
            cost_estimate=pl.CostEstimate(flops=4 * total, bytes_accessed=total, transcendentals=0),
        )(*args)

    return run


def shift(x, axis, by):
    n = lax.axis_size(axis)
    return lax.ppermute(x, axis, [(i, (i + by) % n) for i in range(n)])


def swap(x, odd):
    n = lax.axis_size("tile")
    to = [((k - odd) ^ 1) + odd for k in range(n)]
    return lax.ppermute(x, "tile", [(k, q if 0 <= q < n else k) for k, q in enumerate(to)])


def tables(s):
    p = np.arange(s.we)
    at = p // 4 + np.where(p >= s.wc + HX, s.w1 - s.we // 4, 0)
    down = at[:, None] == np.arange(s.w1)[None, :]
    q = np.arange(s.w1)
    k = q // 4 + np.where(q >= s.w1 - HX // 4, LN - s.w1 // 4, 0)
    used = (q < s.c1 + HX // 4) | (q >= s.w1 - HX // 4)
    spread2 = (np.arange(LN)[:, None] == k[None, :]) & used[None, :]
    r = np.arange(LN)
    down2 = (r // 4)[:, None] == (r % s.c2)[None, :]
    return [jnp.asarray(m, BF16) for m in (down.T, spread2, down2 * 0.25)]


def local(s, source_heating, material_thermal_values, layer_material, via_conductance, via_blocks):
    spread1, spread2, down2 = tables(s)
    down = pl.pallas_call(
        functools.partial(down_kernel, s),
        name="down",
        out_shape=jax.ShapeDtypeStruct((s.we, s.w1), BF16),
        compiler_params=pltpu.CompilerParams(vmem_limit_bytes=4 << 20),
        cost_estimate=pl.CostEstimate(flops=1 << 20, bytes_accessed=1 << 20, transcendentals=0),
    )()
    smem, packed = pltpu.SMEM, (s.part + 8, LN)
    sends = call(
        pack_kernel, s, [packed] * s.nd,
        [
            smem(material_thermal_values.shape, F32), smem(layer_material.shape, jnp.int32),
            smem((1, 1), F32), pltpu.VMEM((4, s.nb), jnp.int32),
            pltpu.VMEM(source_heating.shape, F32), pltpu.SemaphoreType.DMA((s.lz + 4,)),
        ],
        from_hbm=True, in_vmem=True, limit=VMEM - 4 * s.nd * packed[0] * packed[1],
    )(material_thermal_values, layer_material, via_conductance[None], via_blocks[0].T, source_heating)
    parts = [sends[0]] + [shift(sends[k], "die", k) for k in range(1, s.nd)]
    half = (s.nz * s.j0, HY, LN)
    one, two, prm = call(assemble_kernel, s, [half, half, (s.nd, 8, LN)])(*parts)
    f0, f1, small = (s.j0, s.re, LN), (s.j1, s.e1, LN), (s.nz, s.j1, s.r1, LN)
    fine, fine_v = (s.nz, *f0), (s.nz + 2, *f0)
    mid, mid_v = (s.nz, *f1), (s.nz + 2, *f1)
    slab, table = (s.nd * s.lz, s.nt, LN), (s.nz, 8, LN)
    up0, down0, e0, c, ic, cu, cd = call(
        coeff_fine_kernel, s, [(s.nd, *f0), (s.nd, *f0), fine, table, table, table, table]
    )(prm)
    shared = (s.nz + s.nd, s.r1, LN)
    flat, rbuf = (s.nz, s.r1, s.we), (s.nz * s.j0 * s.re, LN)
    from_two = swap(two, 1)
    from_one = swap(one, 0)
    f, v2, r1, ship = call(fine_first_kernel, s, [fine, fine_v, small, shared], [fine_v, rbuf, flat])(
        from_one, from_two, one, two, up0, down0, e0, ic, cu, cd, down
    )
    up1, down1, e1, u2, l2, e2 = call(coeff_coarse_kernel, s, [(s.nd, *f1), (s.nd, *f1), mid, slab, slab, slab])(prm)

    def middle_first(r1, ship):
        return call(
            middle_first_kernel, s,
            [mid, mid_v, (s.nd * s.nt * s.lz, LN)], [mid_v, (s.nz * 8, LN)],
        )(swap(ship, 0), r1, swap(ship, 1), up1, down1, e1, cu, cd, down2)

    def everywhere(send):
        return lax.all_to_all(send, ("die", "tile"), 0, 0, tiled=True)

    spaces = [(s.nd * s.lz, s.nt + 2 * HY, LN), (s.nz * 8, LN), (s.nz, 8, s.w1), mid_v, mid_v]
    spaces += [fine_v, fine_v, flat]
    rx, w2, send = middle_first(r1, ship)
    levels = (u2, l2, e2, up1, down1, e1, up0, down0, e0)
    v, r1, ship = call(back_kernel, s, [fine_v, small, shared], spaces + [rbuf])(
        everywhere(send), v2, f, w2, rx, *levels, cu, cd, spread2, spread1, down
    )
    rx, w2, send = middle_first(r1, ship)
    piece = ((s.lz + 2) * (s.j0 - 1) * s.rows + 2 * s.lz * (s.j0 - 1), LN)
    sends = call(last_kernel, s, [piece] * s.nd, spaces)(
        everywhere(send), w2, rx, v, f, *levels, cu, cd, spread2, spread1
    )
    parts = [sends[0]] + [shift(sends[k], "die", k) for k in range(1, s.nd)]
    whole, columns = (s.lz, s.rows, s.width), (s.width // LN, s.rows, LN)
    own_up, own_down = call(coeff_own_kernel, s, [columns] * 2)(prm)
    scratch = [(s.lz + 2, s.width // LN, s.re, LN), whole, whole, pltpu.SemaphoreType.DMA((2 * s.lz,))]
    return tuple(call(finish_kernel, s, [whole] * 2, scratch, True)(source_heating, c, cu, own_up, own_down, *parts))


def solution(mesh):
    in_specs = (P("die", "tile", None), P(), P("die"), P("die"), P("die", None, None))
    out_specs = (P("die", "tile", None), P("die", "tile", None))

    def body(f, mat, material, conductance, blocks):
        s = Sizes(mesh.shape, f.shape, blocks.shape[1])
        return local(s, f, mat, material, conductance, blocks)

    return jax.shard_map(body, mesh=mesh, in_specs=in_specs, out_specs=out_specs, check_vma=False)
```
